32 devices in a mesh: atoms: 8 (over z, core), kvec: 4 (over y, x).
Axes of the slice: x: 2, y: 2, z: 4, core: 2. Of those that a mesh axis runs over, the one named last changes fastest.
Arguments:
- positions: float32 [3, 8192], P(None, ('atoms', 'kvec')), may hold values from 0 to 8
- features: bfloat16 [8192, 128], P(('atoms', 'kvec')), may hold values from -6 to 6
- atom_mask: int32 [8192], P(('atoms', 'kvec')), may hold values 0 or 1
- neighbours: int32 [64, 12], P(('atoms', 'kvec')), may hold values from 0 to 63, as said below
- lattice: int32 [3, 12288], P(None, 'kvec'), may hold values from -15 to 15, as said below
- pair_weight: bfloat16 [1024, 128], replicated, may hold values from -0.1875 to 0.1875
- kfilter: float32 [8, 128], replicated, may hold values from -4 to 4
- norm_gain: float32 [128], replicated, may hold values from 0.25 to 1.75
- w_in: bfloat16 [128, 512], replicated, may hold values from -0.5 to 0.5
- w_out: bfloat16 [512, 128], replicated, may hold values from -0.25 to 0.25
Outputs:
- updated: bfloat16 [8192, 128], P(('atoms', 'kvec'))
The draws below stay inside these ranges and needn't reach their ends.
Inputs may be any that keep to these rules, and one draw needn't show every extreme that they name: `neighbours`: group of a block = its id // 8. The 12 ids of a block are different and each lies in the block's group, the group below or the group above it, cyclically over the 8 groups. `lattice`: the 12288 wavevectors are distinct, none is zero, and no two are negatives of each other.
All inputs are finite; a program needn't handle non-finite values. No bound on the sum of `atom_mask` on one device may be relied on, other than what follows from the above.
Results may differ from the reference program's by a relative error of at most 0.017.
Values may be sent and summed in bfloat16 or wider, within the bound.
No kernel may reach another device: no remote copies, remote signals or barrier semaphores. Data moves between devices by JAX's collectives and lax.ppermute only.
A program may use at most 64 MiB of HBM per device.

```python
import math
import jax
import jax.numpy as jnp
from jax import lax

C = 128
HID = 512
KW = 12288
KB = 8
KQ = 8
BLOCK_ATOMS = 128
NS = 12
ATOMS = 8192
NBLK = 64
GROUP_BLK = 8


def draw_neighbours(key, part):
    feature_width = 3 * GROUP_BLK
    scores = jax.random.randint(key, (NBLK, feature_width), 0, 1 << 16)
    scores = scores * feature_width + jnp.arange(feature_width, dtype=jnp.int32)[None, :]
    _, picked = lax.top_k(scores, NS)
    group = jnp.arange(NBLK, dtype=jnp.int32) // GROUP_BLK
    atom_identifiers = ((group[:, None] - 1) * GROUP_BLK + picked.astype(jnp.int32)) % NBLK
    return atom_identifiers.astype(jnp.int32)


def draw_lattice(key, part):
    order = jax.random.permutation(jax.random.fold_in(key, 7), 14895).astype(jnp.int32)
    code = order[:KW] + 14896
    first = code // 961 - 15
    second = code // 31 % 31 - 15
    third = code % 31 - 15
    return jnp.stack([first, second, third], axis=0).astype(jnp.int32)


def plant(array, rng, low, top_value):
    index_at = [jax.random.randint(jax.random.fold_in(rng, axis), (), 0, length) for axis, length in enumerate(array.shape)]
    widest = array.shape.index(max(array.shape))
    next_to = index_at[:widest] + [(index_at[widest] + 1) % array.shape[widest]] + index_at[widest + 1:]
    return array.at[tuple(index_at)].set(low).at[tuple(next_to)].set(top_value)


def level_of(stream_key, dims, shards, least, largest):
    def one(dim, shards_of):
        steps = jax.random.uniform(jax.random.fold_in(jax.random.fold_in(stream_key, 6), dim), (shards_of,), jnp.float32, least / len(shards), largest / len(shards))
        return jnp.repeat(jnp.exp(steps), dims[dim] // shards_of).reshape((-1,) + (1,) * (len(dims) - dim - 1))

    loudness = one(*shards[0])
    for cut in shards[1:]:
        loudness = loudness * one(*cut)
    return loudness


def gaussian(rng, extent, spread, most, shards=(), kind=jnp.bfloat16):
    loudness = level_of(rng, extent, shards, -0.22, 0.18) if shards else 1.0
    array = jax.random.normal(rng, extent, jnp.float32) * spread * loudness
    return jnp.minimum(jnp.maximum(array, -most), most).astype(kind)


def setup_inputs(seed: int = 0) -> dict:
    arg_keys = jax.random.split(jax.random.key(seed), 11)
    positions = jnp.clip(8.0 * jax.random.uniform(arg_keys[0], (3, ATOMS), jnp.float32) ** level_of(arg_keys[0], (3, ATOMS), ((1, 32),), -0.2, 0.2), 0.0, 8.0)
    features = gaussian(arg_keys[1], (ATOMS, C), 1.0, 6.0, ((0, 32),))
    atom_mask = plant((jax.random.randint(arg_keys[2], (ATOMS,), 0, 8) < 7).astype(jnp.int32), jax.random.fold_in(arg_keys[2], 1), 0, 1)
    neighbours = draw_neighbours(jax.random.fold_in(arg_keys[10], 71), 0)
    lattice = draw_lattice(jax.random.fold_in(arg_keys[10], 71), 0)
    pair_weight = gaussian(arg_keys[5], (KB * C, C), (KB * C) ** -0.5, 0.1875)
    kfilter = gaussian(arg_keys[6], (KQ, C), 1.0, 4.0, (), jnp.float32)
    norm_gain = jnp.clip(1.0 + 0.15 * jax.random.normal(arg_keys[7], (C,), jnp.float32), 0.25, 1.75)
    w_in = gaussian(arg_keys[8], (C, HID), C ** -0.5, 0.5)
    w_out = gaussian(arg_keys[9], (HID, C), HID ** -0.5, 0.25)
    return {"positions": positions, "features": features, "atom_mask": atom_mask, "neighbours": neighbours, "lattice": lattice, "pair_weight": pair_weight, "kfilter": kfilter, "norm_gain": norm_gain, "w_in": w_in, "w_out": w_out}


def trig_tables(pos, wave):
    phase = pos[0][:, None] * wave[0][None, :] + pos[1][:, None] * wave[1][None, :] + pos[2][:, None] * wave[2][None, :]
    return (jnp.cos(phase).astype(jnp.bfloat16), jnp.sin(phase).astype(jnp.bfloat16))

def radial_filter(wave, kfilter):
    nbasis = kfilter.shape[0]
    kmag = jnp.sqrt(wave[0] * wave[0] + wave[1] * wave[1] + wave[2] * wave[2])
    centers = (jnp.arange(nbasis, dtype=jnp.float32) + 0.5) * (21.0 / nbasis)
    basis = jnp.exp(-0.5 * ((kmag[:, None] - centers[None, :]) / (21.0 / nbasis)) ** 2)
    return lax.optimization_barrier(jnp.sum(basis[:, :, None] * kfilter[None, :, :], axis=1))

def pair_block(own_pos, own_index, nearby_coordinates, nearby_feature_rows, nearby_atom_index, pair_weight, output_scale):
    feature_width = nearby_feature_rows.shape[1]
    nbasis = pair_weight.shape[0] // feature_width
    own_count = own_pos.shape[1]
    dist2 = (own_pos[0][:, None] - nearby_coordinates[0][None, :]) ** 2
    dist2 = dist2 + (own_pos[1][:, None] - nearby_coordinates[1][None, :]) ** 2
    dist2 = dist2 + (own_pos[2][:, None] - nearby_coordinates[2][None, :]) ** 2
    radius = jnp.sqrt(dist2)
    keep = (own_index[:, None] != nearby_atom_index[None, :]).astype(jnp.float32)
    env = keep * output_scale / (1.0 + (radius / 4.0) ** 2)
    centers = (jnp.arange(nbasis, dtype=jnp.float32) + 0.5) * (12.0 / nbasis)
    basis = jnp.exp(-0.5 * ((radius[None] - centers[:, None, None]) / (12.0 / nbasis)) ** 2) * env[None]
    basis = basis.astype(jnp.bfloat16).reshape(nbasis * own_count, radius.shape[1])
    summed = jnp.dot(basis, nearby_feature_rows, preferred_element_type=jnp.float32)
    summed = summed.reshape(nbasis, own_count, feature_width).transpose(1, 0, 2)
    summed = summed.reshape(own_count, nbasis * feature_width).astype(jnp.bfloat16)
    return jnp.dot(summed, pair_weight, preferred_element_type=jnp.float32)

def reference(positions, features, atom_mask, neighbours, lattice, pair_weight, kfilter, norm_gain, w_in, w_out):
    maskf = atom_mask.astype(jnp.float32)
    masked = (features.astype(jnp.float32) * maskf[:, None]).astype(jnp.bfloat16)
    nblk = ATOMS // BLOCK_ATOMS
    position_block_rows = positions.reshape(3, nblk, BLOCK_ATOMS)
    feature_block_rows = masked.reshape(nblk, BLOCK_ATOMS, C)
    output_scale = float(NS * BLOCK_ATOMS) ** (-0.5)
    block_offsets = jnp.arange(BLOCK_ATOMS, dtype=jnp.int32)

    def one_block(index):
        atom_identifiers = neighbours[index]
        nearby_coordinates = position_block_rows[:, atom_identifiers].reshape(3, NS * BLOCK_ATOMS)
        nearby_feature_rows = feature_block_rows[atom_identifiers].reshape(NS * BLOCK_ATOMS, C)
        nearby_atom_index = (atom_identifiers[:, None] * BLOCK_ATOMS + block_offsets[None, :]).reshape(NS * BLOCK_ATOMS)
        return pair_block(position_block_rows[:, index], index * BLOCK_ATOMS + block_offsets, nearby_coordinates, nearby_feature_rows, nearby_atom_index, pair_weight, output_scale)
    pair_msg = lax.map(one_block, jnp.arange(nblk, dtype=jnp.int32)).reshape(ATOMS, C)
    wave = lattice.astype(jnp.float32) * (2.0 * math.pi / 8.0)
    rows = 512 if ATOMS % 512 == 0 else ATOMS
    steps = ATOMS // rows

    def accumulate(carry, index):
        start = index * rows
        pos = lax.dynamic_slice_in_dim(positions, start, rows, 1)
        feat = lax.dynamic_slice_in_dim(masked, start, rows, 0)
        cosines, sines = trig_tables(pos, wave)
        part_c = jnp.dot(cosines.T, feat, preferred_element_type=jnp.float32)
        part_s = jnp.dot(sines.T, feat, preferred_element_type=jnp.float32)
        return ((carry[0] + part_c, carry[1] + part_s), None)
    zero = jnp.zeros((KW, C), jnp.float32)
    (factor_c, factor_s), _ = lax.scan(accumulate, (zero, zero), jnp.arange(steps, dtype=jnp.int32))
    kfilt = radial_filter(wave, kfilter) * float(ATOMS * KW) ** (-0.5)
    filt_c = (kfilt * factor_c).astype(jnp.bfloat16)
    filt_s = (kfilt * factor_s).astype(jnp.bfloat16)

    def inverse(index):
        pos = lax.dynamic_slice_in_dim(positions, index * rows, rows, 1)
        cosines, sines = trig_tables(pos, wave)
        return jnp.dot(cosines, filt_c, preferred_element_type=jnp.float32) + jnp.dot(sines, filt_s, preferred_element_type=jnp.float32)
    long_msg = lax.map(inverse, jnp.arange(steps, dtype=jnp.int32)).reshape(ATOMS, C)
    total = features.astype(jnp.float32) + pair_msg + long_msg
    normed = (total * lax.rsqrt(lax.optimization_barrier(jnp.mean(total * total, axis=-1, keepdims=True)) + 1e-06) * norm_gain).astype(jnp.bfloat16)
    hidden = jax.nn.silu(jnp.dot(normed, w_in, preferred_element_type=jnp.float32)).astype(jnp.bfloat16)
    return (total + jnp.dot(hidden, w_out, preferred_element_type=jnp.float32)).astype(jnp.bfloat16)
```

```python
import functools
import math

import jax
import jax.numpy as jnp
from jax import lax
from jax.experimental import pallas as pl
from jax.experimental.pallas import tpu as pltpu
from jax.sharding import PartitionSpec as P

KW = 12288
BLOCK_ATOMS = 128
F32 = jnp.float32
BF16 = jnp.bfloat16

SIN_COEF = (4.442879586561992, -7.307818050390618, 3.5977887417720016, -0.7912382192058507)
COS_COEF = (
    1.4142134965673514,
    -6.978850988333677,
    5.7394611716098,
    -1.8835629899121002,
    0.3106981922752005,
)
ROUND = 12582912.0


def params(mib=48):
    return pltpu.CompilerParams(vmem_limit_bytes=mib << 20)


def split3(ref, value):
    n = value.shape[0]
    high = value.astype(BF16).astype(F32)
    rest = value - high
    mid = rest.astype(BF16).astype(F32)
    ref[...] = jnp.zeros_like(ref)
    ref[0:n, :] = high
    ref[8 : 8 + n, :] = mid
    ref[16 : 16 + n, :] = rest - mid


def horner(u, coef):
    acc = coef[-1] * u + coef[-2]
    for c in reversed(coef[:-2]):
        acc = acc * u + c
    return acc


def trig_kernel(lattice_ref, pos_ref, out_ref, lat_scr, pos_scr, phase_scr):
    count = lattice_ref.shape[1]
    lat = lattice_ref[...].astype(F32)
    lat_scr[...] = jnp.zeros_like(lat_scr)
    for part in range(3):
        lat_scr[8 * part : 8 * part + 3, :] = lat
    split3(pos_scr, pos_ref[...] * 0.125)
    phase_scr[...] = lax.dot_general(
        lat_scr[...].astype(BF16),
        pos_scr[...].astype(BF16),
        (((0,), (0,)), ((), ())),
        preferred_element_type=F32,
    )
    rows = 16

    def step(i, carry):
        at = pl.multiple_of(i * rows, rows)
        turns = phase_scr[pl.ds(at, rows), :]
        r = turns - ((turns + ROUND) - ROUND)
        u = r * r
        s = horner(u, SIN_COEF) * r
        c = horner(u, COS_COEF)
        out_ref[pl.ds(at, rows), :] = (1.0 - s * s).astype(BF16)
        out_ref[pl.ds(pl.multiple_of(count + at, rows), rows), :] = (s * c).astype(BF16)
        return carry

    lax.fori_loop(0, count // rows, step, 0, unroll=4)


def trig_tables(lattice, pos, width=512):
    count, atoms = lattice.shape[1], pos.shape[1]
    return pl.pallas_call(
        trig_kernel,
        grid=(atoms // width,),
        in_specs=[
            pl.BlockSpec((3, count), lambda i: (0, 0)),
            pl.BlockSpec((3, width), lambda i: (0, i)),
        ],
        out_specs=pl.BlockSpec((2 * count, width), lambda i: (0, i)),
        out_shape=jax.ShapeDtypeStruct((2 * count, atoms), BF16),
        scratch_shapes=[
            pltpu.VMEM((24, count), F32),
            pltpu.VMEM((24, width), F32),
            pltpu.VMEM((count, width), F32),
        ],
        compiler_params=params(),
        cost_estimate=pl.CostEstimate(
            flops=30 * count * atoms, bytes_accessed=4 * count * atoms, transcendentals=0
        ),
        name="trig",
    )(lattice, pos)


def forward_kernel(table_ref, feat_ref, out_ref, low_ref):
    step = pl.program_id(0)
    part = jnp.dot(table_ref[...], feat_ref[...], preferred_element_type=F32)

    @pl.when(step == 0)
    def _():
        out_ref[...] = part

    @pl.when(step > 0)
    def _():
        out_ref[...] += part

    @pl.when(step == pl.num_programs(0) - 1)
    def _():
        low_ref[...] = out_ref[...].astype(BF16)


def forward(table, feat, width=512):
    rows, atoms = table.shape
    channels = feat.shape[1]
    return pl.pallas_call(
        forward_kernel,
        grid=(atoms // width,),
        in_specs=[
            pl.BlockSpec((rows, width), lambda i: (0, i)),
            pl.BlockSpec((width, channels), lambda i: (i, 0)),
        ],
        out_specs=[pl.BlockSpec((rows, channels), lambda i: (0, 0))] * 2,
        out_shape=[
            jax.ShapeDtypeStruct((rows, channels), F32),
            jax.ShapeDtypeStruct((rows, channels), BF16),
        ],
        compiler_params=params(),
        cost_estimate=pl.CostEstimate(
            flops=2 * rows * atoms * channels, bytes_accessed=2 * rows * atoms, transcendentals=0
        ),
        name="forward",
    )(table, feat)


def radial_kernel(nbasis, scale, lattice_ref, kfilter_ref, out_ref):
    wave = lattice_ref[...].astype(F32) * (2.0 * math.pi / 8.0)
    kmag = jnp.sqrt(
        wave[0:1] * wave[0:1] + wave[1:2] * wave[1:2] + wave[2:3] * wave[2:3]
    )
    total = jnp.zeros(out_ref.shape, F32)
    for p in range(nbasis):
        basis = jnp.exp(-0.5 * ((kmag - (p + 0.5) * (21.0 / nbasis)) / (21.0 / nbasis)) ** 2)
        total += kfilter_ref[:, p : p + 1] * basis
    out_ref[...] = total * scale


def radial_filter(lattice, kfilter, scale):
    nbasis, channels = kfilter.shape
    count = lattice.shape[1]
    return pl.pallas_call(
        functools.partial(radial_kernel, nbasis, scale),
        out_shape=jax.ShapeDtypeStruct((channels, count), F32),
        compiler_params=params(16),
        name="radial",
    )(lattice, kfilter.T)


def filter_kernel(own_ref, other_ref, kfilt_ref, out_ref):
    count = kfilt_ref.shape[1]
    for part in range(2):
        rows = pl.ds(part * count, count)
        total = own_ref[rows, :] + other_ref[rows, :].astype(F32)
        out_ref[:, rows] = (total.T * kfilt_ref[...]).astype(BF16)


def filtered(own, other, kfilt):
    rows, channels = own.shape
    return pl.pallas_call(
        filter_kernel,
        out_shape=jax.ShapeDtypeStruct((channels, rows), BF16),
        compiler_params=params(16),
        name="filter",
    )(own, other, kfilt)


def inverse_kernel(filt_ref, table_ref, out_ref):
    out_ref[...] = jnp.dot(
        filt_ref[...], table_ref[...], preferred_element_type=F32
    ).astype(out_ref.dtype)


def inverse(filt, table, first, atoms, dtype, width=512):
    channels, rows = filt.shape
    start = first // width
    return pl.pallas_call(
        inverse_kernel,
        grid=(atoms // width,),
        in_specs=[
            pl.BlockSpec((channels, rows), lambda i: (0, 0)),
            pl.BlockSpec((rows, width), lambda i: (0, start + i)),
        ],
        out_specs=pl.BlockSpec((channels, width), lambda i: (0, i)),
        out_shape=jax.ShapeDtypeStruct((channels, atoms), dtype),
        compiler_params=params(),
        cost_estimate=pl.CostEstimate(
            flops=2 * rows * atoms * channels, bytes_accessed=2 * rows * atoms, transcendentals=0
        ),
        name="inverse",
    )(filt, table)


def pair_kernel(
    nbasis,
    output_scale,
    slots_ref,
    same_ref,
    own_pos_ref,
    feat0_ref,
    feat1_ref,
    feat2_ref,
    pos0_ref,
    pos1_ref,
    pos2_ref,
    weight_ref,
    out_ref,
    feat_scr,
    pos_scr,
    own_scr,
    basis_scr,
    acc_scr,
):
    block = BLOCK_ATOMS
    width = 12.0 / nbasis
    group = feat0_ref.shape[0]
    for g, (f, p) in enumerate(((feat0_ref, pos0_ref), (feat1_ref, pos1_ref), (feat2_ref, pos2_ref))):
        feat_scr[g * group : (g + 1) * group, :] = f[...]
        pos_scr[0:3, g * group : (g + 1) * group] = p[...]
    own_blocks, neighbours = slots_ref.shape
    rows = 64
    ident = (
        lax.broadcasted_iota(jnp.int32, (rows, block), 0)
        - lax.broadcasted_iota(jnp.int32, (rows, block), 1)
    )
    for b in range(own_blocks):
        for d in range(3):
            row = own_pos_ref[d : d + 1, b * block : (b + 1) * block]
            own_scr[d] = jnp.broadcast_to(row, (block, block)).T
        acc_scr[...] = jnp.zeros_like(acc_scr)

        def pair(jp, carry):
            blocks = []
            for h in range(2):
                slot = pl.multiple_of(slots_ref[b, 2 * jp + h] * block, block)
                same = same_ref[b, 2 * jp + h]
                blocks.append(feat_scr[pl.ds(slot, block), :])
                near = [pos_scr[d : d + 1, pl.ds(slot, block)] for d in range(3)]
                for part in range(block // rows):
                    at = part * rows
                    dist2 = (own_scr[0, at : at + rows, :] - near[0]) ** 2
                    dist2 += (own_scr[1, at : at + rows, :] - near[1]) ** 2
                    dist2 += (own_scr[2, at : at + rows, :] - near[2]) ** 2
                    radius = dist2 * lax.rsqrt(jnp.maximum(dist2, 1e-30))
                    env = output_scale / (1.0 + dist2 * (1.0 / 16.0))
                    drop = (ident + at == 0) & (same != 0)
                    env = jnp.where(drop, 0.0, env)
                    v = radius * (1.0 / width) - 0.5
                    value = jnp.exp(-0.5 * v * v) * env
                    ratio = jnp.exp(v)
                    for k in range(nbasis):
                        if k:
                            value = value * ratio
                        basis_scr[
                            k * block + at : k * block + at + rows, h * block : (h + 1) * block
                        ] = value.astype(BF16)
            acc_scr[...] += jnp.dot(
                basis_scr[...], jnp.concatenate(blocks, axis=0), preferred_element_type=F32
            )
            return carry

        lax.fori_loop(0, neighbours // 2, pair, 0)
        total = jnp.zeros((block, out_ref.shape[1]), F32)
        channels = feat0_ref.shape[1]
        for k in range(nbasis):
            gathered = (acc_scr[k * block : (k + 1) * block, :] * math.exp(-0.5 * k * k)).astype(BF16)
            total += jnp.dot(
                gathered,
                weight_ref[k * channels : (k + 1) * channels, :],
                preferred_element_type=F32,
            )
        out_ref[b * block : (b + 1) * block, :] = total


def pair_message(slots, same, own_pos, feats, poss, weight):
    group, channels = feats[0].shape
    nbasis = weight.shape[0] // channels
    shard = own_pos.shape[1]
    neighbours = slots.shape[1]
    scale = float(neighbours * BLOCK_ATOMS) ** (-0.5)
    smem = pl.BlockSpec(memory_space=pltpu.SMEM)
    vmem = pl.BlockSpec(memory_space=pltpu.VMEM)
    return pl.pallas_call(
        functools.partial(pair_kernel, nbasis, scale),
        in_specs=[smem, smem] + [vmem] * 8,
        out_specs=vmem,
        out_shape=jax.ShapeDtypeStruct((shard, channels), F32),
        scratch_shapes=[
            pltpu.VMEM((3 * group, channels), BF16),
            pltpu.VMEM((8, 3 * group), F32),
            pltpu.VMEM((3, BLOCK_ATOMS, BLOCK_ATOMS), F32),
            pltpu.VMEM((nbasis * BLOCK_ATOMS, 2 * BLOCK_ATOMS), BF16),
            pltpu.VMEM((nbasis * BLOCK_ATOMS, channels), F32),
        ],
        compiler_params=params(24),
        cost_estimate=pl.CostEstimate(
            flops=2 * shard * neighbours * BLOCK_ATOMS * (nbasis * channels + 40),
            bytes_accessed=6 * group * channels,
            transcendentals=3 * shard * neighbours * BLOCK_ATOMS,
        ),
        name="pair",
    )(slots, same, own_pos, *feats, *poss, weight)


def update_kernel(count, *refs):
    features_ref, pair_ref, gain_ref, w_in_ref, w_out_ref = refs[:5]
    parts, out_ref = refs[5:-1], refs[-1]
    long_t = parts[0][...].astype(F32)
    for part in parts[1:]:
        long_t = long_t + part[...].astype(F32)
    total = features_ref[...].astype(F32) + pair_ref[...] + long_t.T
    mean = jnp.mean(total * total, axis=-1, keepdims=True)
    normed = (total * lax.rsqrt(mean + 1e-06) * gain_ref[...]).astype(BF16)
    pre = jnp.dot(normed, w_in_ref[...], preferred_element_type=F32)
    hidden = (pre / (1.0 + jnp.exp(-pre))).astype(BF16)
    out_ref[...] = (
        total + jnp.dot(hidden, w_out_ref[...], preferred_element_type=F32)
    ).astype(BF16)


def update(features, pair_msg, gain, w_in, w_out, parts):
    return pl.pallas_call(
        functools.partial(update_kernel, len(parts)),
        out_shape=jax.ShapeDtypeStruct(features.shape, BF16),
        compiler_params=params(16),
        name="update",
    )(features, pair_msg, gain[None, :], w_in, w_out, *parts)


def swap(value, axis, bits):
    return lax.ppermute(value, axis, [(i, i ^ bits) for i in range(lax.axis_size(axis))])


def per_device(
    positions,
    features,
    atom_mask,
    neighbours,
    lattice,
    pair_weight,
    kfilter,
    norm_gain,
    w_in,
    w_out,
):
    shard, channels = features.shape
    n_atoms = lax.axis_size("atoms")
    n_kvec = lax.axis_size("kvec")
    a_index = lax.axis_index("atoms")
    k_index = lax.axis_index("kvec")
    nb = shard // BLOCK_ATOMS
    group_blk = nb * n_kvec
    far = n_atoms // 4
    core = a_index % 2
    part = core + 2 * (a_index // 4)
    count = lattice.shape[1] // (2 * far)
    own_lattice = lax.dynamic_slice_in_dim(lattice, part * count, count, 1)

    masked = (features.astype(F32) * atom_mask.astype(F32)[:, None]).astype(BF16)

    def spread(value, axis):
        near = [value] + [swap(value, "atoms", 4 * z) for z in range(1, far)]
        pieces = []
        for item in near:
            pieces += [item] + [swap(item, "kvec", k) for k in range(1, n_kvec)]
        half = jnp.concatenate(pieces, axis=axis)
        return half, swap(half, "atoms", 1)

    pos_half, pos_other = spread(positions, 1)
    feat_half, feat_other = spread(masked, 0)
    pos = jnp.concatenate([pos_half, pos_other], axis=1)
    feat = jnp.concatenate([feat_half, feat_other], axis=0)

    table = trig_tables(own_lattice, pos)
    own, low = forward(table, feat)
    other = swap(low, "atoms", 2)
    kfilt = radial_filter(own_lattice, kfilter, float(n_atoms * n_kvec * shard * KW) ** (-0.5))
    filt = filtered(own, other, kfilt)

    group = n_kvec * shard
    halo_pairs = [(a, (a + 1) % n_atoms if a % 2 else (a - 1) % n_atoms) for a in range(n_atoms)]
    own_feat, own_pos = feat_half[:group], pos_half[:, :group]
    halo_feat = lax.ppermute(own_feat, "atoms", halo_pairs)
    halo_pos = lax.ppermute(own_pos, "atoms", halo_pairs)
    id_group = neighbours // group_blk
    within = neighbours % group_blk
    ahead = (id_group - a_index) % n_atoms
    toward = jnp.where(core == 0, 1, n_atoms - 1)
    which = jnp.where(ahead == 0, 0, jnp.where(ahead == toward, 1, 2))
    slots = which * group_blk + ((within // nb) ^ k_index) * nb + within % nb
    mine = (a_index * n_kvec + k_index) * nb + jnp.arange(nb, dtype=jnp.int32)
    same = (neighbours == mine[:, None]).astype(jnp.int32)
    pair_msg = pair_message(
        slots.astype(jnp.int32),
        same,
        positions,
        (own_feat, feat_other[:group], halo_feat),
        (own_pos, pos_other[:, :group], halo_pos),
        pair_weight,
    )

    half = pos_half.shape[1]
    away = inverse(filt, table, half, half, BF16)
    arrived = swap(away, "atoms", 1)
    here = inverse(filt, table, 0, half, F32)
    both = here + arrived.astype(F32)
    both = both.reshape(channels, far, n_kvec, shard)
    sends = both.astype(BF16)
    per_z = []
    for z in range(far):
        total = both[:, z, 0]
        for k in range(1, n_kvec):
            total = total + swap(sends[:, z, k], "kvec", k).astype(F32)
        per_z.append(total)
    parts = [per_z[0]] + [swap(per_z[z].astype(BF16), "atoms", 4 * z) for z in range(1, far)]
    return update(features, pair_msg, norm_gain, w_in, w_out, parts)


def solution(mesh):
    return jax.shard_map(
        per_device,
        mesh=mesh,
        in_specs=(
            P(None, ("atoms", "kvec")),
            P(("atoms", "kvec"), None),
            P(("atoms", "kvec")),
            P(("atoms", "kvec"), None),
            P(None, "kvec"),
            P(),
            P(),
            P(),
            P(),
            P(),
        ),
        out_specs=P(("atoms", "kvec"), None),
        check_vma=False,
    )
```

```python
import functools
import math

import jax
import jax.numpy as jnp
from jax import lax
from jax.experimental import pallas as pl
from jax.experimental.pallas import tpu as pltpu
from jax.sharding import PartitionSpec as P

KW = 12288
BLOCK_ATOMS = 128
F32 = jnp.float32
BF16 = jnp.bfloat16

SIN_COEF = (4.442879586561992, -7.307818050390618, 3.5977887417720016, -0.7912382192058507)
ROUND = 12582912.0
TAIL = 16


def params(mib=16):
    return pltpu.CompilerParams(vmem_limit_bytes=mib << 20)


SMEM = pl.BlockSpec(memory_space=pltpu.SMEM)
VMEM = pl.BlockSpec(memory_space=pltpu.VMEM)


def horner(u, coef):
    acc = coef[-1] * u + coef[-2]
    for c in reversed(coef[:-2]):
        acc = acc * u + c
    return acc


def pack_kernel(features_ref, mask_ref, pos_ref, out_ref, scr):
    shard, channels = features_ref.shape
    mask = jnp.broadcast_to(mask_ref[...].astype(F32), (channels, shard)).T
    out_ref[0:shard, :] = (features_ref[...].astype(F32) * mask).astype(BF16)
    value = pos_ref[...] * 0.125
    high = value.astype(BF16).astype(F32)
    rest = value - high
    mid = rest.astype(BF16).astype(F32)
    scr[...] = jnp.zeros_like(scr)
    scr[0:3, :] = high
    scr[3:6, :] = mid
    scr[6:9, :] = rest - mid
    for b in range(shard // BLOCK_ATOMS):
        out_ref[shard + b * TAIL : shard + (b + 1) * TAIL, :] = scr[
            :, b * BLOCK_ATOMS : (b + 1) * BLOCK_ATOMS
        ].astype(BF16)


def pack(features, mask, positions):
    shard, channels = features.shape
    rows = shard + TAIL * (shard // BLOCK_ATOMS)
    return pl.pallas_call(
        pack_kernel,
        in_specs=[VMEM] * 3,
        out_specs=VMEM,
        out_shape=jax.ShapeDtypeStruct((rows, channels), BF16),
        scratch_shapes=[pltpu.VMEM((TAIL, shard), F32)],
        compiler_params=params(),
        name="pack",
    )(features, mask[None, :], positions)


def wave_kernel(pieces, last, shard, *refs):
    lattice_ref, refs = refs[0], refs[1:]
    message_refs, refs = refs[:pieces], refs[pieces:]
    before_ref, refs = (refs[0], refs[1:]) if last is not None else (None, refs)
    table_ref, total_ref = refs[:2]
    low_ref, refs = (refs[2], refs[3:]) if last else (None, refs[2:])
    lat_scr, feat_scr, pos_scr, phase_scr = refs
    blocks, _, width = lattice_ref.shape
    for j in range(blocks):
        lat = lattice_ref[j].astype(F32)
        lat_scr[j] = jnp.zeros_like(lat_scr[j])
        for part in range(3):
            lat_scr[j, 3 * part : 3 * part + 3, :] = lat
    for p, message in enumerate(message_refs):
        feat_scr[p] = message[0:shard, :].astype(F32).T.astype(BF16)
        for b in range(shard // BLOCK_ATOMS):
            pos_scr[p, :, b * BLOCK_ATOMS : (b + 1) * BLOCK_ATOMS] = message[
                shard + b * TAIL : shard + (b + 1) * TAIL, :
            ]
    if before_ref is None:
        total_ref[...] = jnp.zeros_like(total_ref)
    else:
        total_ref[...] = before_ref[...]

    steps = pieces * blocks

    def phase(i, slot):
        piece, block = i // blocks, i % blocks
        phase_scr[slot] = lax.dot_general(
            lat_scr[block].astype(BF16),
            pos_scr[piece],
            (((0,), (0,)), ((), ())),
            preferred_element_type=F32,
        )

    def table(i, slot):
        piece, block = i // blocks, i % blocks
        lanes = pl.ds(pl.multiple_of(piece * shard, shard), shard)
        rows = 16
        for at in range(0, width, rows):
            turns = phase_scr[slot, at : at + rows, :]
            r = turns - ((turns + ROUND) - ROUND)
            s = horner(r * r, SIN_COEF) * r
            c = 1.0 - s * s
            w = jnp.maximum(c + 1.0, 1e-12)
            table_ref[block, at : at + rows, lanes] = c.astype(BF16)
            table_ref[blocks + block, at : at + rows, lanes] = (s * (w * lax.rsqrt(w))).astype(BF16)

    def product(i):
        piece, block = i // blocks, i % blocks
        lanes = pl.ds(pl.multiple_of(piece * shard, shard), shard)
        for half in range(2):
            total_ref[half * blocks + block] += lax.dot_general(
                feat_scr[piece],
                table_ref[half * blocks + block, :, lanes],
                (((1,), (1,)), ((), ())),
                preferred_element_type=F32,
            )

    phase(0, 0)

    def body(i, carry):
        product(i - 1)
        table(i, i % 2)
        phase(jnp.minimum(i + 1, steps - 1), (i + 1) % 2)
        return carry

    table(0, 0)
    phase(min(1, steps - 1), 1)
    lax.fori_loop(1, steps, body, 0)
    product(steps - 1)
    if low_ref is not None:
        low_ref[...] = total_ref[...].astype(BF16)


def wave(lattice, messages, before, last, shard):
    blocks, _, width = lattice.shape
    channels = messages[0].shape[1]
    pieces = len(messages)
    flag = None if before is None else last
    args = [lattice, *messages] + ([] if before is None else [before])
    factor = (2 * blocks, channels, width)
    shapes = [
        jax.ShapeDtypeStruct((2 * blocks, width, pieces * shard), BF16),
        jax.ShapeDtypeStruct(factor, F32),
    ]
    if flag:
        shapes.append(jax.ShapeDtypeStruct(factor, BF16))
    pairs = blocks * width * pieces * shard
    return pl.pallas_call(
        functools.partial(wave_kernel, pieces, flag, shard),
        in_specs=[VMEM] * len(args),
        out_specs=[VMEM] * len(shapes),
        out_shape=shapes,
        scratch_shapes=[
            pltpu.VMEM((blocks, TAIL, width), F32),
            pltpu.VMEM((pieces, channels, shard), BF16),
            pltpu.VMEM((pieces, TAIL, shard), BF16),
            pltpu.VMEM((2, width, shard), F32),
        ],
        compiler_params=params(),
        cost_estimate=pl.CostEstimate(
            flops=4 * pairs * channels, bytes_accessed=4 * pairs, transcendentals=pairs
        ),
        name="wave",
    )(*args)


def radial_kernel(nbasis, scale, lattice_ref, kfilter_ref, out_ref):
    for j in range(lattice_ref.shape[0]):
        wave = lattice_ref[j].astype(F32) * (2.0 * math.pi / 8.0)
        kmag = jnp.sqrt(
            wave[0:1] * wave[0:1] + wave[1:2] * wave[1:2] + wave[2:3] * wave[2:3]
        )
        total = jnp.zeros(out_ref.shape[1:], F32)
        for p in range(nbasis):
            basis = jnp.exp(-0.5 * ((kmag - (p + 0.5) * (21.0 / nbasis)) / (21.0 / nbasis)) ** 2)
            total += kfilter_ref[:, p : p + 1] * basis
        out_ref[j] = total * scale


def radial_filter(lattice, kfilter, scale):
    nbasis, channels = kfilter.shape
    blocks, _, width = lattice.shape
    return pl.pallas_call(
        functools.partial(radial_kernel, nbasis, scale),
        in_specs=[VMEM] * 2,
        out_specs=VMEM,
        out_shape=jax.ShapeDtypeStruct((blocks, channels, width), F32),
        compiler_params=params(),
        name="radial",
    )(lattice, kfilter.T)


def transform(filt_ref, table_refs, out_ref, pieces, shard):
    blocks = filt_ref.shape[0]
    far = len(table_refs)
    for z, table_ref in enumerate(table_refs):
        for p in range(pieces):
            acc = jnp.dot(
                filt_ref[0], table_ref[0, :, p * shard : (p + 1) * shard], preferred_element_type=F32
            )
            for j in range(1, blocks):
                acc += jnp.dot(
                    filt_ref[j],
                    table_ref[j, :, p * shard : (p + 1) * shard],
                    preferred_element_type=F32,
                )
            at = (p * far + z) * shard
            out_ref[:, at : at + shard] = acc.astype(out_ref.dtype)


def away_kernel(pieces, shard, own_ref, other_ref, kfilt_ref, *refs):
    table_refs, (filt_ref, out_ref) = refs[:-2], refs[-2:]
    count = kfilt_ref.shape[0]
    for j in range(2 * count):
        total = own_ref[j] + other_ref[j].astype(F32)
        filt_ref[j] = (total * kfilt_ref[j % count]).astype(BF16)
    transform(filt_ref, table_refs, out_ref, pieces, shard)


def here_kernel(pieces, shard, filt_ref, *refs):
    transform(filt_ref, refs[:-1], refs[-1], pieces, shard)


def inverse_cost(tables, channels):
    pairs = sum(math.prod(t.shape) for t in tables)
    return pl.CostEstimate(
        flops=2 * pairs * channels, bytes_accessed=2 * pairs, transcendentals=0
    )


def inverse_away(own, other, kfilt, tables, pieces, shard):
    channels = own.shape[1]
    atoms = pieces * shard * len(tables)
    return pl.pallas_call(
        functools.partial(away_kernel, pieces, shard),
        in_specs=[VMEM] * (3 + len(tables)),
        out_specs=[VMEM] * 2,
        out_shape=[
            jax.ShapeDtypeStruct(own.shape, BF16),
            jax.ShapeDtypeStruct((channels, atoms), BF16),
        ],
        compiler_params=params(),
        cost_estimate=inverse_cost(tables, channels),
        name="away",
    )(own, other, kfilt, *tables)


def inverse_here(filt, tables, pieces, shard):
    channels = filt.shape[1]
    atoms = pieces * shard * len(tables)
    return pl.pallas_call(
        functools.partial(here_kernel, pieces, shard),
        in_specs=[VMEM] * (1 + len(tables)),
        out_specs=VMEM,
        out_shape=jax.ShapeDtypeStruct((channels, atoms), F32),
        compiler_params=params(),
        cost_estimate=inverse_cost(tables, channels),
        name="here",
    )(filt, *tables)


def join_kernel(here_ref, arrived_ref, own_ref, *send_refs):
    width = own_ref.shape[1]
    for p in range(len(send_refs) + 1):
        lanes = slice(p * width, (p + 1) * width)
        total = here_ref[:, lanes] + arrived_ref[:, lanes].astype(F32)
        if p:
            send_refs[p - 1][...] = total.astype(BF16)
        else:
            own_ref[...] = total


def join(here, arrived, pieces):
    channels, atoms = here.shape
    shape = (channels, atoms // pieces)
    return pl.pallas_call(
        join_kernel,
        in_specs=[VMEM] * 2,
        out_specs=[VMEM] * pieces,
        out_shape=[jax.ShapeDtypeStruct(shape, F32)]
        + [jax.ShapeDtypeStruct(shape, BF16)] * (pieces - 1),
        compiler_params=params(),
        name="join",
    )(here, arrived)


def pair_kernel(nbasis, pieces, output_scale, slots_ref, same_ref, own_pos_ref, *refs):
    message_refs, refs = refs[: 2 * pieces + 1], refs[2 * pieces + 1 :]
    weight_ref, out_ref, feat_scr, pos_scr, own_scr, basis_scr, acc_scr = refs
    block = BLOCK_ATOMS
    width = 12.0 / nbasis
    own_blocks, neighbours = slots_ref.shape
    shard = own_blocks * block
    rows_of = shard + own_blocks * TAIL

    def unpack(place, ref, first):
        feat_scr[place * shard : (place + 1) * shard, :] = ref[first : first + shard, :]
        for b in range(own_blocks):
            tail = ref[first + shard + b * TAIL : first + shard + (b + 1) * TAIL, :].astype(F32)
            at = place * shard + b * block
            pos_scr[0:3, at : at + block] = (tail[0:3] + tail[3:6] + tail[6:9]) * 8.0

    for place in range(2 * pieces):
        unpack(place, message_refs[place], 0)
    for piece in range(pieces):
        unpack(2 * pieces + piece, message_refs[-1], piece * rows_of)
    rows = 64
    ident = lax.broadcasted_iota(jnp.int32, (rows, block), 0) - lax.broadcasted_iota(
        jnp.int32, (rows, block), 1
    )
    for b in range(own_blocks):
        for d in range(3):
            row = own_pos_ref[d : d + 1, b * block : (b + 1) * block]
            own_scr[d] = jnp.broadcast_to(row, (block, block)).T
        acc_scr[...] = jnp.zeros_like(acc_scr)

        def pair(jp, carry):
            blocks = []
            for h in range(2):
                slot = pl.multiple_of(slots_ref[b, 2 * jp + h] * block, block)
                same = same_ref[b, 2 * jp + h]
                blocks.append(feat_scr[pl.ds(slot, block), :])
                near = [pos_scr[d : d + 1, pl.ds(slot, block)] for d in range(3)]
                for part in range(block // rows):
                    at = part * rows
                    dist2 = (own_scr[0, at : at + rows, :] - near[0]) ** 2
                    dist2 += (own_scr[1, at : at + rows, :] - near[1]) ** 2
                    dist2 += (own_scr[2, at : at + rows, :] - near[2]) ** 2
                    radius = dist2 * lax.rsqrt(jnp.maximum(dist2, 1e-30))
                    env = output_scale / (1.0 + dist2 * (1.0 / 16.0))
                    drop = (ident + at == 0) & (same != 0)
                    env = jnp.where(drop, 0.0, env)
                    v = radius * (1.0 / width) - 0.5
                    value = jnp.exp(-0.5 * v * v) * env
                    ratio = jnp.exp(v)
                    for k in range(nbasis):
                        if k:
                            value = value * ratio
                        basis_scr[
                            k * block + at : k * block + at + rows, h * block : (h + 1) * block
                        ] = value.astype(BF16)
            acc_scr[...] += jnp.dot(
                basis_scr[...], jnp.concatenate(blocks, axis=0), preferred_element_type=F32
            )
            return carry

        lax.fori_loop(0, neighbours // 2, pair, 0)
        channels = out_ref.shape[1]
        total = jnp.zeros((block, channels), F32)
        for k in range(nbasis):
            gathered = (acc_scr[k * block : (k + 1) * block, :] * math.exp(-0.5 * k * k)).astype(BF16)
            total += jnp.dot(
                gathered,
                weight_ref[k * channels : (k + 1) * channels, :],
                preferred_element_type=F32,
            )
        out_ref[b * block : (b + 1) * block, :] = total


def pair_message(slots, same, own_pos, own, partner, halo, weight):
    channels = weight.shape[1]
    nbasis = weight.shape[0] // channels
    pieces = len(own)
    shard = own_pos.shape[1]
    neighbours = slots.shape[1]
    scale = float(neighbours * BLOCK_ATOMS) ** (-0.5)
    window = 3 * pieces * shard
    return pl.pallas_call(
        functools.partial(pair_kernel, nbasis, pieces, scale),
        in_specs=[SMEM, SMEM] + [VMEM] * (2 * pieces + 3),
        out_specs=VMEM,
        out_shape=jax.ShapeDtypeStruct((shard, channels), F32),
        scratch_shapes=[
            pltpu.VMEM((window, channels), BF16),
            pltpu.VMEM((8, window), F32),
            pltpu.VMEM((3, BLOCK_ATOMS, BLOCK_ATOMS), F32),
            pltpu.VMEM((nbasis * BLOCK_ATOMS, 2 * BLOCK_ATOMS), BF16),
            pltpu.VMEM((nbasis * BLOCK_ATOMS, channels), F32),
        ],
        compiler_params=params(),
        cost_estimate=pl.CostEstimate(
            flops=2 * shard * neighbours * BLOCK_ATOMS * (nbasis * channels + 40),
            bytes_accessed=2 * window * channels,
            transcendentals=3 * shard * neighbours * BLOCK_ATOMS,
        ),
        name="pair",
    )(slots, same, own_pos, *own, *partner, halo, weight)


def update_kernel(*refs):
    features_ref, pair_ref, gain_ref, w_in_ref, w_out_ref = refs[:5]
    parts, out_ref = refs[5:-1], refs[-1]
    long_t = parts[0][...].astype(F32)
    for part in parts[1:]:
        long_t = long_t + part[...].astype(F32)
    total = features_ref[...].astype(F32) + pair_ref[...] + long_t.T
    mean = jnp.mean(total * total, axis=-1, keepdims=True)
    normed = (total * lax.rsqrt(mean + 1e-06) * gain_ref[...]).astype(BF16)
    pre = jnp.dot(normed, w_in_ref[...], preferred_element_type=F32)
    hidden = (pre / (1.0 + jnp.exp(-pre))).astype(BF16)
    out_ref[...] = (
        total + jnp.dot(hidden, w_out_ref[...], preferred_element_type=F32)
    ).astype(BF16)


def update(features, pair_msg, gain, w_in, w_out, parts):
    return pl.pallas_call(
        update_kernel,
        in_specs=[VMEM] * (5 + len(parts)),
        out_specs=VMEM,
        out_shape=jax.ShapeDtypeStruct(features.shape, BF16),
        compiler_params=params(),
        name="update",
    )(features, pair_msg, gain[None, :], w_in, w_out, *parts)


def swap(value, axis, bits):
    return lax.ppermute(value, axis, [(i, i ^ bits) for i in range(lax.axis_size(axis))])


def per_device(
    positions,
    features,
    atom_mask,
    neighbours,
    lattice,
    pair_weight,
    kfilter,
    norm_gain,
    w_in,
    w_out,
):
    shard, channels = features.shape
    n_atoms = lax.axis_size("atoms")
    n_kvec = lax.axis_size("kvec")
    a_index = lax.axis_index("atoms")
    k_index = lax.axis_index("kvec")
    nb = shard // BLOCK_ATOMS
    group_blk = nb * n_kvec
    far = n_atoms // 4
    core = a_index % 2
    part = core + 2 * (a_index // 4)
    count = lattice.shape[1] // (2 * far)
    width = 256 if count % 256 == 0 else count
    own_lattice = lax.dynamic_slice_in_dim(lattice, part * count, count, 1)
    own_lattice = own_lattice.reshape(3, count // width, width).transpose(1, 0, 2)

    message = pack(features, atom_mask, positions)
    near = [message] + [swap(message, "atoms", 4 * z) for z in range(1, far)]
    pieces = [[item] + [swap(item, "kvec", k) for k in range(1, n_kvec)] for item in near]
    partner = [[swap(item, "atoms", 1) for item in row] for row in pieces]

    order = []
    for z in range(far):
        order += [pieces[z], partner[z]]
    total, tables = None, []
    for i, row in enumerate(order):
        result = wave(own_lattice, row, total, i == len(order) - 1, shard)
        tables.append(result[0])
        total = result[1]
    other = swap(result[2], "atoms", 2)

    halo_pairs = [(a, (a + 1) % n_atoms if a % 2 else (a - 1) % n_atoms) for a in range(n_atoms)]
    halo = lax.ppermute(jnp.concatenate(pieces[0], axis=0), "atoms", halo_pairs)
    id_group = neighbours // group_blk
    within = neighbours % group_blk
    ahead = (id_group - a_index) % n_atoms
    toward = jnp.where(core == 0, 1, n_atoms - 1)
    which = jnp.where(ahead == 0, 0, jnp.where(ahead == toward, 1, 2))
    slots = which * group_blk + ((within // nb) ^ k_index) * nb + within % nb
    mine = (a_index * n_kvec + k_index) * nb + jnp.arange(nb, dtype=jnp.int32)
    same = (neighbours == mine[:, None]).astype(jnp.int32)
    pair_msg = pair_message(
        slots.astype(jnp.int32), same, positions, pieces[0], partner[0], halo, pair_weight
    )

    kfilt = radial_filter(own_lattice, kfilter, float(n_atoms * n_kvec * shard * KW) ** (-0.5))
    filt, away = inverse_away(total, other, kfilt, tables[1::2], n_kvec, shard)
    arrived = swap(away, "atoms", 1)
    here = inverse_here(filt, tables[0::2], n_kvec, shard)
    own, *sends = join(here, arrived, n_kvec)
    for k, item in enumerate(sends):
        own = own + swap(item, "kvec", k + 1).astype(F32)
    parts = [own[:, :shard]]
    for z in range(1, far):
        parts.append(swap(own[:, z * shard : (z + 1) * shard].astype(BF16), "atoms", 4 * z))
    return update(features, pair_msg, norm_gain, w_in, w_out, parts)


def solution(mesh):
    return jax.shard_map(
        per_device,
        mesh=mesh,
        in_specs=(
            P(None, ("atoms", "kvec")),
            P(("atoms", "kvec"), None),
            P(("atoms", "kvec")),
            P(("atoms", "kvec"), None),
            P(None, "kvec"),
            P(),
            P(),
            P(),
            P(),
            P(),
        ),
        out_specs=P(("atoms", "kvec"), None),
        check_vma=False,
    )
```

```python
import functools
import math

import jax
import jax.numpy as jnp
from jax import lax
from jax.experimental import pallas as pl
from jax.experimental.pallas import tpu as pltpu
from jax.sharding import PartitionSpec as P

KW = 12288
BLOCK_ATOMS = 128
F32 = jnp.float32
BF16 = jnp.bfloat16

SIN_COEF = (4.442879586561992, -7.307818050390618, 3.5977887417720016, -0.7912382192058507)
ROUND = 12582912.0
TAIL = 16


def params(mib=16):
    return pltpu.CompilerParams(vmem_limit_bytes=mib << 20)


SMEM = pl.BlockSpec(memory_space=pltpu.SMEM)
VMEM = pl.BlockSpec(memory_space=pltpu.VMEM)


def horner(u, coef):
    acc = coef[-1] * u + coef[-2]
    for c in reversed(coef[:-2]):
        acc = acc * u + c
    return acc


def pack_kernel(features_hbm, mask_hbm, pos_hbm, out_ref, features_ref, mask_ref, pos_ref, scr, sems):
    copies = [
        pltpu.make_async_copy(source, target, sems.at[i])
        for i, (source, target) in enumerate(
            ((features_hbm, features_ref), (mask_hbm, mask_ref), (pos_hbm, pos_ref))
        )
    ]
    for copy in copies:
        copy.start()
    for copy in copies:
        copy.wait()
    channels = features_ref.shape[1]
    mask = mask_ref[...].astype(F32)
    out_ref[0:channels, :] = (features_ref[...].astype(F32).T * mask).astype(BF16)
    value = pos_ref[...] * 0.125
    high = value.astype(BF16).astype(F32)
    rest = value - high
    mid = rest.astype(BF16).astype(F32)
    scr[...] = jnp.zeros_like(scr)
    scr[0:3, :] = high
    scr[3:6, :] = mid
    scr[6:9, :] = rest - mid
    out_ref[channels : channels + TAIL, :] = scr[...].astype(BF16)


def pack(features, mask, positions):
    shard, channels = features.shape
    anywhere = pl.BlockSpec(memory_space=pltpu.HBM)
    return pl.pallas_call(
        pack_kernel,
        in_specs=[anywhere] * 3,
        out_specs=VMEM,
        out_shape=jax.ShapeDtypeStruct((channels + TAIL, shard), BF16),
        scratch_shapes=[
            pltpu.VMEM((shard, channels), BF16),
            pltpu.VMEM((1, shard), jnp.int32),
            pltpu.VMEM((3, shard), F32),
            pltpu.VMEM((TAIL, shard), F32),
            pltpu.SemaphoreType.DMA((3,)),
        ],
        compiler_params=params(),
        name="pack",
    )(features, mask[None, :], positions)


def setup_kernel(far, nbasis, scale, lattice_ref, kfilter_ref, wave_ref, kfilt_ref, scr):
    blocks, width, _ = wave_ref.shape
    a_index = lax.axis_index("atoms")
    part = a_index % 2 + 2 * (a_index // 4)
    count = blocks * width
    for j in range(blocks):
        lattice = jnp.zeros((3, width), F32)
        for p in range(2 * far):
            at = p * count + j * width
            mine = (part == p).astype(F32)
            lattice += lattice_ref[:, at : at + width].astype(F32) * mine
        scr[...] = jnp.zeros_like(scr)
        for copy in range(3):
            scr[3 * copy : 3 * copy + 3, :] = lattice
        wave_ref[j] = scr[...].T.astype(BF16)
        wave = lattice * (2.0 * math.pi / 8.0)
        kmag = jnp.sqrt(
            wave[0:1] * wave[0:1] + wave[1:2] * wave[1:2] + wave[2:3] * wave[2:3]
        )
        total = jnp.zeros(kfilt_ref.shape[1:], F32)
        for p in range(nbasis):
            basis = jnp.exp(-0.5 * ((kmag - (p + 0.5) * (21.0 / nbasis)) / (21.0 / nbasis)) ** 2)
            total += kfilter_ref[:, p : p + 1] * basis
        kfilt_ref[j] = total * scale


def setup(lattice, kfilter, far, width, scale):
    nbasis, channels = kfilter.shape
    blocks = lattice.shape[1] // (2 * far * width)
    return pl.pallas_call(
        functools.partial(setup_kernel, far, nbasis, scale),
        in_specs=[VMEM] * 2,
        out_specs=[VMEM] * 2,
        out_shape=[
            jax.ShapeDtypeStruct((blocks, width, TAIL), BF16),
            jax.ShapeDtypeStruct((blocks, channels, width), F32),
        ],
        scratch_shapes=[pltpu.VMEM((TAIL, width), F32)],
        compiler_params=params(),
        name="setup",
    )(lattice, kfilter.T)


def wave_kernel(pieces, kind, *refs):
    lattice_ref, refs = refs[0], refs[1:]
    message_refs, refs = refs[:pieces], refs[pieces:]
    before_ref, refs = (None, refs) if kind == "first" else (refs[0], refs[1:])
    table_ref, total_ref, refs = refs[0], refs[1], refs[2:]
    extra_ref, refs = (None, refs) if kind == "middle" else (refs[0], refs[1:])
    feat_scr, pos_scr, phases, buffers = refs[0], refs[1], refs[2:4], refs[4:6]
    blocks, width, _ = lattice_ref.shape
    channels, shard = feat_scr.shape[1:]
    for p, message in enumerate(message_refs):
        feat_scr[p] = message[0:channels, :]
        pos_scr[p] = message[channels:, :]
        if kind == "first":
            extra_ref[p] = message[...]
    if before_ref is None:
        total_ref[...] = jnp.zeros_like(total_ref)
    else:
        total_ref[...] = before_ref[...]
    steps = pieces * blocks

    def phase(i, slot):
        phases[slot][...] = jnp.dot(
            lattice_ref[i % blocks], pos_scr[i // blocks], preferred_element_type=F32
        )

    def table(i, slot):
        piece, block = i // blocks, i % blocks
        lanes = pl.ds(pl.multiple_of(piece * shard, shard), shard)
        rows = 16
        for at in range(0, width, rows):
            turns = phases[slot][at : at + rows, :]
            r = turns - ((turns + ROUND) - ROUND)
            s = horner(r * r, SIN_COEF) * r
            c = 1.0 - s * s
            w = jnp.maximum(c + 1.0, 1e-12)
            cosine = c.astype(BF16)
            sine = (s * (w * lax.rsqrt(w))).astype(BF16)
            buffers[slot][0, at : at + rows, :] = cosine
            buffers[slot][1, at : at + rows, :] = sine
            table_ref[block, at : at + rows, lanes] = cosine
            table_ref[blocks + block, at : at + rows, lanes] = sine

    def product(i, slot):
        piece, block = i // blocks, i % blocks
        for half in range(2):
            total_ref[half * blocks + block] += lax.dot_general(
                feat_scr[piece],
                buffers[slot][half],
                (((1,), (1,)), ((), ())),
                preferred_element_type=F32,
            )

    phase(0, 0)
    phase(1, 1)
    table(0, 0)

    def body(n, carry):
        i = 2 * n
        phase(jnp.minimum(i + 2, steps - 2), 0)
        product(i, 0)
        table(i + 1, 1)
        phase(jnp.minimum(i + 3, steps - 1), 1)
        table(jnp.minimum(i + 2, steps - 2), 0)
        product(i + 1, 1)
        return carry

    lax.fori_loop(0, steps // 2, body, 0)
    if kind == "last":
        extra_ref[...] = total_ref[...].astype(BF16)


def wave(lattice, messages, before, kind):
    blocks, width, _ = lattice.shape
    rows, shard = messages[0].shape
    channels = rows - TAIL
    pieces = len(messages)
    args = [lattice, *messages] + ([] if before is None else [before])
    factor = (2 * blocks, channels, width)
    shapes = [
        jax.ShapeDtypeStruct((2 * blocks, width, pieces * shard), BF16),
        jax.ShapeDtypeStruct(factor, F32),
    ]
    if kind == "first":
        shapes.append(jax.ShapeDtypeStruct((pieces, rows, shard), BF16))
    if kind == "last":
        shapes.append(jax.ShapeDtypeStruct(factor, BF16))
    pairs = blocks * width * pieces * shard
    return pl.pallas_call(
        functools.partial(wave_kernel, pieces, kind),
        in_specs=[VMEM] * len(args),
        out_specs=[VMEM] * len(shapes),
        out_shape=shapes,
        scratch_shapes=[
            pltpu.VMEM((pieces, channels, shard), BF16),
            pltpu.VMEM((pieces, TAIL, shard), BF16),
            pltpu.VMEM((width, shard), F32),
            pltpu.VMEM((width, shard), F32),
            pltpu.VMEM((2, width, shard), BF16),
            pltpu.VMEM((2, width, shard), BF16),
        ],
        compiler_params=params(),
        cost_estimate=pl.CostEstimate(
            flops=4 * pairs * channels, bytes_accessed=4 * pairs, transcendentals=pairs
        ),
        name="wave",
    )(*args)


def transform(filt_ref, table_refs, out_ref, pieces, shard):
    blocks = filt_ref.shape[0]
    far = len(table_refs)
    for z, table_ref in enumerate(table_refs):
        for p in range(pieces):
            acc = jnp.dot(
                filt_ref[0], table_ref[0, :, p * shard : (p + 1) * shard], preferred_element_type=F32
            )
            for j in range(1, blocks):
                acc += jnp.dot(
                    filt_ref[j],
                    table_ref[j, :, p * shard : (p + 1) * shard],
                    preferred_element_type=F32,
                )
            at = (p * far + z) * shard
            out_ref[:, at : at + shard] = acc.astype(out_ref.dtype)


def away_kernel(pieces, shard, own_ref, other_ref, kfilt_ref, _, *refs):
    table_refs, (filt_ref, out_ref) = refs[:-2], refs[-2:]
    count = kfilt_ref.shape[0]
    for j in range(2 * count):
        total = own_ref[j] + other_ref[j].astype(F32)
        filt_ref[j] = (total * kfilt_ref[j % count]).astype(BF16)
    transform(filt_ref, table_refs, out_ref, pieces, shard)


def here_kernel(pieces, shard, filt_ref, *refs):
    transform(filt_ref, refs[:-1], refs[-1], pieces, shard)


def inverse_cost(tables, channels):
    pairs = sum(math.prod(t.shape) for t in tables)
    return pl.CostEstimate(
        flops=2 * pairs * channels, bytes_accessed=2 * pairs, transcendentals=0
    )


def inverse_away(own, other, kfilt, after, tables, pieces, shard):
    channels = own.shape[1]
    atoms = pieces * shard * len(tables)
    return pl.pallas_call(
        functools.partial(away_kernel, pieces, shard),
        in_specs=[VMEM] * 3 + [pl.BlockSpec(memory_space=pl.ANY)] + [VMEM] * len(tables),
        out_specs=[VMEM] * 2,
        out_shape=[
            jax.ShapeDtypeStruct(own.shape, BF16),
            jax.ShapeDtypeStruct((channels, atoms), BF16),
        ],
        compiler_params=params(),
        cost_estimate=inverse_cost(tables, channels),
        name="away",
    )(own, other, kfilt, after, *tables)


def inverse_here(filt, tables, pieces, shard):
    channels = filt.shape[1]
    atoms = pieces * shard * len(tables)
    return pl.pallas_call(
        functools.partial(here_kernel, pieces, shard),
        in_specs=[VMEM] * (1 + len(tables)),
        out_specs=VMEM,
        out_shape=jax.ShapeDtypeStruct((channels, atoms), F32),
        compiler_params=params(),
        cost_estimate=inverse_cost(tables, channels),
        name="here",
    )(filt, *tables)


def join_kernel(here_ref, arrived_ref, own_ref, *send_refs):
    width = own_ref.shape[1]
    for p in range(len(send_refs) + 1):
        lanes = slice(p * width, (p + 1) * width)
        total = here_ref[:, lanes] + arrived_ref[:, lanes].astype(F32)
        if p:
            send_refs[p - 1][...] = total.astype(BF16)
        else:
            own_ref[...] = total


def join(here, arrived, pieces):
    channels, atoms = here.shape
    shape = (channels, atoms // pieces)
    return pl.pallas_call(
        join_kernel,
        in_specs=[VMEM] * 2,
        out_specs=[VMEM] * pieces,
        out_shape=[jax.ShapeDtypeStruct(shape, F32)]
        + [jax.ShapeDtypeStruct(shape, BF16)] * (pieces - 1),
        compiler_params=params(),
        name="join",
    )(here, arrived)


def pair_kernel(nbasis, pieces, output_scale, neighbours_ref, own_pos_ref, *refs):
    message_refs, refs = refs[: 2 * pieces + 1], refs[2 * pieces + 1 :]
    weight_ref, out_ref, feat_scr, pos_scr, own_scr, basis_scr, acc_scr = refs
    block = BLOCK_ATOMS
    width = 12.0 / nbasis
    own_blocks, neighbours = neighbours_ref.shape
    shard = own_blocks * block
    channels = out_ref.shape[1]

    views = list(message_refs[:-1]) + [message_refs[-1].at[p] for p in range(pieces)]
    for place, ref in enumerate(views):
        lanes = slice(place * shard, (place + 1) * shard)
        feat_scr[:, lanes] = ref[0:channels, :]
        parts = ref[channels:, :].astype(F32)
        pos_scr[0:3, lanes] = (parts[0:3] + parts[3:6] + parts[6:9]) * 8.0

    a_index = lax.axis_index("atoms")
    k_index = lax.axis_index("kvec")
    n_atoms = lax.axis_size("atoms")
    group_blk = own_blocks * pieces
    first = (a_index * pieces + k_index) * own_blocks
    toward = jnp.where(a_index % 2 == 0, 1, n_atoms - 1)

    def place_of(ident):
        group, within = ident // group_blk, ident % group_blk
        ahead = (group - a_index + n_atoms) % n_atoms
        which = jnp.where(ahead == 0, 0, jnp.where(ahead == toward, 1, 2))
        piece = (within // own_blocks) ^ k_index
        return (which * pieces + piece) * own_blocks + within % own_blocks

    rows = 64
    diagonal = lax.broadcasted_iota(jnp.int32, (rows, block), 0) - lax.broadcasted_iota(
        jnp.int32, (rows, block), 1
    )
    for b in range(own_blocks):
        for d in range(3):
            row = own_pos_ref[d : d + 1, b * block : (b + 1) * block]
            own_scr[d] = jnp.broadcast_to(row, (block, block)).T
        acc_scr[...] = jnp.zeros_like(acc_scr)

        def pair(jp, carry):
            near_feat = []
            for h in range(2):
                ident = neighbours_ref[b, 2 * jp + h]
                lanes = pl.ds(pl.multiple_of(place_of(ident) * block, block), block)
                same = ident == first + b
                near_feat.append(feat_scr[:, lanes])
                near = [pos_scr[d : d + 1, lanes] for d in range(3)]
                for part in range(block // rows):
                    at = part * rows
                    dist2 = (own_scr[0, at : at + rows, :] - near[0]) ** 2
                    dist2 += (own_scr[1, at : at + rows, :] - near[1]) ** 2
                    dist2 += (own_scr[2, at : at + rows, :] - near[2]) ** 2
                    radius = dist2 * lax.rsqrt(jnp.maximum(dist2, 1e-30))
                    env = output_scale / (1.0 + dist2 * (1.0 / 16.0))
                    env = jnp.where((diagonal + at == 0) & same, 0.0, env)
                    v = radius * (1.0 / width) - 0.5
                    value = jnp.exp(-0.5 * v * v) * env
                    ratio = jnp.exp(v)
                    for k in range(nbasis):
                        if k:
                            value = value * ratio
                        basis_scr[
                            k * block + at : k * block + at + rows, h * block : (h + 1) * block
                        ] = value.astype(BF16)
            acc_scr[...] += lax.dot_general(
                basis_scr[...],
                jnp.concatenate(near_feat, axis=1),
                (((1,), (1,)), ((), ())),
                preferred_element_type=F32,
            )
            return carry

        lax.fori_loop(0, neighbours // 2, pair, 0)
        total = jnp.zeros((block, channels), F32)
        for k in range(nbasis):
            gathered = (acc_scr[k * block : (k + 1) * block, :] * math.exp(-0.5 * k * k)).astype(BF16)
            total += jnp.dot(
                gathered,
                weight_ref[k * channels : (k + 1) * channels, :],
                preferred_element_type=F32,
            )
        out_ref[b * block : (b + 1) * block, :] = total


def pair_message(neighbours, own_pos, own, partner, halo, weight):
    channels = weight.shape[1]
    nbasis = weight.shape[0] // channels
    pieces = len(own)
    shard = own_pos.shape[1]
    count = neighbours.shape[1]
    scale = float(count * BLOCK_ATOMS) ** (-0.5)
    window = 3 * pieces * shard
    return pl.pallas_call(
        functools.partial(pair_kernel, nbasis, pieces, scale),
        in_specs=[SMEM] + [VMEM] * (2 * pieces + 3),
        out_specs=VMEM,
        out_shape=jax.ShapeDtypeStruct((shard, channels), F32),
        scratch_shapes=[
            pltpu.VMEM((channels, window), BF16),
            pltpu.VMEM((8, window), F32),
            pltpu.VMEM((3, BLOCK_ATOMS, BLOCK_ATOMS), F32),
            pltpu.VMEM((nbasis * BLOCK_ATOMS, 2 * BLOCK_ATOMS), BF16),
            pltpu.VMEM((nbasis * BLOCK_ATOMS, channels), F32),
        ],
        compiler_params=params(),
        cost_estimate=pl.CostEstimate(
            flops=2 * shard * count * BLOCK_ATOMS * (nbasis * channels + 40),
            bytes_accessed=2 * window * channels,
            transcendentals=3 * shard * count * BLOCK_ATOMS,
        ),
        name="pair",
    )(neighbours, own_pos, *own, *partner, halo, weight)


def update_kernel(*refs):
    features_ref, pair_ref, gain_ref, w_in_ref, w_out_ref = refs[:5]
    parts, out_ref = refs[5:-1], refs[-1]
    long_t = parts[0][...].astype(F32)
    for part in parts[1:]:
        long_t = long_t + part[...].astype(F32)
    total = features_ref[...].astype(F32) + pair_ref[...] + long_t.T
    mean = jnp.mean(total * total, axis=-1, keepdims=True)
    normed = (total * lax.rsqrt(mean + 1e-06) * gain_ref[...]).astype(BF16)
    pre = jnp.dot(normed, w_in_ref[...], preferred_element_type=F32)
    hidden = (pre / (1.0 + jnp.exp(-pre))).astype(BF16)
    out_ref[...] = (
        total + jnp.dot(hidden, w_out_ref[...], preferred_element_type=F32)
    ).astype(BF16)


def update(features, pair_msg, gain, w_in, w_out, parts):
    return pl.pallas_call(
        update_kernel,
        in_specs=[VMEM] * (5 + len(parts)),
        out_specs=VMEM,
        out_shape=jax.ShapeDtypeStruct(features.shape, BF16),
        compiler_params=params(),
        name="update",
    )(features, pair_msg, gain[None, :], w_in, w_out, *parts)


def swap(value, axis, bits):
    return lax.ppermute(value, axis, [(i, i ^ bits) for i in range(lax.axis_size(axis))])


def send(value, a_bits, k_bits):
    if not a_bits and not k_bits:
        return value
    n_atoms, n_kvec = lax.axis_size("atoms"), lax.axis_size("kvec")
    pairs = [
        (a * n_kvec + k, (a ^ a_bits) * n_kvec + (k ^ k_bits))
        for a in range(n_atoms)
        for k in range(n_kvec)
    ]
    return lax.ppermute(value, ("atoms", "kvec"), pairs)


def per_device(
    positions,
    features,
    atom_mask,
    neighbours,
    lattice,
    pair_weight,
    kfilter,
    norm_gain,
    w_in,
    w_out,
):
    shard, channels = features.shape
    n_atoms = lax.axis_size("atoms")
    n_kvec = lax.axis_size("kvec")
    far = n_atoms // 4
    count = lattice.shape[1] // (2 * far)
    width = 256 if count % 256 == 0 else count

    message = pack(features, atom_mask, positions)
    pieces = [[send(message, 4 * z, k) for k in range(n_kvec)] for z in range(far)]
    partner = [[swap(item, "atoms", 1) for item in row] for row in pieces]
    scale = float(n_atoms * n_kvec * shard * KW) ** (-0.5)
    waves, kfilt = setup(lattice, kfilter, far, width, scale)

    order = []
    for z in range(far):
        order += [pieces[z], partner[z]]
    total, tables, halo = None, [], None
    for i, row in enumerate(order):
        kind = "first" if i == 0 else "last" if i == len(order) - 1 else "middle"
        table, total, *extra = wave(waves, row, total, kind)
        tables.append(table)
        if kind == "first":
            halo_pairs = [
                (a, (a + 1) % n_atoms if a % 2 else (a - 1) % n_atoms) for a in range(n_atoms)
            ]
            halo = lax.ppermute(extra[0], "atoms", halo_pairs)
    other = swap(extra[0], "atoms", 2)

    pair_msg = pair_message(neighbours, positions, pieces[0], partner[0], halo, pair_weight)

    filt, away = inverse_away(total, other, kfilt, pair_msg, tables[1::2], n_kvec, shard)
    arrived = swap(away, "atoms", 1)
    here = inverse_here(filt, tables[0::2], n_kvec, shard)
    own, *sends = join(here, arrived, n_kvec)
    for k, item in enumerate(sends):
        own = own + swap(item, "kvec", k + 1).astype(F32)
    parts = [own[:, :shard]]
    for z in range(1, far):
        parts.append(swap(own[:, z * shard : (z + 1) * shard].astype(BF16), "atoms", 4 * z))
    return update(features, pair_msg, norm_gain, w_in, w_out, parts)


def solution(mesh):
    return jax.shard_map(
        per_device,
        mesh=mesh,
        in_specs=(
            P(None, ("atoms", "kvec")),
            P(("atoms", "kvec"), None),
            P(("atoms", "kvec")),
            P(("atoms", "kvec"), None),
            P(None, "kvec"),
            P(),
            P(),
            P(),
            P(),
            P(),
        ),
        out_specs=P(("atoms", "kvec"), None),
        check_vma=False,
    )
```

```python
import functools
import math

import jax
import jax.numpy as jnp
from jax import lax
from jax.experimental import pallas as pl
from jax.experimental.pallas import tpu as pltpu
from jax.sharding import PartitionSpec as P

KW = 12288
BLOCK_ATOMS = 128
F32 = jnp.float32
BF16 = jnp.bfloat16

SIN_COEF = (4.442879586561992, -7.307818050390618, 3.5977887417720016, -0.7912382192058507)
ROUND = 12582912.0
TAIL = 16


def params(mib=16):
    return pltpu.CompilerParams(vmem_limit_bytes=mib << 20)


SMEM = pl.BlockSpec(memory_space=pltpu.SMEM)
VMEM = pl.BlockSpec(memory_space=pltpu.VMEM)


def horner(u, coef):
    acc = coef[-1] * u + coef[-2]
    for c in reversed(coef[:-2]):
        acc = acc * u + c
    return acc


def pack_kernel(features_hbm, mask_hbm, pos_hbm, out_ref, features_ref, mask_ref, pos_ref, scr, sems):
    copies = [
        pltpu.make_async_copy(source, target, sems.at[i])
        for i, (source, target) in enumerate(
            ((features_hbm, features_ref), (mask_hbm, mask_ref), (pos_hbm, pos_ref))
        )
    ]
    for copy in copies:
        copy.start()
    for copy in copies:
        copy.wait()
    channels = features_ref.shape[1]
    mask = mask_ref[...].astype(F32)
    out_ref[0:channels, :] = (features_ref[...].astype(F32).T * mask).astype(BF16)
    value = pos_ref[...] * 0.125
    high = value.astype(BF16).astype(F32)
    rest = value - high
    mid = rest.astype(BF16).astype(F32)
    scr[...] = jnp.zeros_like(scr)
    scr[0:3, :] = high
    scr[3:6, :] = mid
    scr[6:9, :] = rest - mid
    out_ref[channels : channels + TAIL, :] = scr[...].astype(BF16)


def pack(features, mask, positions):
    shard, channels = features.shape
    anywhere = pl.BlockSpec(memory_space=pltpu.HBM)
    return pl.pallas_call(
        pack_kernel,
        in_specs=[anywhere] * 3,
        out_specs=VMEM,
        out_shape=jax.ShapeDtypeStruct((channels + TAIL, shard), BF16),
        scratch_shapes=[
            pltpu.VMEM((shard, channels), BF16),
            pltpu.VMEM((1, shard), jnp.int32),
            pltpu.VMEM((3, shard), F32),
            pltpu.VMEM((TAIL, shard), F32),
            pltpu.SemaphoreType.DMA((3,)),
        ],
        compiler_params=params(),
        name="pack",
    )(*(pltpu.with_memory_space_constraint(x, pltpu.HBM) for x in (features, mask[None, :], positions)))


def setup_kernel(far, nbasis, scale, lattice_ref, kfilter_ref, wave_ref, kfilt_ref, scr):
    blocks, width, _ = wave_ref.shape
    a_index = lax.axis_index("atoms")
    part = a_index % 2 + 2 * (a_index // 4)
    count = blocks * width
    for j in range(blocks):
        lattice = jnp.zeros((3, width), F32)
        for p in range(2 * far):
            at = p * count + j * width
            mine = (part == p).astype(F32)
            lattice += lattice_ref[:, at : at + width].astype(F32) * mine
        scr[...] = jnp.zeros_like(scr)
        for copy in range(3):
            scr[3 * copy : 3 * copy + 3, :] = lattice
        wave_ref[j] = scr[...].T.astype(BF16)
        wave = lattice * (2.0 * math.pi / 8.0)
        kmag = jnp.sqrt(
            wave[0:1] * wave[0:1] + wave[1:2] * wave[1:2] + wave[2:3] * wave[2:3]
        )
        total = jnp.zeros(kfilt_ref.shape[1:], F32)
        for p in range(nbasis):
            basis = jnp.exp(-0.5 * ((kmag - (p + 0.5) * (21.0 / nbasis)) / (21.0 / nbasis)) ** 2)
            total += kfilter_ref[:, p : p + 1] * basis
        kfilt_ref[j] = total * scale


def setup(lattice, kfilter, far, width, scale):
    nbasis, channels = kfilter.shape
    blocks = lattice.shape[1] // (2 * far * width)
    return pl.pallas_call(
        functools.partial(setup_kernel, far, nbasis, scale),
        in_specs=[VMEM] * 2,
        out_specs=[VMEM] * 2,
        out_shape=[
            jax.ShapeDtypeStruct((blocks, width, TAIL), BF16),
            jax.ShapeDtypeStruct((blocks, channels, width), F32),
        ],
        scratch_shapes=[pltpu.VMEM((TAIL, width), F32)],
        compiler_params=params(),
        name="setup",
    )(lattice, kfilter.T)


def wave_kernel(pieces, listed, passed, start, waits, emit, low, *refs):
    refs = list(refs)
    take = lambda n: [refs.pop(0) for _ in range(n)]
    (lattice_ref,) = take(1)
    messages = take(pieces) if listed else take(1)[0]
    if listed:
        rows_of = lambda p, rows: messages[p][rows, :]
    else:
        rows_of = lambda p, rows: messages[p, rows, :]
    through = take(passed)
    before_ref = None if start else take(1)[0]
    take(waits)
    table_ref, total_ref = take(2)
    out_through = take(passed)
    joined_ref = take(1)[0] if emit else None
    low_ref = take(1)[0] if low else None
    feat_scr, pos_scr = take(2)
    phases, buffers = take(2), take(2)
    blocks, width, _ = lattice_ref.shape
    channels, shard = feat_scr.shape[1:]
    for p in range(pieces):
        feat_scr[p] = rows_of(p, slice(0, channels))
        pos_scr[p] = rows_of(p, slice(channels, channels + TAIL))
        if emit:
            joined_ref[p] = rows_of(p, slice(0, channels + TAIL))
    for source, target in zip(through, out_through):
        target[...] = source[...]
    if start:
        total_ref[...] = jnp.zeros_like(total_ref)
    else:
        total_ref[...] = before_ref[...]
    steps = pieces * blocks

    def phase(i, slot):
        phases[slot][...] = jnp.dot(
            lattice_ref[i % blocks], pos_scr[i // blocks], preferred_element_type=F32
        )

    def table(i, slot):
        piece, block = i // blocks, i % blocks
        lanes = pl.ds(pl.multiple_of(piece * shard, shard), shard)
        rows = 16
        for at in range(0, width, rows):
            turns = phases[slot][at : at + rows, :]
            r = turns - ((turns + ROUND) - ROUND)
            s = horner(r * r, SIN_COEF) * r
            c = 1.0 - s * s
            w = jnp.maximum(c + 1.0, 1e-12)
            cosine = c.astype(BF16)
            sine = (s * (w * lax.rsqrt(w))).astype(BF16)
            buffers[slot][0, at : at + rows, :] = cosine
            buffers[slot][1, at : at + rows, :] = sine
            table_ref[block, at : at + rows, lanes] = cosine
            table_ref[blocks + block, at : at + rows, lanes] = sine

    def product(i, slot):
        piece, block = i // blocks, i % blocks
        for half in range(2):
            total_ref[half * blocks + block] += lax.dot_general(
                feat_scr[piece],
                buffers[slot][half],
                (((1,), (1,)), ((), ())),
                preferred_element_type=F32,
            )

    phase(0, 0)
    phase(1, 1)
    table(0, 0)

    def body(n, carry):
        i = 2 * n
        phase(jnp.minimum(i + 2, steps - 2), 0)
        product(i, 0)
        table(i + 1, 1)
        phase(jnp.minimum(i + 3, steps - 1), 1)
        table(jnp.minimum(i + 2, steps - 2), 0)
        product(i + 1, 1)
        return carry

    lax.fori_loop(0, steps // 2, body, 0)
    if low:
        low_ref[...] = total_ref[...].astype(BF16)


def wave(lattice, messages, before, through=(), after=(), emit=False, low=False):
    blocks, width, _ = lattice.shape
    listed = isinstance(messages, (list, tuple))
    pieces = len(messages) if listed else messages.shape[0]
    sources = list(messages) if listed else [messages]
    rows, shard = sources[0].shape[-2:]
    channels = rows - TAIL
    args = [lattice, *sources, *through] + ([] if before is None else [before])
    factor = (2 * blocks, channels, width)
    shapes = [
        jax.ShapeDtypeStruct((2 * blocks, width, pieces * shard), BF16),
        jax.ShapeDtypeStruct(factor, F32),
    ]
    shapes += [jax.ShapeDtypeStruct(x.shape, x.dtype) for x in through]
    if emit:
        shapes.append(jax.ShapeDtypeStruct((pieces, rows, shard), BF16))
    if low:
        shapes.append(jax.ShapeDtypeStruct(factor, BF16))
    pairs = blocks * width * pieces * shard
    return pl.pallas_call(
        functools.partial(
            wave_kernel, pieces, listed, len(through), before is None, len(after), emit, low
        ),
        in_specs=[VMEM] * len(args) + [pl.BlockSpec(memory_space=pl.ANY)] * len(after),
        out_specs=[VMEM] * len(shapes),
        out_shape=shapes,
        scratch_shapes=[
            pltpu.VMEM((pieces, channels, shard), BF16),
            pltpu.VMEM((pieces, TAIL, shard), BF16),
            pltpu.VMEM((width, shard), F32),
            pltpu.VMEM((width, shard), F32),
            pltpu.VMEM((2, width, shard), BF16),
            pltpu.VMEM((2, width, shard), BF16),
        ],
        compiler_params=params(),
        cost_estimate=pl.CostEstimate(
            flops=4 * pairs * channels, bytes_accessed=4 * pairs, transcendentals=pairs
        ),
        name="wave",
    )(*args, *after)


def gather_kernel(*refs):
    for p, ref in enumerate(refs[1:-1]):
        refs[-1][p] = ref[...]


def gather(after, messages):
    return pl.pallas_call(
        gather_kernel,
        in_specs=[pl.BlockSpec(memory_space=pl.ANY)] + [VMEM] * len(messages),
        out_specs=VMEM,
        out_shape=jax.ShapeDtypeStruct((len(messages), *messages[0].shape), BF16),
        compiler_params=params(),
        name="gather",
    )(after, *messages)


def transform(filt_ref, table_refs, out_ref, pieces, shard):
    blocks = filt_ref.shape[0]
    far = len(table_refs)
    for z, table_ref in enumerate(table_refs):
        for p in range(pieces):
            acc = jnp.dot(
                filt_ref[0], table_ref[0, :, p * shard : (p + 1) * shard], preferred_element_type=F32
            )
            for j in range(1, blocks):
                acc += jnp.dot(
                    filt_ref[j],
                    table_ref[j, :, p * shard : (p + 1) * shard],
                    preferred_element_type=F32,
                )
            at = (p * far + z) * shard
            out_ref[:, at : at + shard] = acc.astype(out_ref.dtype)


def away_kernel(pieces, shard, own_ref, other_ref, kfilt_ref, _, *refs):
    table_refs, (filt_ref, out_ref) = refs[:-2], refs[-2:]
    count = kfilt_ref.shape[0]
    for j in range(2 * count):
        total = own_ref[j] + other_ref[j].astype(F32)
        filt_ref[j] = (total * kfilt_ref[j % count]).astype(BF16)
    transform(filt_ref, table_refs, out_ref, pieces, shard)


def here_kernel(pieces, shard, filt_ref, *refs):
    transform(filt_ref, refs[:-1], refs[-1], pieces, shard)


def inverse_cost(tables, channels):
    pairs = sum(math.prod(t.shape) for t in tables)
    return pl.CostEstimate(
        flops=2 * pairs * channels, bytes_accessed=2 * pairs, transcendentals=0
    )


def inverse_away(own, other, kfilt, after, tables, pieces, shard):
    channels = own.shape[1]
    atoms = pieces * shard * len(tables)
    return pl.pallas_call(
        functools.partial(away_kernel, pieces, shard),
        in_specs=[VMEM] * 3 + [pl.BlockSpec(memory_space=pl.ANY)] + [VMEM] * len(tables),
        out_specs=[VMEM] * 2,
        out_shape=[
            jax.ShapeDtypeStruct(own.shape, BF16),
            jax.ShapeDtypeStruct((channels, atoms), BF16),
        ],
        compiler_params=params(),
        cost_estimate=inverse_cost(tables, channels),
        name="away",
    )(own, other, kfilt, after, *tables)


def inverse_here(filt, tables, pieces, shard):
    channels = filt.shape[1]
    atoms = pieces * shard * len(tables)
    return pl.pallas_call(
        functools.partial(here_kernel, pieces, shard),
        in_specs=[VMEM] * (1 + len(tables)),
        out_specs=VMEM,
        out_shape=jax.ShapeDtypeStruct((channels, atoms), F32),
        compiler_params=params(),
        cost_estimate=inverse_cost(tables, channels),
        name="here",
    )(filt, *tables)


def join_kernel(here_ref, arrived_ref, own_ref, *send_refs):
    width = own_ref.shape[1]
    for p in range(len(send_refs) + 1):
        lanes = slice(p * width, (p + 1) * width)
        total = here_ref[:, lanes] + arrived_ref[:, lanes].astype(F32)
        if p:
            send_refs[p - 1][...] = total.astype(BF16)
        else:
            own_ref[...] = total


def join(here, arrived, pieces):
    channels, atoms = here.shape
    shape = (channels, atoms // pieces)
    return pl.pallas_call(
        join_kernel,
        in_specs=[VMEM] * 2,
        out_specs=[VMEM] * pieces,
        out_shape=[jax.ShapeDtypeStruct(shape, F32)]
        + [jax.ShapeDtypeStruct(shape, BF16)] * (pieces - 1),
        compiler_params=params(),
        name="join",
    )(here, arrived)


def pair_kernel(nbasis, pieces, output_scale, neighbours_ref, own_pos_ref, *refs):
    message_refs, refs = refs[:3], refs[3:]
    weight_ref, out_ref, feat_scr, pos_scr, own_scr, basis_scr, acc_scr = refs
    block = BLOCK_ATOMS
    width = 12.0 / nbasis
    own_blocks, neighbours = neighbours_ref.shape
    shard = own_blocks * block
    channels = out_ref.shape[1]

    views = [ref.at[p] for ref in message_refs for p in range(pieces)]
    for place, ref in enumerate(views):
        lanes = slice(place * shard, (place + 1) * shard)
        feat_scr[:, lanes] = ref[0:channels, :]
        parts = ref[channels:, :].astype(F32)
        pos_scr[0:3, lanes] = (parts[0:3] + parts[3:6] + parts[6:9]) * 8.0

    a_index = lax.axis_index("atoms")
    k_index = lax.axis_index("kvec")
    n_atoms = lax.axis_size("atoms")
    group_blk = own_blocks * pieces
    first = (a_index * pieces + k_index) * own_blocks
    toward = jnp.where(a_index % 2 == 0, 1, n_atoms - 1)

    def place_of(ident):
        group, within = ident // group_blk, ident % group_blk
        ahead = (group - a_index + n_atoms) % n_atoms
        which = jnp.where(ahead == 0, 0, jnp.where(ahead == toward, 1, 2))
        piece = (within // own_blocks) ^ k_index
        return (which * pieces + piece) * own_blocks + within % own_blocks

    rows = 64
    diagonal = lax.broadcasted_iota(jnp.int32, (rows, block), 0) - lax.broadcasted_iota(
        jnp.int32, (rows, block), 1
    )
    for b in range(own_blocks):
        for d in range(3):
            row = own_pos_ref[d : d + 1, b * block : (b + 1) * block]
            own_scr[d] = jnp.broadcast_to(row, (block, block)).T
        acc_scr[...] = jnp.zeros_like(acc_scr)

        def pair(jp, carry):
            near_feat = []
            for h in range(2):
                ident = neighbours_ref[b, 2 * jp + h]
                lanes = pl.ds(pl.multiple_of(place_of(ident) * block, block), block)
                same = ident == first + b
                near_feat.append(feat_scr[:, lanes])
                near = [pos_scr[d : d + 1, lanes] for d in range(3)]
                for part in range(block // rows):
                    at = part * rows
                    dist2 = (own_scr[0, at : at + rows, :] - near[0]) ** 2
                    dist2 += (own_scr[1, at : at + rows, :] - near[1]) ** 2
                    dist2 += (own_scr[2, at : at + rows, :] - near[2]) ** 2
                    radius = dist2 * lax.rsqrt(jnp.maximum(dist2, 1e-30))
                    env = output_scale / (1.0 + dist2 * (1.0 / 16.0))
                    env = jnp.where((diagonal + at == 0) & same, 0.0, env)
                    v = radius * (1.0 / width) - 0.5
                    value = jnp.exp(-0.5 * v * v) * env
                    ratio = jnp.exp(v)
                    for k in range(nbasis):
                        if k:
                            value = value * ratio
                        basis_scr[
                            k * block + at : k * block + at + rows, h * block : (h + 1) * block
                        ] = value.astype(BF16)
            acc_scr[...] += lax.dot_general(
                basis_scr[...],
                jnp.concatenate(near_feat, axis=1),
                (((1,), (1,)), ((), ())),
                preferred_element_type=F32,
            )
            return carry

        lax.fori_loop(0, neighbours // 2, pair, 0)
        total = jnp.zeros((block, channels), F32)
        for k in range(nbasis):
            gathered = (acc_scr[k * block : (k + 1) * block, :] * math.exp(-0.5 * k * k)).astype(BF16)
            total += jnp.dot(
                gathered,
                weight_ref[k * channels : (k + 1) * channels, :],
                preferred_element_type=F32,
            )
        out_ref[b * block : (b + 1) * block, :] = total


def pair_message(neighbours, own_pos, own, partner, halo, weight):
    channels = weight.shape[1]
    nbasis = weight.shape[0] // channels
    pieces = own.shape[0]
    shard = own_pos.shape[1]
    count = neighbours.shape[1]
    scale = float(count * BLOCK_ATOMS) ** (-0.5)
    window = 3 * pieces * shard
    return pl.pallas_call(
        functools.partial(pair_kernel, nbasis, pieces, scale),
        in_specs=[SMEM] + [VMEM] * 5,
        out_specs=VMEM,
        out_shape=jax.ShapeDtypeStruct((shard, channels), F32),
        scratch_shapes=[
            pltpu.VMEM((channels, window), BF16),
            pltpu.VMEM((8, window), F32),
            pltpu.VMEM((3, BLOCK_ATOMS, BLOCK_ATOMS), F32),
            pltpu.VMEM((nbasis * BLOCK_ATOMS, 2 * BLOCK_ATOMS), BF16),
            pltpu.VMEM((nbasis * BLOCK_ATOMS, channels), F32),
        ],
        compiler_params=params(),
        cost_estimate=pl.CostEstimate(
            flops=2 * shard * count * BLOCK_ATOMS * (nbasis * channels + 40),
            bytes_accessed=2 * window * channels,
            transcendentals=3 * shard * count * BLOCK_ATOMS,
        ),
        name="pair",
    )(neighbours, own_pos, own, partner, halo, weight)


def update_kernel(*refs):
    features_ref, pair_ref, gain_ref, w_in_ref, w_out_ref = refs[:5]
    parts, out_ref = refs[5:-1], refs[-1]
    long_t = parts[0][...].astype(F32)
    for part in parts[1:]:
        long_t = long_t + part[...].astype(F32)
    total = features_ref[...].astype(F32) + pair_ref[...] + long_t.T
    mean = jnp.mean(total * total, axis=-1, keepdims=True)
    normed = (total * lax.rsqrt(mean + 1e-06) * gain_ref[...]).astype(BF16)
    pre = jnp.dot(normed, w_in_ref[...], preferred_element_type=F32)
    hidden = (pre / (1.0 + jnp.exp(-pre))).astype(BF16)
    out_ref[...] = (
        total + jnp.dot(hidden, w_out_ref[...], preferred_element_type=F32)
    ).astype(BF16)


def update(features, pair_msg, gain, w_in, w_out, parts):
    return pl.pallas_call(
        update_kernel,
        in_specs=[VMEM] * (5 + len(parts)),
        out_specs=VMEM,
        out_shape=jax.ShapeDtypeStruct(features.shape, BF16),
        compiler_params=params(),
        name="update",
    )(features, pair_msg, gain[None, :], w_in, w_out, *parts)


def swap(value, axis, bits):
    return lax.ppermute(value, axis, [(i, i ^ bits) for i in range(lax.axis_size(axis))])


def per_device(
    positions,
    features,
    atom_mask,
    neighbours,
    lattice,
    pair_weight,
    kfilter,
    norm_gain,
    w_in,
    w_out,
):
    shard, channels = features.shape
    n_atoms = lax.axis_size("atoms")
    n_kvec = lax.axis_size("kvec")
    far = n_atoms // 4
    count = lattice.shape[1] // (2 * far)
    width = 256 if count % 256 == 0 else count

    message = pack(features, atom_mask, positions)
    scale = float(n_atoms * n_kvec * shard * KW) ** (-0.5)
    waves, kfilt = setup(lattice, kfilter, far, width, scale)
    own = [message] + [swap(message, "kvec", k) for k in range(1, n_kvec)]
    distant = [swap(message, "atoms", 4 * z) for z in range(1, far)]

    tables = [None] * (2 * far)
    tables[0], total, *distant, joined = wave(waves, own, None, through=distant, emit=True)
    partner = swap(joined, "atoms", 1)
    relayed = [[item] + [swap(item, "kvec", k) for k in range(1, n_kvec)] for item in distant]
    tables[1], total, beyond = wave(waves, partner, total, emit=True)
    halo_pairs = [(a, (a + 2) % n_atoms if a % 2 == 0 else (a - 2) % n_atoms) for a in range(n_atoms)]
    halo = lax.ppermute(beyond, "atoms", halo_pairs)
    for z in range(1, far):
        both = gather(total, relayed[z - 1])
        crossed = swap(both, "atoms", 1)
        tables[2 * z], total = wave(waves, both, total)
        tables[2 * z + 1], total, *low = wave(
            waves, crossed, total, after=(halo,) if z == 1 else (), low=z == far - 1
        )
    other = swap(low[0], "atoms", 2)

    pair_msg = pair_message(neighbours, positions, joined, partner, halo, pair_weight)

    filt, away = inverse_away(total, other, kfilt, pair_msg, tables[1::2], n_kvec, shard)
    arrived = swap(away, "atoms", 1)
    here = inverse_here(filt, tables[0::2], n_kvec, shard)
    own, *sends = join(here, arrived, n_kvec)
    for k, item in enumerate(sends):
        own = own + swap(item, "kvec", k + 1).astype(F32)
    parts = [own[:, :shard]]
    for z in range(1, far):
        parts.append(swap(own[:, z * shard : (z + 1) * shard].astype(BF16), "atoms", 4 * z))
    return update(features, pair_msg, norm_gain, w_in, w_out, parts)


def solution(mesh):
    return jax.shard_map(
        per_device,
        mesh=mesh,
        in_specs=(
            P(None, ("atoms", "kvec")),
            P(("atoms", "kvec"), None),
            P(("atoms", "kvec")),
            P(("atoms", "kvec"), None),
            P(None, "kvec"),
            P(),
            P(),
            P(),
            P(),
            P(),
        ),
        out_specs=P(("atoms", "kvec"), None),
        check_vma=False,
    )
```

```python
import functools
import math

import jax
import jax.numpy as jnp
from jax import lax
from jax.experimental import pallas as pl
from jax.experimental.pallas import tpu as pltpu
from jax.sharding import PartitionSpec as P

KW = 12288
BLOCK_ATOMS = 128
F32 = jnp.float32
BF16 = jnp.bfloat16

SIN_COEF = (4.442879586561992, -7.307818050390618, 3.5977887417720016, -0.7912382192058507)
ROUND = 12582912.0
SLACK = 1e-5
TAIL = 16


def params(mib=16):
    return pltpu.CompilerParams(vmem_limit_bytes=mib << 20)


SMEM = pl.BlockSpec(memory_space=pltpu.SMEM)
VMEM = pl.BlockSpec(memory_space=pltpu.VMEM)
ANY = pl.BlockSpec(memory_space=pl.ANY)


def horner(u, coef):
    acc = coef[-1] * u + coef[-2]
    for c in reversed(coef[:-2]):
        acc = acc * u + c
    return acc


def pack_kernel(features_hbm, mask_hbm, pos_hbm, out_ref, features_ref, mask_ref, pos_ref, scr, sems):
    copies = [
        pltpu.make_async_copy(source, target, sems.at[i])
        for i, (source, target) in enumerate(
            ((features_hbm, features_ref), (mask_hbm, mask_ref), (pos_hbm, pos_ref))
        )
    ]
    for copy in copies:
        copy.start()
    for copy in copies:
        copy.wait()
    channels = features_ref.shape[1]
    mask = mask_ref[...].astype(F32)
    out_ref[0:channels, :] = (features_ref[...].astype(F32).T * mask).astype(BF16)
    value = pos_ref[...] * 0.125
    high = value.astype(BF16).astype(F32)
    rest = value - high
    mid = rest.astype(BF16).astype(F32)
    scr[...] = jnp.zeros_like(scr)
    scr[0:3, :] = high
    scr[3:6, :] = mid
    scr[6:9, :] = rest - mid
    out_ref[channels : channels + TAIL, :] = scr[...].astype(BF16)


def pack(features, mask, positions):
    shard, channels = features.shape
    anywhere = pl.BlockSpec(memory_space=pltpu.HBM)
    return pl.pallas_call(
        pack_kernel,
        in_specs=[anywhere] * 3,
        out_specs=VMEM,
        out_shape=jax.ShapeDtypeStruct((channels + TAIL, shard), BF16),
        scratch_shapes=[
            pltpu.VMEM((shard, channels), BF16),
            pltpu.VMEM((1, shard), jnp.int32),
            pltpu.VMEM((3, shard), F32),
            pltpu.VMEM((TAIL, shard), F32),
            pltpu.SemaphoreType.DMA((3,)),
        ],
        compiler_params=params(),
        name="pack",
    )(*(pltpu.with_memory_space_constraint(x, pltpu.HBM) for x in (features, mask[None, :], positions)))


def setup_kernel(far, nbasis, scale, lattice_ref, kfilter_ref, wave_ref, kfilt_ref, scr):
    blocks, width, _ = wave_ref.shape
    a_index = lax.axis_index("atoms")
    part = a_index % 2 + 2 * (a_index // 4)
    count = blocks * width
    for j in range(blocks):
        lattice = jnp.zeros((3, width), F32)
        for p in range(2 * far):
            at = p * count + j * width
            mine = (part == p).astype(F32)
            lattice += lattice_ref[:, at : at + width].astype(F32) * mine
        scr[...] = jnp.zeros_like(scr)
        for copy in range(3):
            scr[3 * copy : 3 * copy + 3, :] = lattice
        wave_ref[j] = scr[...].T.astype(BF16)
        wave = lattice * (2.0 * math.pi / 8.0)
        kmag = jnp.sqrt(
            wave[0:1] * wave[0:1] + wave[1:2] * wave[1:2] + wave[2:3] * wave[2:3]
        )
        total = jnp.zeros(kfilt_ref.shape[1:], F32)
        for p in range(nbasis):
            basis = jnp.exp(-0.5 * ((kmag - (p + 0.5) * (21.0 / nbasis)) / (21.0 / nbasis)) ** 2)
            total += kfilter_ref[:, p : p + 1] * basis
        kfilt_ref[j] = total * scale


def setup(lattice, kfilter, far, width, scale):
    nbasis, channels = kfilter.shape
    blocks = lattice.shape[1] // (2 * far * width)
    return pl.pallas_call(
        functools.partial(setup_kernel, far, nbasis, scale),
        in_specs=[VMEM] * 2,
        out_specs=[VMEM] * 2,
        out_shape=[
            jax.ShapeDtypeStruct((blocks, width, TAIL), BF16),
            jax.ShapeDtypeStruct((blocks, channels, width), F32),
        ],
        scratch_shapes=[pltpu.VMEM((TAIL, width), F32)],
        compiler_params=params(),
        name="setup",
    )(lattice, kfilter.T)


def wave_kernel(counts, start, waits, low, *refs):
    refs = list(refs)
    take = lambda n: [refs.pop(0) for _ in range(n)]
    (lattice_ref,) = take(1)
    messages = take(len(counts))
    before_ref = None if start else take(1)[0]
    take(waits)
    table_ref, total_ref = take(2)
    low_ref = take(1)[0] if low else None
    feat_scr, pos_scr = take(2)
    phases, buffers = take(2), take(2)
    blocks, width, _ = lattice_ref.shape
    pairs, channels, both = feat_scr.shape
    shard = both // 2
    place = 0
    for ref, count in zip(messages, counts):
        for p in range(count):
            lanes = slice(place % 2 * shard, (place % 2 + 1) * shard)
            feat_scr[place // 2, :, lanes] = ref[p, 0:channels, :]
            pos_scr[place // 2, :, lanes] = ref[p, channels:, :]
            place += 1
    if start:
        total_ref[...] = jnp.zeros_like(total_ref)
    else:
        total_ref[...] = before_ref[...]
    for buffer in buffers:
        buffer[...] = jnp.zeros_like(buffer)
    steps = pairs * blocks

    def phase(i, side):
        phases[side][...] = jnp.dot(
            lattice_ref[i % blocks],
            pos_scr[i // blocks, :, side * shard : (side + 1) * shard],
            preferred_element_type=F32,
        )

    def table(i, side):
        pair, block = i // blocks, i % blocks
        lanes = pl.ds(pl.multiple_of(pair * both + side * shard, shard), shard)
        rows = 16
        for at in range(0, width, rows):
            turns = phases[side][at : at + rows, :]
            r = turns - ((turns + ROUND) - ROUND)
            s = horner(r * r, SIN_COEF) * r
            square = s * s
            w = (2.0 + SLACK) - square
            cosine = (1.0 - square).astype(BF16)
            sine = (s * (w * lax.rsqrt(w))).astype(BF16)
            buffers[side][0, at : at + rows, :] = cosine
            buffers[side][1, at : at + rows, :] = sine
            table_ref[block, at : at + rows, lanes] = cosine
            table_ref[blocks + block, at : at + rows, lanes] = sine

    def product(i):
        pair, block = i // blocks, i % blocks
        for half in range(2):
            parts = [
                lax.dot_general(
                    feat_scr[pair, :, side * shard : (side + 1) * shard],
                    buffers[side][half],
                    (((1,), (1,)), ((), ())),
                    preferred_element_type=F32,
                )
                for side in range(2)
            ]
            total_ref[half * blocks + block] += parts[0] + parts[1]

    phase(0, 0)
    phase(0, 1)

    def body(i, carry):
        later = jnp.minimum(i + 1, steps - 1)
        product(jnp.maximum(i - 1, 0))
        table(i, 0)
        phase(later, 0)
        table(i, 1)
        phase(later, 1)
        return carry

    lax.fori_loop(0, steps, body, 0)
    product(steps - 1)
    if low:
        low_ref[...] = total_ref[...].astype(BF16)


def wave(lattice, messages, before, after=(), low=False):
    blocks, width, _ = lattice.shape
    counts = tuple(x.shape[0] for x in messages)
    pieces = sum(counts)
    rows, shard = messages[0].shape[1:]
    channels = rows - TAIL
    args = [lattice, *messages] + ([] if before is None else [before])
    factor = (2 * blocks, channels, width)
    shapes = [
        jax.ShapeDtypeStruct((2 * blocks, width, pieces * shard), BF16),
        jax.ShapeDtypeStruct(factor, F32),
    ]
    if low:
        shapes.append(jax.ShapeDtypeStruct(factor, BF16))
    pairs = blocks * width * pieces * shard
    return pl.pallas_call(
        functools.partial(wave_kernel, counts, before is None, len(after), low),
        in_specs=[VMEM] * len(args) + [ANY] * len(after),
        out_specs=[VMEM] * len(shapes),
        out_shape=shapes,
        scratch_shapes=[
            pltpu.VMEM((pieces // 2, channels, 2 * shard), BF16),
            pltpu.VMEM((pieces // 2, TAIL, 2 * shard), BF16),
            pltpu.VMEM((width, shard), F32),
            pltpu.VMEM((width, shard), F32),
            pltpu.VMEM((2, width, shard), BF16),
            pltpu.VMEM((2, width, shard), BF16),
        ],
        compiler_params=params(),
        cost_estimate=pl.CostEstimate(
            flops=4 * pairs * channels, bytes_accessed=4 * pairs, transcendentals=pairs
        ),
        name="wave",
    )(*args, *after)


def collect_kernel(picks, *refs):
    for p, (array, index) in enumerate(picks):
        ref = refs[array]
        refs[-1][p] = ref[...] if index is None else ref[index]


def collect(arrays, picks, after=()):
    return pl.pallas_call(
        functools.partial(collect_kernel, picks),
        in_specs=[VMEM] * len(arrays) + [ANY] * len(after),
        out_specs=VMEM,
        out_shape=jax.ShapeDtypeStruct((len(picks), *arrays[0].shape[-2:]), BF16),
        compiler_params=params(),
        name="collect",
    )(*arrays, *after)


def transform(filt_ref, parts, out_ref, shard):
    blocks = filt_ref.shape[0]
    at = 0
    for table_ref, first, pieces in parts:
        for p in range(first, first + pieces):
            acc = jnp.dot(
                filt_ref[0], table_ref[0, :, p * shard : (p + 1) * shard], preferred_element_type=F32
            )
            for j in range(1, blocks):
                acc += jnp.dot(
                    filt_ref[j],
                    table_ref[j, :, p * shard : (p + 1) * shard],
                    preferred_element_type=F32,
                )
            out_ref[:, at : at + shard] = acc.astype(out_ref.dtype)
            at += shard


def away_kernel(runs, shard, own_ref, other_ref, kfilt_ref, _, *refs):
    table_refs, (filt_ref, out_ref) = refs[:-2], refs[-2:]
    count = kfilt_ref.shape[0]
    for j in range(2 * count):
        total = own_ref[j] + other_ref[j].astype(F32)
        filt_ref[j] = (total * kfilt_ref[j % count]).astype(BF16)
    transform(filt_ref, [(t, *r) for t, r in zip(table_refs, runs)], out_ref, shard)


def here_kernel(runs, shard, filt_ref, *refs):
    transform(filt_ref, [(t, *r) for t, r in zip(refs[:-1], runs)], refs[-1], shard)


def inverse_cost(filt, atoms):
    return pl.CostEstimate(
        flops=2 * math.prod(filt.shape) * atoms,
        bytes_accessed=2 * math.prod(filt.shape[::2]) * atoms,
        transcendentals=0,
    )


def inverse_away(own, other, kfilt, after, tables, runs, shard):
    channels = own.shape[1]
    atoms = shard * sum(r[1] for r in runs)
    return pl.pallas_call(
        functools.partial(away_kernel, runs, shard),
        in_specs=[VMEM] * 3 + [ANY] + [VMEM] * len(tables),
        out_specs=[VMEM] * 2,
        out_shape=[
            jax.ShapeDtypeStruct(own.shape, BF16),
            jax.ShapeDtypeStruct((channels, atoms), BF16),
        ],
        compiler_params=params(),
        cost_estimate=inverse_cost(own, atoms),
        name="away",
    )(own, other, kfilt, after, *tables)


def inverse_here(filt, tables, runs, shard):
    channels = filt.shape[1]
    atoms = shard * sum(r[1] for r in runs)
    return pl.pallas_call(
        functools.partial(here_kernel, runs, shard),
        in_specs=[VMEM] * (1 + len(tables)),
        out_specs=VMEM,
        out_shape=jax.ShapeDtypeStruct((channels, atoms), F32),
        compiler_params=params(),
        cost_estimate=inverse_cost(filt, atoms),
        name="here",
    )(filt, *tables)


def join_kernel(here_ref, arrived_ref, own_ref, *send_refs):
    width = own_ref.shape[1]
    for p in range(len(send_refs) + 1):
        lanes = slice(p * width, (p + 1) * width)
        total = here_ref[:, lanes] + arrived_ref[:, lanes].astype(F32)
        if p:
            send_refs[p - 1][...] = total.astype(BF16)
        else:
            own_ref[...] = total


def join(here, arrived, pieces):
    channels, atoms = here.shape
    shape = (channels, atoms // pieces)
    return pl.pallas_call(
        join_kernel,
        in_specs=[VMEM] * 2,
        out_specs=[VMEM] * pieces,
        out_shape=[jax.ShapeDtypeStruct(shape, F32)]
        + [jax.ShapeDtypeStruct(shape, BF16)] * (pieces - 1),
        compiler_params=params(),
        name="join",
    )(here, arrived)


def pair_kernel(nbasis, pieces, output_scale, picks, arrays, neighbours_ref, own_pos_ref, *refs):
    message_refs, refs = refs[:arrays], refs[arrays:]
    weight_ref, out_ref, feat_scr, pos_scr, own_scr, basis_scr, acc_scr = refs
    block = BLOCK_ATOMS
    width = 12.0 / nbasis
    own_blocks, neighbours = neighbours_ref.shape
    shard = own_blocks * block
    channels = out_ref.shape[1]

    views = [message_refs[array].at[index] for array, index in picks]
    for place, ref in enumerate(views):
        lanes = slice(place * shard, (place + 1) * shard)
        feat_scr[:, lanes] = ref[0:channels, :]
        parts = ref[channels:, :].astype(F32)
        pos_scr[0:3, lanes] = (parts[0:3] + parts[3:6] + parts[6:9]) * 8.0

    a_index = lax.axis_index("atoms")
    k_index = lax.axis_index("kvec")
    n_atoms = lax.axis_size("atoms")
    group_blk = own_blocks * pieces
    first = (a_index * pieces + k_index) * own_blocks
    toward = jnp.where(a_index % 2 == 0, 1, n_atoms - 1)

    def place_of(ident):
        group, within = ident // group_blk, ident % group_blk
        ahead = (group - a_index + n_atoms) % n_atoms
        which = jnp.where(ahead == 0, 0, jnp.where(ahead == toward, 1, 2))
        piece = (within // own_blocks) ^ k_index
        return (which * pieces + piece) * own_blocks + within % own_blocks

    rows = 64
    diagonal = lax.broadcasted_iota(jnp.int32, (rows, block), 0) - lax.broadcasted_iota(
        jnp.int32, (rows, block), 1
    )
    for b in range(own_blocks):
        for d in range(3):
            row = own_pos_ref[d : d + 1, b * block : (b + 1) * block]
            own_scr[d] = jnp.broadcast_to(row, (block, block)).T
        acc_scr[...] = jnp.zeros_like(acc_scr)

        def pair(jp, carry):
            near_feat = []
            for h in range(2):
                ident = neighbours_ref[b, 2 * jp + h]
                lanes = pl.ds(pl.multiple_of(place_of(ident) * block, block), block)
                same = ident == first + b
                near_feat.append(feat_scr[:, lanes])
                near = [pos_scr[d : d + 1, lanes] for d in range(3)]
                for part in range(block // rows):
                    at = part * rows
                    dist2 = (own_scr[0, at : at + rows, :] - near[0]) ** 2
                    dist2 += (own_scr[1, at : at + rows, :] - near[1]) ** 2
                    dist2 += (own_scr[2, at : at + rows, :] - near[2]) ** 2
                    radius = dist2 * lax.rsqrt(jnp.maximum(dist2, 1e-30))
                    env = output_scale / (1.0 + dist2 * (1.0 / 16.0))
                    env = jnp.where((diagonal + at == 0) & same, 0.0, env)
                    v = radius * (1.0 / width) - 0.5
                    value = jnp.exp(-0.5 * v * v) * env
                    ratio = jnp.exp(v)
                    for k in range(nbasis):
                        if k:
                            value = value * ratio
                        basis_scr[
                            k * block + at : k * block + at + rows, h * block : (h + 1) * block
                        ] = value.astype(BF16)
            acc_scr[...] += lax.dot_general(
                basis_scr[...],
                jnp.concatenate(near_feat, axis=1),
                (((1,), (1,)), ((), ())),
                preferred_element_type=F32,
            )
            return carry

        lax.fori_loop(0, neighbours // 2, pair, 0)
        total = jnp.zeros((block, channels), F32)
        for k in range(nbasis):
            gathered = (acc_scr[k * block : (k + 1) * block, :] * math.exp(-0.5 * k * k)).astype(BF16)
            total += jnp.dot(
                gathered,
                weight_ref[k * channels : (k + 1) * channels, :],
                preferred_element_type=F32,
            )
        out_ref[b * block : (b + 1) * block, :] = total


def pair_message(neighbours, own_pos, arrays, picks, weight):
    channels = weight.shape[1]
    nbasis = weight.shape[0] // channels
    pieces = len(picks) // 3
    shard = own_pos.shape[1]
    count = neighbours.shape[1]
    scale = float(count * BLOCK_ATOMS) ** (-0.5)
    window = 3 * pieces * shard
    return pl.pallas_call(
        functools.partial(pair_kernel, nbasis, pieces, scale, picks, len(arrays)),
        in_specs=[SMEM] + [VMEM] * (2 + len(arrays)),
        out_specs=VMEM,
        out_shape=jax.ShapeDtypeStruct((shard, channels), F32),
        scratch_shapes=[
            pltpu.VMEM((channels, window), BF16),
            pltpu.VMEM((8, window), F32),
            pltpu.VMEM((3, BLOCK_ATOMS, BLOCK_ATOMS), F32),
            pltpu.VMEM((nbasis * BLOCK_ATOMS, 2 * BLOCK_ATOMS), BF16),
            pltpu.VMEM((nbasis * BLOCK_ATOMS, channels), F32),
        ],
        compiler_params=params(),
        cost_estimate=pl.CostEstimate(
            flops=2 * shard * count * BLOCK_ATOMS * (nbasis * channels + 40),
            bytes_accessed=2 * window * channels,
            transcendentals=3 * shard * count * BLOCK_ATOMS,
        ),
        name="pair",
    )(neighbours, own_pos, *arrays, weight)


def update_kernel(*refs):
    features_ref, pair_ref, gain_ref, w_in_ref, w_out_ref = refs[:5]
    parts, out_ref = refs[5:-1], refs[-1]
    long_t = parts[0][...].astype(F32)
    for part in parts[1:]:
        long_t = long_t + part[...].astype(F32)
    total = features_ref[...].astype(F32) + pair_ref[...] + long_t.T
    mean = jnp.mean(total * total, axis=-1, keepdims=True)
    normed = (total * lax.rsqrt(mean + 1e-06) * gain_ref[...]).astype(BF16)
    pre = jnp.dot(normed, w_in_ref[...], preferred_element_type=F32)
    hidden = (pre / (1.0 + jnp.exp(-pre))).astype(BF16)
    out_ref[...] = (
        total + jnp.dot(hidden, w_out_ref[...], preferred_element_type=F32)
    ).astype(BF16)


def update(features, pair_msg, gain, w_in, w_out, parts):
    return pl.pallas_call(
        update_kernel,
        in_specs=[VMEM] * (5 + len(parts)),
        out_specs=VMEM,
        out_shape=jax.ShapeDtypeStruct(features.shape, BF16),
        compiler_params=params(),
        name="update",
    )(features, pair_msg, gain[None, :], w_in, w_out, *parts)


def swap(value, axis, bits):
    return lax.ppermute(value, axis, [(i, i ^ bits) for i in range(lax.axis_size(axis))])


def per_device(
    positions,
    features,
    atom_mask,
    neighbours,
    lattice,
    pair_weight,
    kfilter,
    norm_gain,
    w_in,
    w_out,
):
    shard, _ = features.shape
    n_atoms = lax.axis_size("atoms")
    n_kvec = lax.axis_size("kvec")
    far = n_atoms // 4
    count = lattice.shape[1] // (2 * far)
    width = 256 if count % 256 == 0 else count

    message = pack(features, atom_mask, positions)
    scale = float(n_atoms * n_kvec * shard * KW) ** (-0.5)
    waves, kfilt = setup(lattice, kfilter, far, width, scale)
    distant = [swap(message, "atoms", 4 * z) for z in range(1, far)]
    bundle = collect([message, *distant], [(z, None) for z in range(far)], after=(waves,))
    bundle_x = swap(bundle, "atoms", 1)
    arrived = [None] * n_kvec
    for k in range(n_kvec - 1, 0, -1):
        arrived[k] = swap(bundle, "kvec", k)
    arrived = arrived[1:]

    table_0, total = wave(waves, [bundle, bundle_x], None)
    every = [(k, z) for k in range(n_kvec - 1) for z in range(far)]
    gathered = collect(arrived, every, after=(total,))
    gathered_x = swap(gathered, "atoms", 1)
    table_1, total = wave(waves, [gathered], total)
    halo_pairs = [(a, (a + 2) % n_atoms if a % 2 == 0 else (a - 2) % n_atoms) for a in range(n_atoms)]
    near = [(0, 0)] + [(1, k * far) for k in range(n_kvec - 1)]
    halo = lax.ppermute(collect([bundle_x, gathered_x], near), "atoms", halo_pairs)
    table_2, total, low = wave(waves, [gathered_x], total, low=True)
    other = swap(low, "atoms", 2)

    picks = near + [(2 + array, index) for array, index in near]
    picks += [(4, k) for k in range(n_kvec)]
    pair_msg = pair_message(
        neighbours,
        positions,
        [bundle, gathered, bundle_x, gathered_x, halo],
        picks,
        pair_weight,
    )

    rest = far * (n_kvec - 1)
    filt, away = inverse_away(
        total, other, kfilt, pair_msg, [table_0, table_2], [(far, far), (0, rest)], shard
    )
    crossed = swap(away, "atoms", 1)
    here = inverse_here(filt, [table_0, table_1], [(0, far), (0, rest)], shard)
    own, *sends = join(here, crossed, n_kvec)
    came = [swap(sends[k - 1], "kvec", k).astype(F32) for k in range(n_kvec - 1, 0, -1)]
    for item in came:
        own = own + item
    parts = [own[:, :shard]]
    for z in range(1, far):
        parts.append(swap(own[:, z * shard : (z + 1) * shard].astype(BF16), "atoms", 4 * z))
    return update(features, pair_msg, norm_gain, w_in, w_out, parts)


def solution(mesh):
    return jax.shard_map(
        per_device,
        mesh=mesh,
        in_specs=(
            P(None, ("atoms", "kvec")),
            P(("atoms", "kvec"), None),
            P(("atoms", "kvec")),
            P(("atoms", "kvec"), None),
            P(None, "kvec"),
            P(),
            P(),
            P(),
            P(),
            P(),
        ),
        out_specs=P(("atoms", "kvec"), None),
        check_vma=False,
    )
```

```python
import functools
import math

import jax
import jax.numpy as jnp
from jax import lax
from jax.experimental import pallas as pl
from jax.experimental.pallas import tpu as pltpu
from jax.sharding import PartitionSpec as P

KW = 12288
BLOCK_ATOMS = 128
F32 = jnp.float32
BF16 = jnp.bfloat16

SIN_COEF = (4.442879586561992, -7.307818050390618, 3.5977887417720016, -0.7912382192058507)
ROUND = 12582912.0
SLACK = 1e-5
TAIL = 16


def params(mib=16):
    return pltpu.CompilerParams(vmem_limit_bytes=mib << 20)


SMEM = pl.BlockSpec(memory_space=pltpu.SMEM)
VMEM = pl.BlockSpec(memory_space=pltpu.VMEM)
ANY = pl.BlockSpec(memory_space=pl.ANY)


def horner(u, coef):
    acc = coef[-1] * u + coef[-2]
    for c in reversed(coef[:-2]):
        acc = acc * u + c
    return acc


def pack_kernel(*refs):
    features_hbm, mask_hbm, pos_hbm, lattice_hbm, kfilter_hbm = refs[:5]
    out_ref, lattice_ref, kfilter_ref, features_ref, mask_ref, pos_ref, scr, sems = refs[5:]
    copies = [
        pltpu.make_async_copy(source, target, sems.at[i])
        for i, (source, target) in enumerate(
            (
                (features_hbm, features_ref),
                (mask_hbm, mask_ref),
                (pos_hbm, pos_ref),
                (lattice_hbm, lattice_ref),
                (kfilter_hbm, kfilter_ref),
            )
        )
    ]
    for copy in copies:
        copy.start()
    for copy in copies:
        copy.wait()
    channels = features_ref.shape[1]
    mask = mask_ref[...].astype(F32)
    out_ref[0:channels, :] = (features_ref[...].astype(F32).T * mask).astype(BF16)
    value = pos_ref[...] * 0.125
    high = value.astype(BF16).astype(F32)
    rest = value - high
    mid = rest.astype(BF16).astype(F32)
    scr[...] = jnp.zeros_like(scr)
    scr[0:3, :] = high
    scr[3:6, :] = mid
    scr[6:9, :] = rest - mid
    out_ref[channels : channels + TAIL, :] = scr[...].astype(BF16)


def pack(features, mask, positions, lattice, kfilter):
    shard, channels = features.shape
    arrays = (features, mask[None, :], positions, lattice, kfilter)
    return pl.pallas_call(
        pack_kernel,
        in_specs=[pl.BlockSpec(memory_space=pltpu.HBM)] * 5,
        out_specs=[VMEM] * 3,
        out_shape=[
            jax.ShapeDtypeStruct((channels + TAIL, shard), BF16),
            jax.ShapeDtypeStruct(lattice.shape, lattice.dtype),
            jax.ShapeDtypeStruct(kfilter.shape, kfilter.dtype),
        ],
        scratch_shapes=[
            pltpu.VMEM((shard, channels), BF16),
            pltpu.VMEM((1, shard), jnp.int32),
            pltpu.VMEM((3, shard), F32),
            pltpu.VMEM((TAIL, shard), F32),
            pltpu.SemaphoreType.DMA((5,)),
        ],
        compiler_params=params(),
        name="pack",
    )(*(pltpu.with_memory_space_constraint(x, pltpu.HBM) for x in arrays))


def setup_kernel(far, nbasis, scale, lattice_ref, kfilter_ref, wave_ref, kfilt_ref, scr):
    blocks, width, _ = wave_ref.shape
    a_index = lax.axis_index("atoms")
    part = a_index % 2 + 2 * (a_index // 4)
    count = blocks * width
    kfilter = kfilter_ref[...].T
    for j in range(blocks):
        lattice = jnp.zeros((3, width), F32)
        for p in range(2 * far):
            at = p * count + j * width
            mine = (part == p).astype(F32)
            lattice += lattice_ref[:, at : at + width].astype(F32) * mine
        scr[...] = jnp.zeros_like(scr)
        for copy in range(3):
            scr[3 * copy : 3 * copy + 3, :] = lattice
        wave_ref[j] = scr[...].T.astype(BF16)
        wave = lattice * (2.0 * math.pi / 8.0)
        kmag = jnp.sqrt(
            wave[0:1] * wave[0:1] + wave[1:2] * wave[1:2] + wave[2:3] * wave[2:3]
        )
        total = jnp.zeros(kfilt_ref.shape[1:], F32)
        for p in range(nbasis):
            basis = jnp.exp(-0.5 * ((kmag - (p + 0.5) * (21.0 / nbasis)) / (21.0 / nbasis)) ** 2)
            total += kfilter[:, p : p + 1] * basis
        kfilt_ref[j] = total * scale


def setup(lattice, kfilter, far, width, scale):
    nbasis, channels = kfilter.shape
    blocks = lattice.shape[1] // (2 * far * width)
    return pl.pallas_call(
        functools.partial(setup_kernel, far, nbasis, scale),
        in_specs=[VMEM] * 2,
        out_specs=[VMEM] * 2,
        out_shape=[
            jax.ShapeDtypeStruct((blocks, width, TAIL), BF16),
            jax.ShapeDtypeStruct((blocks, channels, width), F32),
        ],
        scratch_shapes=[pltpu.VMEM((TAIL, width), F32)],
        compiler_params=params(),
        name="setup",
    )(lattice, kfilter)


def wave_kernel(counts, start, waits, low, *refs):
    refs = list(refs)
    take = lambda n: [refs.pop(0) for _ in range(n)]
    (lattice_ref,) = take(1)
    messages = take(len(counts))
    before_ref = None if start else take(1)[0]
    take(waits)
    table_ref, total_ref = take(2)
    low_ref = take(1)[0] if low else None
    feat_scr, pos_scr = take(2)
    blocks, width, _ = lattice_ref.shape
    phases, buffers = take(blocks), take(blocks)
    pairs, channels, both = feat_scr.shape
    shard = both // 2
    place = 0
    for ref, count in zip(messages, counts):
        for p in range(count):
            lanes = slice(place % 2 * shard, (place % 2 + 1) * shard)
            item = ref if len(ref.shape) == 2 else ref.at[p]
            feat_scr[place // 2, :, lanes] = item[0:channels, :]
            pos_scr[place // 2, :, lanes] = item[channels:, :]
            place += 1
    if start:
        total_ref[...] = jnp.zeros_like(total_ref)
    else:
        total_ref[...] = before_ref[...]
    buffers[-1][...] = jnp.zeros_like(buffers[-1])

    def phase(pair, block):
        phases[block][...] = jnp.dot(
            lattice_ref[block], pos_scr[pair], preferred_element_type=F32
        )

    def table(pair, block):
        rows = 16
        for side in range(2):
            part = slice(side * shard, (side + 1) * shard)
            lanes = pl.ds(pl.multiple_of(pair * both + side * shard, shard), shard)
            for at in range(0, width, rows):
                turns = phases[block][at : at + rows, part]
                r = turns - ((turns + ROUND) - ROUND)
                s = horner(r * r, SIN_COEF) * r
                square = s * s
                w = (2.0 + SLACK) - square
                cosine = (1.0 - square).astype(BF16)
                sine = (s * (w * lax.rsqrt(w))).astype(BF16)
                buffers[block][0, at : at + rows, part] = cosine
                buffers[block][1, at : at + rows, part] = sine
                table_ref[block, at : at + rows, lanes] = cosine
                table_ref[blocks + block, at : at + rows, lanes] = sine

    def product(pair, block):
        for half in range(2):
            total_ref[half * blocks + block] += lax.dot_general(
                feat_scr[pair],
                buffers[block][half],
                (((1,), (1,)), ((), ())),
                preferred_element_type=F32,
            )

    def body(pair, carry):
        before = jnp.maximum(pair - 1, 0)
        later = jnp.minimum(pair + 1, pairs - 1)
        for block in range(blocks):
            if block + 1 < blocks:
                phase(pair, block + 1)
            if blocks == 1:
                product(before, 0)
            table(pair, block)
            if block == 0:
                phase(later, 0)
            if blocks > 1:
                product(pair if block else before, (block - 1) % blocks)
        return carry

    phase(0, 0)
    lax.fori_loop(0, pairs, body, 0)
    product(pairs - 1, blocks - 1)
    if low:
        low_ref[...] = total_ref[...].astype(BF16)


def wave(lattice, messages, before, after=(), low=False):
    blocks, width, _ = lattice.shape
    counts = tuple(x.shape[0] if x.ndim == 3 else 1 for x in messages)
    pieces = sum(counts)
    rows, shard = messages[0].shape[-2:]
    channels = rows - TAIL
    args = [lattice, *messages] + ([] if before is None else [before])
    factor = (2 * blocks, channels, width)
    shapes = [
        jax.ShapeDtypeStruct((2 * blocks, width, pieces * shard), BF16),
        jax.ShapeDtypeStruct(factor, F32),
    ]
    if low:
        shapes.append(jax.ShapeDtypeStruct(factor, BF16))
    pairs = blocks * width * pieces * shard
    return pl.pallas_call(
        functools.partial(wave_kernel, counts, before is None, len(after), low),
        in_specs=[VMEM] * len(args) + [ANY] * len(after),
        out_specs=[VMEM] * len(shapes),
        out_shape=shapes,
        scratch_shapes=[
            pltpu.VMEM((pieces // 2, channels, 2 * shard), BF16),
            pltpu.VMEM((pieces // 2, TAIL, 2 * shard), BF16),
            *[pltpu.VMEM((width, 2 * shard), F32)] * blocks,
            *[pltpu.VMEM((2, width, 2 * shard), BF16)] * blocks,
        ],
        compiler_params=params(),
        cost_estimate=pl.CostEstimate(
            flops=4 * pairs * channels, bytes_accessed=4 * pairs, transcendentals=pairs
        ),
        name="wave",
    )(*args, *after)


def collect_kernel(picks, *refs):
    for p, (array, index) in enumerate(picks):
        ref = refs[array]
        refs[-1][p] = ref[...] if index is None else ref[index]


def collect(arrays, picks, after=()):
    return pl.pallas_call(
        functools.partial(collect_kernel, picks),
        in_specs=[VMEM] * len(arrays) + [ANY] * len(after),
        out_specs=VMEM,
        out_shape=jax.ShapeDtypeStruct((len(picks), *arrays[0].shape[-2:]), BF16),
        compiler_params=params(),
        name="collect",
    )(*arrays, *after)


def transform(filt_ref, parts, out_ref, shard):
    blocks = filt_ref.shape[0]
    at = 0
    for table_ref, first, pieces in parts:
        for p in range(first, first + pieces):
            acc = jnp.dot(
                filt_ref[0], table_ref[0, :, p * shard : (p + 1) * shard], preferred_element_type=F32
            )
            for j in range(1, blocks):
                acc += jnp.dot(
                    filt_ref[j],
                    table_ref[j, :, p * shard : (p + 1) * shard],
                    preferred_element_type=F32,
                )
            out_ref[:, at : at + shard] = acc.astype(out_ref.dtype)
            at += shard


def away_kernel(runs, shard, own_ref, other_ref, kfilt_ref, _, *refs):
    table_refs, (filt_ref, out_ref) = refs[:-2], refs[-2:]
    count = kfilt_ref.shape[0]
    for j in range(2 * count):
        total = own_ref[j] + other_ref[j].astype(F32)
        filt_ref[j] = (total * kfilt_ref[j % count]).astype(BF16)
    transform(filt_ref, [(table_refs[t], p, 1) for t, p in runs], out_ref, shard)


def here_kernel(runs, shard, filt_ref, *refs):
    transform(filt_ref, [(refs[t], p, 1) for t, p in runs], refs[-1], shard)


def inverse_cost(filt, atoms):
    return pl.CostEstimate(
        flops=2 * math.prod(filt.shape) * atoms,
        bytes_accessed=2 * math.prod(filt.shape[::2]) * atoms,
        transcendentals=0,
    )


def used(tables, runs):
    names = sorted({t for t, _ in runs})
    return [tables[t] for t in names], tuple((names.index(t), p) for t, p in runs)


def inverse_first(own, other, kfilt, after, tables, runs, shard):
    channels = own.shape[1]
    tables, runs = used(tables, runs)
    atoms = shard * len(runs)
    return pl.pallas_call(
        functools.partial(away_kernel, runs, shard),
        in_specs=[VMEM] * 3 + [ANY] + [VMEM] * len(tables),
        out_specs=[VMEM] * 2,
        out_shape=[
            jax.ShapeDtypeStruct(own.shape, BF16),
            jax.ShapeDtypeStruct((channels, atoms), BF16),
        ],
        compiler_params=params(),
        cost_estimate=inverse_cost(own, atoms),
        name="first",
    )(own, other, kfilt, after, *tables)


def inverse(filt, tables, runs, shard, dtype):
    channels = filt.shape[1]
    tables, runs = used(tables, runs)
    atoms = shard * len(runs)
    return pl.pallas_call(
        functools.partial(here_kernel, runs, shard),
        in_specs=[VMEM] * (1 + len(tables)),
        out_specs=VMEM,
        out_shape=jax.ShapeDtypeStruct((channels, atoms), dtype),
        compiler_params=params(),
        cost_estimate=inverse_cost(filt, atoms),
        name="inverse",
    )(filt, *tables)


def join_kernel(here_ref, arrived_ref, own_ref, *send_refs):
    width = own_ref.shape[1]
    for p in range(len(send_refs) + 1):
        lanes = slice(p * width, (p + 1) * width)
        total = here_ref[:, lanes] + arrived_ref[:, lanes].astype(F32)
        if p:
            send_refs[p - 1][...] = total.astype(BF16)
        else:
            own_ref[...] = total


def join(here, arrived, pieces):
    channels, atoms = here.shape
    shape = (channels, atoms // pieces)
    return pl.pallas_call(
        join_kernel,
        in_specs=[VMEM] * 2,
        out_specs=[VMEM] * pieces,
        out_shape=[jax.ShapeDtypeStruct(shape, F32)]
        + [jax.ShapeDtypeStruct(shape, BF16)] * (pieces - 1),
        compiler_params=params(),
        name="join",
    )(here, arrived)


def pair_kernel(nbasis, pieces, output_scale, picks, arrays, neighbours_ref, own_pos_ref, *refs):
    message_refs, refs = refs[:arrays], refs[arrays:]
    weight_ref, out_ref, feat_scr, pos_scr, own_scr, basis_scr, acc_scr = refs
    block = BLOCK_ATOMS
    width = 12.0 / nbasis
    own_blocks, neighbours = neighbours_ref.shape
    shard = own_blocks * block
    channels = out_ref.shape[1]

    views = [
        message_refs[array] if index is None else message_refs[array].at[index]
        for array, index in picks
    ]
    for place, ref in enumerate(views):
        lanes = slice(place * shard, (place + 1) * shard)
        feat_scr[:, lanes] = ref[0:channels, :]
        parts = ref[channels:, :].astype(F32)
        pos_scr[0:3, lanes] = (parts[0:3] + parts[3:6] + parts[6:9]) * 8.0

    a_index = lax.axis_index("atoms")
    k_index = lax.axis_index("kvec")
    n_atoms = lax.axis_size("atoms")
    group_blk = own_blocks * pieces
    first = (a_index * pieces + k_index) * own_blocks
    toward = jnp.where(a_index % 2 == 0, 1, n_atoms - 1)

    def place_of(ident):
        group, within = ident // group_blk, ident % group_blk
        ahead = (group - a_index + n_atoms) % n_atoms
        which = jnp.where(ahead == 0, 0, jnp.where(ahead == toward, 1, 2))
        piece = (within // own_blocks) ^ k_index
        return (which * pieces + piece) * own_blocks + within % own_blocks

    rows = 64
    diagonal = lax.broadcasted_iota(jnp.int32, (rows, block), 0) - lax.broadcasted_iota(
        jnp.int32, (rows, block), 1
    )
    for b in range(own_blocks):
        for d in range(3):
            row = own_pos_ref[d : d + 1, b * block : (b + 1) * block]
            own_scr[d] = jnp.broadcast_to(row, (block, block)).T
        acc_scr[...] = jnp.zeros_like(acc_scr)

        def pair(jp, carry):
            near_feat = []
            for h in range(2):
                ident = neighbours_ref[b, 2 * jp + h]
                lanes = pl.ds(pl.multiple_of(place_of(ident) * block, block), block)
                same = ident == first + b
                near_feat.append(feat_scr[:, lanes])
                near = [pos_scr[d : d + 1, lanes] for d in range(3)]
                for part in range(block // rows):
                    at = part * rows
                    dist2 = (own_scr[0, at : at + rows, :] - near[0]) ** 2
                    dist2 += (own_scr[1, at : at + rows, :] - near[1]) ** 2
                    dist2 += (own_scr[2, at : at + rows, :] - near[2]) ** 2
                    radius = dist2 * lax.rsqrt(jnp.maximum(dist2, 1e-30))
                    env = output_scale / (1.0 + dist2 * (1.0 / 16.0))
                    env = jnp.where((diagonal + at == 0) & same, 0.0, env)
                    v = radius * (1.0 / width) - 0.5
                    value = jnp.exp(-0.5 * v * v) * env
                    ratio = jnp.exp(v)
                    for k in range(nbasis):
                        if k:
                            value = value * ratio
                        basis_scr[
                            k * block + at : k * block + at + rows, h * block : (h + 1) * block
                        ] = value.astype(BF16)
            acc_scr[...] += lax.dot_general(
                basis_scr[...],
                jnp.concatenate(near_feat, axis=1),
                (((1,), (1,)), ((), ())),
                preferred_element_type=F32,
            )
            return carry

        lax.fori_loop(0, neighbours // 2, pair, 0)
        total = jnp.zeros((block, channels), F32)
        for k in range(nbasis):
            gathered = (acc_scr[k * block : (k + 1) * block, :] * math.exp(-0.5 * k * k)).astype(BF16)
            total += jnp.dot(
                gathered,
                weight_ref[k * channels : (k + 1) * channels, :],
                preferred_element_type=F32,
            )
        out_ref[b * block : (b + 1) * block, :] = total


def pair_message(neighbours, own_pos, arrays, picks, weight):
    channels = weight.shape[1]
    nbasis = weight.shape[0] // channels
    pieces = len(picks) // 3
    shard = own_pos.shape[1]
    count = neighbours.shape[1]
    scale = float(count * BLOCK_ATOMS) ** (-0.5)
    window = 3 * pieces * shard
    return pl.pallas_call(
        functools.partial(pair_kernel, nbasis, pieces, scale, picks, len(arrays)),
        in_specs=[SMEM] + [VMEM] * (2 + len(arrays)),
        out_specs=VMEM,
        out_shape=jax.ShapeDtypeStruct((shard, channels), F32),
        scratch_shapes=[
            pltpu.VMEM((channels, window), BF16),
            pltpu.VMEM((8, window), F32),
            pltpu.VMEM((3, BLOCK_ATOMS, BLOCK_ATOMS), F32),
            pltpu.VMEM((nbasis * BLOCK_ATOMS, 2 * BLOCK_ATOMS), BF16),
            pltpu.VMEM((nbasis * BLOCK_ATOMS, channels), F32),
        ],
        compiler_params=params(),
        cost_estimate=pl.CostEstimate(
            flops=2 * shard * count * BLOCK_ATOMS * (nbasis * channels + 40),
            bytes_accessed=2 * window * channels,
            transcendentals=3 * shard * count * BLOCK_ATOMS,
        ),
        name="pair",
    )(neighbours, own_pos, *arrays, weight)


def update_kernel(*refs):
    features_ref, pair_ref, gain_ref, w_in_ref, w_out_ref = refs[:5]
    parts, out_ref = refs[5:-1], refs[-1]
    long_t = parts[0][...].astype(F32)
    for part in parts[1:]:
        long_t = long_t + part[...].astype(F32)
    total = features_ref[...].astype(F32) + pair_ref[...] + long_t.T
    mean = jnp.mean(total * total, axis=-1, keepdims=True)
    normed = (total * lax.rsqrt(mean + 1e-06) * gain_ref[...]).astype(BF16)
    pre = jnp.dot(normed, w_in_ref[...], preferred_element_type=F32)
    hidden = (pre / (1.0 + jnp.exp(-pre))).astype(BF16)
    out_ref[...] = (
        total + jnp.dot(hidden, w_out_ref[...], preferred_element_type=F32)
    ).astype(BF16)


def update(features, pair_msg, gain, w_in, w_out, parts):
    return pl.pallas_call(
        update_kernel,
        in_specs=[VMEM] * (5 + len(parts)),
        out_specs=VMEM,
        out_shape=jax.ShapeDtypeStruct(features.shape, BF16),
        compiler_params=params(),
        name="update",
    )(features, pair_msg, gain[None, :], w_in, w_out, *parts)


def swap(value, axis, bits):
    return lax.ppermute(value, axis, [(i, i ^ bits) for i in range(lax.axis_size(axis))])


def per_device(
    positions,
    features,
    atom_mask,
    neighbours,
    lattice,
    pair_weight,
    kfilter,
    norm_gain,
    w_in,
    w_out,
):
    shard, _ = features.shape
    n_atoms = lax.axis_size("atoms")
    n_kvec = lax.axis_size("kvec")
    far = n_atoms // 4
    count = lattice.shape[1] // (2 * far)
    width = 256 if count % 256 == 0 else count

    message, lattice, kfilter = pack(features, atom_mask, positions, lattice, kfilter)
    scale = float(n_atoms * n_kvec * shard * KW) ** (-0.5)
    waves, kfilt = setup(lattice, kfilter, far, width, scale)
    others = range(n_kvec - 1, 0, -1)
    zs = range(1, far)
    message_x = swap(message, "atoms", 1)
    near = {k: swap(message, "kvec", k) for k in others}
    distant = [swap(message, "atoms", 4 * z) for z in zs]
    distant = collect(distant, [(z, None) for z in range(far - 1)])
    distant_x = swap(distant, "atoms", 1)
    relayed = {k: swap(distant, "kvec", k) for k in others}

    where = {}
    table_0, total = wave(waves, [message, message_x], None)
    where[0, 0, 0], where[1, 0, 0] = (0, 0), (0, 1)
    near_own = collect([near[k] for k in others], [(i, None) for i in range(n_kvec - 1)], after=(total,))
    near_x = swap(near_own, "atoms", 1)
    halo_pairs = [(a, (a + 1) % n_atoms if a % 2 else (a - 1) % n_atoms) for a in range(n_atoms)]
    own_group = [message, near_own]
    picks = [(0, None)] + [(1, n_kvec - 1 - k) for k in range(1, n_kvec)]
    halo = lax.ppermute(collect(own_group, picks), "atoms", halo_pairs)
    table_1, total = wave(waves, [near_own, near_x], total)
    for i, k in enumerate(others):
        where[0, 0, k], where[1, 0, k] = (1, i), (1, n_kvec - 1 + i)
    every = [(i, z) for i in range(n_kvec - 1) for z in range(far - 1)]
    far_own = collect([relayed[k] for k in others], every, after=(total,))
    far_x = swap(far_own, "atoms", 1)
    table_2, total = wave(waves, [distant, far_own], total)
    table_3, total, low = wave(waves, [distant_x, far_x], total, low=True)
    for core, table in ((0, 2), (1, 3)):
        for z in zs:
            where[core, z, 0] = (table, z - 1)
            for i, k in enumerate(others):
                where[core, z, k] = (table, (1 + i) * (far - 1) + z - 1)
    tables = [table_0, table_1, table_2, table_3]
    other = swap(low, "atoms", 2)

    arrays = [message, message_x, near_own, near_x, halo]
    picks = [(0, None)] + [(2, n_kvec - 1 - k) for k in range(1, n_kvec)]
    picks += [(1, None)] + [(3, n_kvec - 1 - k) for k in range(1, n_kvec)]
    picks += [(4, k) for k in range(n_kvec)]
    pair_msg = pair_message(neighbours, positions, arrays, tuple(picks), pair_weight)

    def runs(core, distances):
        return tuple(where[core, z, k] for k in range(n_kvec) for z in distances)

    filt, away_far = inverse_first(total, other, kfilt, pair_msg, tables, runs(1, zs), shard)
    crossed_far = swap(away_far, "atoms", 1)
    away_near = inverse(filt, tables, runs(1, (0,)), shard, BF16)
    crossed_near = swap(away_near, "atoms", 1)
    here_far = inverse(filt, tables, runs(0, zs), shard, F32)
    sum_far, *sends = join(here_far, crossed_far, n_kvec)
    for k in others:
        sum_far = sum_far + swap(sends[k - 1], "kvec", k).astype(F32)
    sum_far = sum_far.astype(BF16)
    here_near = inverse(filt, tables, runs(0, (0,)), shard, F32)
    own_near, *sends = join(here_near, crossed_near, n_kvec)
    parts = [own_near] + [swap(sends[k - 1], "kvec", k) for k in others]
    for z in zs:
        parts.append(swap(sum_far[:, (z - 1) * shard : z * shard], "atoms", 4 * z))
    return update(features, pair_msg, norm_gain, w_in, w_out, parts)


def solution(mesh):
    return jax.shard_map(
        per_device,
        mesh=mesh,
        in_specs=(
            P(None, ("atoms", "kvec")),
            P(("atoms", "kvec"), None),
            P(("atoms", "kvec")),
            P(("atoms", "kvec"), None),
            P(None, "kvec"),
            P(),
            P(),
            P(),
            P(),
            P(),
        ),
        out_specs=P(("atoms", "kvec"), None),
        check_vma=False,
    )
```

```python
import functools
import math

import jax
import jax.numpy as jnp
from jax import lax
from jax.experimental import pallas as pl
from jax.experimental.pallas import tpu as pltpu
from jax.sharding import PartitionSpec as P

KW = 12288
BLOCK_ATOMS = 128
F32 = jnp.float32
BF16 = jnp.bfloat16

SIN_COEF = (4.442879586561992, -7.307818050390618, 3.5977887417720016, -0.7912382192058507)
ROUND = 12582912.0
SLACK = 1e-5
TAIL = 16


def params(mib=16):
    return pltpu.CompilerParams(vmem_limit_bytes=mib << 20)


SMEM = pl.BlockSpec(memory_space=pltpu.SMEM)
VMEM = pl.BlockSpec(memory_space=pltpu.VMEM)
ANY = pl.BlockSpec(memory_space=pl.ANY)


def horner(u, coef):
    acc = coef[-1] * u + coef[-2]
    for c in reversed(coef[:-2]):
        acc = acc * u + c
    return acc


def pack_kernel(*refs):
    features_hbm, mask_hbm, pos_hbm, lattice_hbm, kfilter_hbm = refs[:5]
    out_ref, lattice_ref, kfilter_ref, features_ref, mask_ref, pos_ref, scr, sems = refs[5:]
    copies = [
        pltpu.make_async_copy(source, target, sems.at[i])
        for i, (source, target) in enumerate(
            (
                (features_hbm, features_ref),
                (mask_hbm, mask_ref),
                (pos_hbm, pos_ref),
                (lattice_hbm, lattice_ref),
                (kfilter_hbm, kfilter_ref),
            )
        )
    ]
    for copy in copies:
        copy.start()
    for copy in copies:
        copy.wait()
    channels = features_ref.shape[1]
    mask = mask_ref[...].astype(F32)
    out_ref[0:channels, :] = (features_ref[...].astype(F32).T * mask).astype(BF16)
    value = pos_ref[...] * 0.125
    high = value.astype(BF16).astype(F32)
    rest = value - high
    mid = rest.astype(BF16).astype(F32)
    scr[...] = jnp.zeros_like(scr)
    scr[0:3, :] = high
    scr[3:6, :] = mid
    scr[6:9, :] = rest - mid
    out_ref[channels : channels + TAIL, :] = scr[...].astype(BF16)


def pack(features, mask, positions, lattice, kfilter):
    shard, channels = features.shape
    arrays = (features, mask[None, :], positions, lattice, kfilter)
    return pl.pallas_call(
        pack_kernel,
        in_specs=[pl.BlockSpec(memory_space=pltpu.HBM)] * 5,
        out_specs=[VMEM] * 3,
        out_shape=[
            jax.ShapeDtypeStruct((channels + TAIL, shard), BF16),
            jax.ShapeDtypeStruct(lattice.shape, lattice.dtype),
            jax.ShapeDtypeStruct(kfilter.shape, kfilter.dtype),
        ],
        scratch_shapes=[
            pltpu.VMEM((shard, channels), BF16),
            pltpu.VMEM((1, shard), jnp.int32),
            pltpu.VMEM((3, shard), F32),
            pltpu.VMEM((TAIL, shard), F32),
            pltpu.SemaphoreType.DMA((5,)),
        ],
        compiler_params=params(),
        name="pack",
    )(*(pltpu.with_memory_space_constraint(x, pltpu.HBM) for x in arrays))


def setup_kernel(far, nbasis, scale, lattice_ref, kfilter_ref, wave_ref, kfilt_ref, scr):
    blocks, width, _ = wave_ref.shape
    a_index = lax.axis_index("atoms")
    part = a_index % 2 + 2 * (a_index // 4)
    count = blocks * width
    kfilter = kfilter_ref[...].T
    for j in range(blocks):
        lattice = jnp.zeros((3, width), F32)
        for p in range(2 * far):
            at = p * count + j * width
            mine = (part == p).astype(F32)
            lattice += lattice_ref[:, at : at + width].astype(F32) * mine
        scr[...] = jnp.zeros_like(scr)
        for copy in range(3):
            scr[3 * copy : 3 * copy + 3, :] = lattice
        wave_ref[j] = scr[...].T.astype(BF16)
        wave = lattice * (2.0 * math.pi / 8.0)
        kmag = jnp.sqrt(
            wave[0:1] * wave[0:1] + wave[1:2] * wave[1:2] + wave[2:3] * wave[2:3]
        )
        total = jnp.zeros(kfilt_ref.shape[1:], F32)
        for p in range(nbasis):
            basis = jnp.exp(-0.5 * ((kmag - (p + 0.5) * (21.0 / nbasis)) / (21.0 / nbasis)) ** 2)
            total += kfilter[:, p : p + 1] * basis
        kfilt_ref[j] = total * scale


def setup(lattice, kfilter, far, width, scale):
    nbasis, channels = kfilter.shape
    blocks = lattice.shape[1] // (2 * far * width)
    return pl.pallas_call(
        functools.partial(setup_kernel, far, nbasis, scale),
        in_specs=[VMEM] * 2,
        out_specs=[VMEM] * 2,
        out_shape=[
            jax.ShapeDtypeStruct((blocks, width, TAIL), BF16),
            jax.ShapeDtypeStruct((blocks, channels, width), F32),
        ],
        scratch_shapes=[pltpu.VMEM((TAIL, width), F32)],
        compiler_params=params(),
        name="setup",
    )(lattice, kfilter)


def wave_kernel(picks, arrays, first, start, waits, low, *refs):
    refs = list(refs)
    take = lambda n: [refs.pop(0) for _ in range(n)]
    (lattice_ref,) = take(1)
    messages = take(arrays)
    before_ref = None if start else take(1)[0]
    take(waits)
    table_ref, total_ref = take(2)
    low_ref = take(1)[0] if low else None
    feat_scr, pos_scr, phase_scr = refs
    blocks, width = table_ref.shape[0] // 2, table_ref.shape[1]
    every = lattice_ref.shape[0]
    pairs, _, both = pos_scr.shape
    channels = feat_scr.shape[0]
    shard = both // 2
    for place, (array, index) in enumerate(picks):
        item = messages[array] if index is None else messages[array].at[index]
        feat_scr[:, place * shard : (place + 1) * shard] = item[0:channels, :]
        lanes = slice(place % 2 * shard, (place % 2 + 1) * shard)
        pos_scr[place // 2, :, lanes] = item[channels:, :]
    steps = pairs * blocks

    def phase(i):
        phase_scr[...] = jnp.dot(
            lattice_ref[first + i % blocks], pos_scr[i // blocks], preferred_element_type=F32
        )

    def table(i):
        pair, block = i // blocks, i % blocks
        lanes = pl.ds(pl.multiple_of(pair * both, both), both)
        rows = 16
        for at in range(0, width, rows):
            turns = phase_scr[at : at + rows, :]
            r = turns - ((turns + ROUND) - ROUND)
            s = horner(r * r, SIN_COEF) * r
            square = s * s
            w = (2.0 + SLACK) - square
            table_ref[block, at : at + rows, lanes] = (1.0 - square).astype(BF16)
            table_ref[blocks + block, at : at + rows, lanes] = (s * (w * lax.rsqrt(w))).astype(BF16)

    def body(i, carry):
        table(i)
        phase(jnp.minimum(i + 1, steps - 1))
        return carry

    phase(0)
    lax.fori_loop(0, steps, body, 0)
    for j in range(2 * blocks):
        part = lax.dot_general(
            feat_scr[...], table_ref[j], (((1,), (1,)), ((), ())), preferred_element_type=F32
        )
        if not start:
            part += before_ref[j // blocks * every + first + j % blocks]
        total_ref[j] = part
        if low:
            low_ref[j] = part.astype(BF16)


def wave(lattice, arrays, picks, before, subset=None, after=(), low=False):
    every, width, _ = lattice.shape
    first, blocks = subset or (0, every)
    pieces = len(picks)
    rows, shard = arrays[0].shape[-2:]
    channels = rows - TAIL
    args = [lattice, *arrays] + ([] if before is None else [before])
    factor = (2 * blocks, channels, width)
    shapes = [
        jax.ShapeDtypeStruct((2 * blocks, width, pieces * shard), BF16),
        jax.ShapeDtypeStruct(factor, F32),
    ]
    if low:
        shapes.append(jax.ShapeDtypeStruct(factor, BF16))
    pairs = blocks * width * pieces * shard
    return pl.pallas_call(
        functools.partial(
            wave_kernel, tuple(picks), len(arrays), first, before is None, len(after), low
        ),
        in_specs=[VMEM] * len(args) + [ANY] * len(after),
        out_specs=[VMEM] * len(shapes),
        out_shape=shapes,
        scratch_shapes=[
            pltpu.VMEM((channels, pieces * shard), BF16),
            pltpu.VMEM((pieces // 2, TAIL, 2 * shard), BF16),
            pltpu.VMEM((width, 2 * shard), F32),
        ],
        compiler_params=params(),
        cost_estimate=pl.CostEstimate(
            flops=4 * pairs * channels, bytes_accessed=4 * pairs, transcendentals=pairs
        ),
        name="wave",
    )(*args, *after)


def collect_kernel(picks, *refs):
    for p, (array, index) in enumerate(picks):
        ref = refs[array]
        refs[-1][p] = ref[...] if index is None else ref[index]


def collect(arrays, picks, after=()):
    return pl.pallas_call(
        functools.partial(collect_kernel, picks),
        in_specs=[VMEM] * len(arrays) + [ANY] * len(after),
        out_specs=VMEM,
        out_shape=jax.ShapeDtypeStruct((len(picks), *arrays[0].shape[-2:]), BF16),
        compiler_params=params(),
        name="collect",
    )(*arrays, *after)


def transform(filt_ref, table_refs, pieces, out_ref, shard):
    for at, places in enumerate(pieces):
        acc = None
        for j, (table, index, place) in enumerate(places):
            part = jnp.dot(
                filt_ref[j],
                table_refs[table][index, :, place * shard : (place + 1) * shard],
                preferred_element_type=F32,
            )
            acc = part if acc is None else acc + part
        out_ref[:, at * shard : (at + 1) * shard] = acc.astype(out_ref.dtype)


def first_kernel(pieces, shard, parts, blocks, *refs):
    own_refs, other_refs, refs = refs[:parts], refs[parts : 2 * parts], refs[2 * parts :]
    kfilt_ref, table_refs, (filt_ref, out_ref) = refs[0], refs[2:-2], refs[-2:]
    count = kfilt_ref.shape[0]
    for half in range(2):
        for j in range(count):
            part, index = j // blocks, half * blocks + j % blocks
            total = own_refs[part][index] + other_refs[part][index].astype(F32)
            filt_ref[half * count + j] = (total * kfilt_ref[j]).astype(BF16)
    transform(filt_ref, table_refs, pieces, out_ref, shard)


def inverse_kernel(pieces, shard, filt_ref, *refs):
    transform(filt_ref, refs[:-1], pieces, refs[-1], shard)


def inverse_cost(count, channels, width, atoms):
    return pl.CostEstimate(
        flops=2 * count * channels * width * atoms,
        bytes_accessed=2 * count * width * atoms,
        transcendentals=0,
    )


def used(tables, pieces):
    names = sorted({place[0] for places in pieces for place in places})
    moved = tuple(tuple((names.index(t), i, p) for t, i, p in places) for places in pieces)
    return [tables[t] for t in names], moved


def inverse_first(own, other, kfilt, after, tables, pieces, shard):
    count, channels, width = kfilt.shape
    tables, pieces = used(tables, pieces)
    atoms = shard * len(pieces)
    blocks = count // len(own)
    return pl.pallas_call(
        functools.partial(first_kernel, pieces, shard, len(own), blocks),
        in_specs=[VMEM] * (2 * len(own) + 1) + [ANY] + [VMEM] * len(tables),
        out_specs=[VMEM] * 2,
        out_shape=[
            jax.ShapeDtypeStruct((2 * count, channels, width), BF16),
            jax.ShapeDtypeStruct((channels, atoms), BF16),
        ],
        compiler_params=params(),
        cost_estimate=inverse_cost(2 * count, channels, width, atoms),
        name="first",
    )(*own, *other, kfilt, after, *tables)


def inverse(filt, tables, pieces, shard, dtype):
    count, channels, width = filt.shape
    tables, pieces = used(tables, pieces)
    atoms = shard * len(pieces)
    return pl.pallas_call(
        functools.partial(inverse_kernel, pieces, shard),
        in_specs=[VMEM] * (1 + len(tables)),
        out_specs=VMEM,
        out_shape=jax.ShapeDtypeStruct((channels, atoms), dtype),
        compiler_params=params(),
        cost_estimate=inverse_cost(count, channels, width, atoms),
        name="inverse",
    )(filt, *tables)


def join_kernel(here_ref, arrived_ref, own_ref, *send_refs):
    width = own_ref.shape[1]
    for p in range(len(send_refs) + 1):
        lanes = slice(p * width, (p + 1) * width)
        total = here_ref[:, lanes] + arrived_ref[:, lanes].astype(F32)
        if p:
            send_refs[p - 1][...] = total.astype(BF16)
        else:
            own_ref[...] = total


def join(here, arrived, pieces):
    channels, atoms = here.shape
    shape = (channels, atoms // pieces)
    return pl.pallas_call(
        join_kernel,
        in_specs=[VMEM] * 2,
        out_specs=[VMEM] * pieces,
        out_shape=[jax.ShapeDtypeStruct(shape, F32)]
        + [jax.ShapeDtypeStruct(shape, BF16)] * (pieces - 1),
        compiler_params=params(),
        name="join",
    )(here, arrived)


def pair_kernel(nbasis, pieces, output_scale, picks, arrays, neighbours_ref, own_pos_ref, *refs):
    message_refs, refs = refs[:arrays], refs[arrays:]
    weight_ref, _, out_ref, feat_scr, pos_scr, own_scr, basis_scr, near_scr = refs
    block = BLOCK_ATOMS
    width = 12.0 / nbasis
    own_blocks, neighbours = neighbours_ref.shape
    shard = own_blocks * block
    channels = out_ref.shape[0]

    views = [
        message_refs[array] if index is None else message_refs[array].at[index]
        for array, index in picks
    ]
    for place, ref in enumerate(views):
        lanes = slice(place * shard, (place + 1) * shard)
        feat_scr[:, lanes] = ref[0:channels, :]
        parts = ref[channels:, :].astype(F32)
        pos_scr[0:3, lanes] = (parts[0:3] + parts[3:6] + parts[6:9]) * 8.0

    a_index = lax.axis_index("atoms")
    k_index = lax.axis_index("kvec")
    n_atoms = lax.axis_size("atoms")
    group_blk = own_blocks * pieces
    first = (a_index * pieces + k_index) * own_blocks
    toward = jnp.where(a_index % 2 == 0, 1, n_atoms - 1)

    def place_of(ident):
        group, within = ident // group_blk, ident % group_blk
        ahead = (group - a_index + n_atoms) % n_atoms
        which = jnp.where(ahead == 0, 0, jnp.where(ahead == toward, 1, 2))
        piece = (within // own_blocks) ^ k_index
        return (which * pieces + piece) * own_blocks + within % own_blocks

    rows = 32
    diagonal = lax.broadcasted_iota(jnp.int32, (rows, block), 0) - lax.broadcasted_iota(
        jnp.int32, (rows, block), 1
    )
    for b in range(own_blocks):
        for d in range(3):
            row = own_pos_ref[d : d + 1, b * block : (b + 1) * block]
            own_scr[d] = jnp.broadcast_to(row, (block, block)).T

        def pair(n, carry):
            ident = neighbours_ref[b, n]
            lanes = pl.ds(pl.multiple_of(place_of(ident) * block, block), block)
            here = pl.ds(pl.multiple_of(n * block, block), block)
            near_scr[:, here] = feat_scr[:, lanes]
            same = ident == first + b
            near = [pos_scr[d : d + 1, lanes] for d in range(3)]
            for at in range(0, block, rows):
                dist2 = (own_scr[0, at : at + rows, :] - near[0]) ** 2
                dist2 += (own_scr[1, at : at + rows, :] - near[1]) ** 2
                dist2 += (own_scr[2, at : at + rows, :] - near[2]) ** 2
                radius = dist2 * lax.rsqrt(jnp.maximum(dist2, 1e-30))
                env = output_scale / (1.0 + dist2 * (1.0 / 16.0))
                env = jnp.where((diagonal + at == 0) & same, 0.0, env)
                v = radius * (1.0 / width) - 0.5
                value = jnp.exp(-0.5 * v * v) * env
                ratio = jnp.exp(v)
                for k in range(nbasis):
                    if k:
                        value = value * ratio
                    basis_scr[k * block + at : k * block + at + rows, here] = value.astype(BF16)
            return carry

        lax.fori_loop(0, neighbours, pair, 0)
        total = jnp.zeros((channels, block), F32)
        for k in range(nbasis):
            gathered = lax.dot_general(
                near_scr[...],
                basis_scr[k * block : (k + 1) * block, :],
                (((1,), (1,)), ((), ())),
                preferred_element_type=F32,
            )
            total += lax.dot_general(
                weight_ref[k * channels : (k + 1) * channels, :],
                (gathered * math.exp(-0.5 * k * k)).astype(BF16),
                (((0,), (0,)), ((), ())),
                preferred_element_type=F32,
            )
        out_ref[:, b * block : (b + 1) * block] = total


def pair_message(neighbours, own_pos, arrays, picks, weight, after):
    channels = weight.shape[1]
    nbasis = weight.shape[0] // channels
    pieces = len(picks) // 3
    shard = own_pos.shape[1]
    count = neighbours.shape[1]
    scale = float(count * BLOCK_ATOMS) ** (-0.5)
    window = 3 * pieces * shard
    return pl.pallas_call(
        functools.partial(pair_kernel, nbasis, pieces, scale, picks, len(arrays)),
        in_specs=[SMEM] + [VMEM] * (2 + len(arrays)) + [ANY],
        out_specs=VMEM,
        out_shape=jax.ShapeDtypeStruct((channels, shard), F32),
        scratch_shapes=[
            pltpu.VMEM((channels, window), BF16),
            pltpu.VMEM((8, window), F32),
            pltpu.VMEM((3, BLOCK_ATOMS, BLOCK_ATOMS), F32),
            pltpu.VMEM((nbasis * BLOCK_ATOMS, count * BLOCK_ATOMS), BF16),
            pltpu.VMEM((channels, count * BLOCK_ATOMS), BF16),
        ],
        compiler_params=params(),
        cost_estimate=pl.CostEstimate(
            flops=2 * shard * count * BLOCK_ATOMS * (nbasis * channels + 40),
            bytes_accessed=2 * window * channels,
            transcendentals=3 * shard * count * BLOCK_ATOMS,
        ),
        name="pair",
    )(neighbours, own_pos, *arrays, weight, after)


def update_kernel(*refs):
    features_ref, pair_ref, gain_ref, w_in_ref, w_out_ref = refs[:5]
    parts, out_ref = refs[5:-1], refs[-1]
    long_t = parts[0][...].astype(F32)
    for part in parts[1:]:
        long_t = long_t + part[...].astype(F32)
    total = features_ref[...].astype(F32) + (pair_ref[...] + long_t).T
    mean = jnp.mean(total * total, axis=-1, keepdims=True)
    normed = (total * lax.rsqrt(mean + 1e-06) * gain_ref[...]).astype(BF16)
    pre = jnp.dot(normed, w_in_ref[...], preferred_element_type=F32)
    hidden = (pre / (1.0 + jnp.exp(-pre))).astype(BF16)
    out_ref[...] = (
        total + jnp.dot(hidden, w_out_ref[...], preferred_element_type=F32)
    ).astype(BF16)


def update(features, pair_msg, gain, w_in, w_out, parts):
    return pl.pallas_call(
        update_kernel,
        in_specs=[VMEM] * (5 + len(parts)),
        out_specs=VMEM,
        out_shape=jax.ShapeDtypeStruct(features.shape, BF16),
        compiler_params=params(),
        name="update",
    )(features, pair_msg, gain[None, :], w_in, w_out, *parts)


def swap(value, axis, bits):
    return lax.ppermute(value, axis, [(i, i ^ bits) for i in range(lax.axis_size(axis))])


def per_device(
    positions,
    features,
    atom_mask,
    neighbours,
    lattice,
    pair_weight,
    kfilter,
    norm_gain,
    w_in,
    w_out,
):
    shard, _ = features.shape
    n_atoms = lax.axis_size("atoms")
    n_kvec = lax.axis_size("kvec")
    far = n_atoms // 4
    count = lattice.shape[1] // (2 * far)
    width = 256 if count % 256 == 0 else count

    message, lattice, kfilter = pack(features, atom_mask, positions, lattice, kfilter)
    scale = float(n_atoms * n_kvec * shard * KW) ** (-0.5)
    waves, kfilt = setup(lattice, kfilter, far, width, scale)
    others = range(n_kvec - 1, 0, -1)
    zs = range(1, far)
    message_x = swap(message, "atoms", 1)
    near = {k: swap(message, "kvec", k) for k in others}
    distant = [swap(message, "atoms", 4 * z) for z in zs]
    blocks = waves.shape[0]
    tables, where = [], {}

    def keep(table, names):
        tables.append(table)
        for place, name in enumerate(names):
            where[name] = tuple((len(tables) - 1, j, place) for j in range(2 * blocks))

    table, total = wave(waves, [message, message_x], [(0, None), (1, None)], None)
    keep(table, [(0, 0, 0), (1, 0, 0)])
    near_own = collect([near[k] for k in others], [(i, None) for i in range(n_kvec - 1)], after=(total,))
    near_x = swap(near_own, "atoms", 1)
    names = [(0, 0, k) for k in others] + [(1, 0, k) for k in others]
    picks = [(core, i) for core in range(2) for i in range(n_kvec - 1)]
    table, total = wave(waves, [near_own], picks[:2], total)
    keep(table, names[:2])
    distant = collect(distant, [(z, None) for z in range(far - 1)], after=(total,))
    distant_x = swap(distant, "atoms", 1)
    relayed = {k: swap(distant, "kvec", k) for k in others}
    halo_pairs = [(a, (a + 1) % n_atoms if a % 2 else (a - 1) % n_atoms) for a in range(n_atoms)]
    group = [(0, None)] + [(1, n_kvec - 1 - k) for k in range(1, n_kvec)]
    halo = lax.ppermute(collect([message, near_own], group), "atoms", halo_pairs)
    table, total = wave(waves, [near_own, near_x], picks[2:], total)
    keep(table, names[2:])
    every = [(i, z) for i in range(n_kvec - 1) for z in range(far - 1)]
    far_own = collect([relayed[k] for k in others], every, after=(total,))
    far_x = swap(far_own, "atoms", 1)
    picks = [(0, z) for z in range(far - 1)] + [(1, i) for i in range(len(every))]
    spots = [(z, k) for k in (0, *others) for z in zs]
    table, total = wave(waves, [distant, far_own], picks, total)
    keep(table, [(0, *spot) for spot in spots])
    own_factors, other_factors, low = [], [], None
    for j in range(blocks):
        after = () if low is None else (low,)
        table, part, low = wave(
            waves, [distant_x, far_x], picks, total, subset=(j, 1), after=after, low=True
        )
        tables.append(table)
        own_factors.append(part)
        other_factors.append(swap(low, "atoms", 2))
    for place, spot in enumerate(spots):
        first = len(tables) - blocks
        where[1, *spot] = tuple((first + j, half, place) for half in range(2) for j in range(blocks))

    arrays = [message, message_x, near_own, near_x, halo]
    picks = [(0, None)] + [(2, n_kvec - 1 - k) for k in range(1, n_kvec)]
    picks += [(1, None)] + [(3, n_kvec - 1 - k) for k in range(1, n_kvec)]
    picks += [(4, k) for k in range(n_kvec)]
    pair_msg = pair_message(neighbours, positions, arrays, tuple(picks), pair_weight, low)

    def runs(core, distances):
        return tuple(where[core, z, k] for k in range(n_kvec) for z in distances)

    filt, away_far = inverse_first(
        own_factors, other_factors, kfilt, pair_msg, tables, runs(1, zs), shard
    )
    crossed_far = swap(away_far, "atoms", 1)
    away_near = inverse(filt, tables, runs(1, (0,)), shard, BF16)
    crossed_near = swap(away_near, "atoms", 1)
    here_far = inverse(filt, tables, runs(0, zs), shard, F32)
    sum_far, *sends = join(here_far, crossed_far, n_kvec)
    for k in others:
        sum_far = sum_far + swap(sends[k - 1], "kvec", k).astype(F32)
    sum_far = sum_far.astype(BF16)
    here_near = inverse(filt, tables, runs(0, (0,)), shard, F32)
    own_near, *sends = join(here_near, crossed_near, n_kvec)
    parts = [own_near] + [swap(sends[k - 1], "kvec", k) for k in others]
    for z in zs:
        parts.append(swap(sum_far[:, (z - 1) * shard : z * shard], "atoms", 4 * z))
    return update(features, pair_msg, norm_gain, w_in, w_out, parts)


def solution(mesh):
    return jax.shard_map(
        per_device,
        mesh=mesh,
        in_specs=(
            P(None, ("atoms", "kvec")),
            P(("atoms", "kvec"), None),
            P(("atoms", "kvec")),
            P(("atoms", "kvec"), None),
            P(None, "kvec"),
            P(),
            P(),
            P(),
            P(),
            P(),
        ),
        out_specs=P(("atoms", "kvec"), None),
        check_vma=False,
    )
```

```python
import functools
import math

import jax
import jax.numpy as jnp
from jax import lax
from jax.experimental import pallas as pl
from jax.experimental.pallas import tpu as pltpu
from jax.sharding import PartitionSpec as P

KW = 12288
BLOCK_ATOMS = 128
F32 = jnp.float32
BF16 = jnp.bfloat16

SIN_COEF = (4.442879586561992, -7.307818050390618, 3.5977887417720016, -0.7912382192058507)
SLACK = 1e-5
TAIL = 16


def params(mib=16):
    return pltpu.CompilerParams(vmem_limit_bytes=mib << 20)


SMEM = pl.BlockSpec(memory_space=pltpu.SMEM)
VMEM = pl.BlockSpec(memory_space=pltpu.VMEM)
ANY = pl.BlockSpec(memory_space=pl.ANY)


def horner(u, coef):
    acc = coef[-1] * u + coef[-2]
    for c in reversed(coef[:-2]):
        acc = acc * u + c
    return acc


def pack_kernel(*refs):
    features_hbm, mask_hbm, pos_hbm, lattice_hbm, kfilter_hbm = refs[:5]
    out_ref, lattice_ref, kfilter_ref, features_ref, mask_ref, pos_ref, scr, sems = refs[5:]
    copies = [
        pltpu.make_async_copy(source, target, sems.at[i])
        for i, (source, target) in enumerate(
            (
                (features_hbm, features_ref),
                (mask_hbm, mask_ref),
                (pos_hbm, pos_ref),
                (lattice_hbm, lattice_ref),
                (kfilter_hbm, kfilter_ref),
            )
        )
    ]
    for copy in copies:
        copy.start()
    for copy in copies:
        copy.wait()
    channels = features_ref.shape[1]
    mask = mask_ref[...].astype(F32)
    out_ref[0:channels, :] = (features_ref[...].astype(F32).T * mask).astype(BF16)
    value = pos_ref[...] * 0.125
    high = value.astype(BF16).astype(F32)
    rest = value - high
    mid = rest.astype(BF16).astype(F32)
    scr[...] = jnp.zeros_like(scr)
    scr[0:3, :] = high
    scr[3:6, :] = mid
    scr[6:9, :] = rest - mid
    out_ref[channels : channels + TAIL, :] = scr[...].astype(BF16)


def pack(features, mask, positions, lattice, kfilter):
    shard, channels = features.shape
    arrays = (features, mask[None, :], positions, lattice, kfilter)
    return pl.pallas_call(
        pack_kernel,
        in_specs=[pl.BlockSpec(memory_space=pltpu.HBM)] * 5,
        out_specs=[VMEM] * 3,
        out_shape=[
            jax.ShapeDtypeStruct((channels + TAIL, shard), BF16),
            jax.ShapeDtypeStruct(lattice.shape, lattice.dtype),
            jax.ShapeDtypeStruct(kfilter.shape, kfilter.dtype),
        ],
        scratch_shapes=[
            pltpu.VMEM((shard, channels), BF16),
            pltpu.VMEM((1, shard), jnp.int32),
            pltpu.VMEM((3, shard), F32),
            pltpu.VMEM((TAIL, shard), F32),
            pltpu.SemaphoreType.DMA((5,)),
        ],
        compiler_params=params(),
        name="pack",
    )(*(pltpu.with_memory_space_constraint(x, pltpu.HBM) for x in arrays))


def setup_kernel(far, nbasis, scale, lattice_ref, kfilter_ref, wave_ref, kfilt_ref, scr):
    blocks, width, _ = wave_ref.shape
    a_index = lax.axis_index("atoms")
    part = a_index % 2 + 2 * (a_index // 4)
    count = blocks * width
    kfilter = kfilter_ref[...].T
    for j in range(blocks):
        lattice = jnp.zeros((3, width), F32)
        for p in range(2 * far):
            at = p * count + j * width
            mine = (part == p).astype(F32)
            lattice += lattice_ref[:, at : at + width].astype(F32) * mine
        scr[...] = jnp.zeros_like(scr)
        for copy in range(3):
            scr[3 * copy : 3 * copy + 3, :] = lattice
        wave_ref[j] = scr[...].T.astype(BF16)
        wave = lattice * (2.0 * math.pi / 8.0)
        kmag = jnp.sqrt(
            wave[0:1] * wave[0:1] + wave[1:2] * wave[1:2] + wave[2:3] * wave[2:3]
        )
        total = jnp.zeros(kfilt_ref.shape[1:], F32)
        for p in range(nbasis):
            basis = jnp.exp(-0.5 * ((kmag - (p + 0.5) * (21.0 / nbasis)) / (21.0 / nbasis)) ** 2)
            total += kfilter[:, p : p + 1] * basis
        kfilt_ref[j] = total * scale


def setup(lattice, kfilter, far, width, scale):
    nbasis, channels = kfilter.shape
    blocks = lattice.shape[1] // (2 * far * width)
    return pl.pallas_call(
        functools.partial(setup_kernel, far, nbasis, scale),
        in_specs=[VMEM] * 2,
        out_specs=[VMEM] * 2,
        out_shape=[
            jax.ShapeDtypeStruct((blocks, width, TAIL), BF16),
            jax.ShapeDtypeStruct((blocks, channels, width), F32),
        ],
        scratch_shapes=[pltpu.VMEM((TAIL, width), F32)],
        compiler_params=params(),
        name="setup",
    )(lattice, kfilter)


def wave_kernel(picks, arrays, first, start, waits, low, *refs):
    refs = list(refs)
    take = lambda n: [refs.pop(0) for _ in range(n)]
    (lattice_ref,) = take(1)
    messages = take(arrays)
    before_ref = None if start else take(1)[0]
    take(waits)
    table_ref, total_ref = take(2)
    low_ref = take(1)[0] if low else None
    feat_scr, pos_scr = take(2)
    phases, buffers = take(2), take(2)
    blocks, width = table_ref.shape[0] // 2, table_ref.shape[1]
    every = lattice_ref.shape[0]
    pairs, channels, both = feat_scr.shape
    shard = both // 2
    for place, (array, index) in enumerate(picks):
        item = messages[array] if index is None else messages[array].at[index]
        lanes = slice(place % 2 * shard, (place % 2 + 1) * shard)
        feat_scr[place // 2, :, lanes] = item[0:channels, :]
        pos_scr[place // 2, :, lanes] = item[channels:, :]
    for j in range(2 * blocks):
        if start:
            total_ref[j] = jnp.zeros_like(total_ref[j])
        else:
            total_ref[j] = before_ref[j // blocks * every + first + j % blocks]
    buffers[1][...] = jnp.zeros_like(buffers[1])
    steps = pairs * blocks

    def phase(i, slot):
        i = jnp.minimum(i, steps - 1)
        phases[slot][...] = jnp.dot(
            lattice_ref[first + i % blocks], pos_scr[i // blocks], preferred_element_type=F32
        )

    def product(i, slot, half):
        pair, block = i // blocks, i % blocks
        total_ref[half * blocks + block] += lax.dot_general(
            feat_scr[pair], buffers[slot][half], (((1,), (1,)), ((), ())), preferred_element_type=F32
        )

    def unit(i, slot):
        pair, block = i // blocks, i % blocks
        before = jnp.maximum(i - 1, 0)
        lanes = pl.ds(pl.multiple_of(pair * both, both), both)
        rows = 16
        for n, at in enumerate(range(0, width, rows)):
            if n == 4:
                product(before, 1 - slot, 0)
            if n == 10:
                product(before, 1 - slot, 1)
            turns = phases[slot][at : at + rows, :]
            r = turns - jnp.round(turns)
            s = horner(r * r, SIN_COEF) * r
            square = s * s
            w = (2.0 + SLACK) - square
            cosine = (1.0 - square).astype(BF16)
            sine = (s * (w * lax.rsqrt(w))).astype(BF16)
            buffers[slot][0, at : at + rows, :] = cosine
            buffers[slot][1, at : at + rows, :] = sine
            table_ref[block, at : at + rows, lanes] = cosine
            table_ref[blocks + block, at : at + rows, lanes] = sine
        phase(i + 2, slot)

    phase(0, 0)
    phase(1, 1)

    def body(n, carry):
        unit(2 * n, 0)
        unit(2 * n + 1, 1)
        return carry

    lax.fori_loop(0, steps // 2, body, 0)
    if steps % 2:
        unit(steps - 1, 0)
    for half in range(2):
        product(steps - 1, (steps - 1) % 2, half)
    if low:
        low_ref[...] = total_ref[...].astype(BF16)


def wave(lattice, arrays, picks, before, subset=None, after=(), low=False):
    every, width, _ = lattice.shape
    first, blocks = subset or (0, every)
    pieces = len(picks)
    rows, shard = arrays[0].shape[-2:]
    channels = rows - TAIL
    args = [lattice, *arrays] + ([] if before is None else [before])
    factor = (2 * blocks, channels, width)
    shapes = [
        jax.ShapeDtypeStruct((2 * blocks, width, pieces * shard), BF16),
        jax.ShapeDtypeStruct(factor, F32),
    ]
    if low:
        shapes.append(jax.ShapeDtypeStruct(factor, BF16))
    pairs = blocks * width * pieces * shard
    return pl.pallas_call(
        functools.partial(
            wave_kernel, tuple(picks), len(arrays), first, before is None, len(after), low
        ),
        in_specs=[VMEM] * len(args) + [ANY] * len(after),
        out_specs=[VMEM] * len(shapes),
        out_shape=shapes,
        scratch_shapes=[
            pltpu.VMEM((pieces // 2, channels, 2 * shard), BF16),
            pltpu.VMEM((pieces // 2, TAIL, 2 * shard), BF16),
            pltpu.VMEM((width, 2 * shard), F32),
            pltpu.VMEM((width, 2 * shard), F32),
            pltpu.VMEM((2, width, 2 * shard), BF16),
            pltpu.VMEM((2, width, 2 * shard), BF16),
        ],
        compiler_params=params(),
        cost_estimate=pl.CostEstimate(
            flops=4 * pairs * channels, bytes_accessed=4 * pairs, transcendentals=pairs
        ),
        name="wave",
    )(*args, *after)


def collect_kernel(picks, *refs):
    for p, (array, index) in enumerate(picks):
        ref = refs[array]
        refs[-1][p] = ref[...] if index is None else ref[index]


def collect(arrays, picks, after=()):
    return pl.pallas_call(
        functools.partial(collect_kernel, picks),
        in_specs=[VMEM] * len(arrays) + [ANY] * len(after),
        out_specs=VMEM,
        out_shape=jax.ShapeDtypeStruct((len(picks), *arrays[0].shape[-2:]), BF16),
        compiler_params=params(),
        name="collect",
    )(*arrays, *after)


def transform(filt_ref, table_refs, pieces, out_ref, shard):
    for at, places in enumerate(pieces):
        acc = None
        for j, (table, index, place) in enumerate(places):
            part = jnp.dot(
                filt_ref[j],
                table_refs[table][index, :, place * shard : (place + 1) * shard],
                preferred_element_type=F32,
            )
            acc = part if acc is None else acc + part
        out_ref[:, at * shard : (at + 1) * shard] = acc.astype(out_ref.dtype)


def first_kernel(pieces, shard, parts, blocks, *refs):
    own_refs, other_refs, refs = refs[:parts], refs[parts : 2 * parts], refs[2 * parts :]
    kfilt_ref, table_refs, (filt_ref, out_ref) = refs[0], refs[2:-2], refs[-2:]
    count = kfilt_ref.shape[0]
    for half in range(2):
        for j in range(count):
            part, index = j // blocks, half * blocks + j % blocks
            total = own_refs[part][index] + other_refs[part][index].astype(F32)
            filt_ref[half * count + j] = (total * kfilt_ref[j]).astype(BF16)
    transform(filt_ref, table_refs, pieces, out_ref, shard)


def inverse_kernel(pieces, shard, filt_ref, *refs):
    transform(filt_ref, refs[:-1], pieces, refs[-1], shard)


def inverse_cost(count, channels, width, atoms):
    return pl.CostEstimate(
        flops=2 * count * channels * width * atoms,
        bytes_accessed=2 * count * width * atoms,
        transcendentals=0,
    )


def used(tables, pieces):
    names = sorted({place[0] for places in pieces for place in places})
    moved = tuple(tuple((names.index(t), i, p) for t, i, p in places) for places in pieces)
    return [tables[t] for t in names], moved


def inverse_first(own, other, kfilt, after, tables, pieces, shard):
    count, channels, width = kfilt.shape
    tables, pieces = used(tables, pieces)
    atoms = shard * len(pieces)
    blocks = count // len(own)
    return pl.pallas_call(
        functools.partial(first_kernel, pieces, shard, len(own), blocks),
        in_specs=[VMEM] * (2 * len(own) + 1) + [ANY] + [VMEM] * len(tables),
        out_specs=[VMEM] * 2,
        out_shape=[
            jax.ShapeDtypeStruct((2 * count, channels, width), BF16),
            jax.ShapeDtypeStruct((channels, atoms), BF16),
        ],
        compiler_params=params(),
        cost_estimate=inverse_cost(2 * count, channels, width, atoms),
        name="first",
    )(*own, *other, kfilt, after, *tables)


def inverse(filt, tables, pieces, shard, dtype):
    count, channels, width = filt.shape
    tables, pieces = used(tables, pieces)
    atoms = shard * len(pieces)
    return pl.pallas_call(
        functools.partial(inverse_kernel, pieces, shard),
        in_specs=[VMEM] * (1 + len(tables)),
        out_specs=VMEM,
        out_shape=jax.ShapeDtypeStruct((channels, atoms), dtype),
        compiler_params=params(),
        cost_estimate=inverse_cost(count, channels, width, atoms),
        name="inverse",
    )(filt, *tables)


def join_kernel(here_ref, arrived_ref, own_ref, *send_refs):
    width = own_ref.shape[1]
    for p in range(len(send_refs) + 1):
        lanes = slice(p * width, (p + 1) * width)
        total = here_ref[:, lanes] + arrived_ref[:, lanes].astype(F32)
        if p:
            send_refs[p - 1][...] = total.astype(BF16)
        else:
            own_ref[...] = total


def join(here, arrived, pieces):
    channels, atoms = here.shape
    shape = (channels, atoms // pieces)
    return pl.pallas_call(
        join_kernel,
        in_specs=[VMEM] * 2,
        out_specs=[VMEM] * pieces,
        out_shape=[jax.ShapeDtypeStruct(shape, F32)]
        + [jax.ShapeDtypeStruct(shape, BF16)] * (pieces - 1),
        compiler_params=params(),
        name="join",
    )(here, arrived)


def pair_kernel(nbasis, pieces, output_scale, picks, arrays, neighbours_ref, own_pos_ref, *refs):
    message_refs, refs = refs[:arrays], refs[arrays:]
    weight_ref, _, out_ref, feat_scr, pos_scr, own_scr, basis_scr, near_scr, spot_scr = refs
    block = BLOCK_ATOMS
    both = 2 * block
    width = 12.0 / nbasis
    own_blocks, neighbours = neighbours_ref.shape
    shard = own_blocks * block
    channels = out_ref.shape[1]

    views = [
        message_refs[array] if index is None else message_refs[array].at[index]
        for array, index in picks
    ]
    for place, ref in enumerate(views):
        lanes = slice(place * shard, (place + 1) * shard)
        feat_scr[:, lanes] = ref[0:channels, :]
        parts = ref[channels:, :].astype(F32)
        pos_scr[0:3, lanes] = (parts[0:3] + parts[3:6] + parts[6:9]) * 8.0
    for b in range(own_blocks):
        for d in range(3):
            row = own_pos_ref[d : d + 1, b * block : (b + 1) * block]
            own_scr[b, d] = jnp.broadcast_to(row, (both, block)).T

    a_index = lax.axis_index("atoms")
    k_index = lax.axis_index("kvec")
    n_atoms = lax.axis_size("atoms")
    group_blk = own_blocks * pieces
    first = (a_index * pieces + k_index) * own_blocks
    toward = jnp.where(a_index % 2 == 0, 1, n_atoms - 1)

    def divide(value, by):
        if by & (by - 1):
            return value // by, value % by
        return lax.shift_right_logical(value, by.bit_length() - 1), value & (by - 1)

    def place_of(ident):
        group, within = divide(ident, group_blk)
        ahead = divide(group - a_index + n_atoms, n_atoms)[1]
        which = jnp.where(ahead == 0, 0, jnp.where(ahead == toward, 1, 2))
        piece, rest = divide(within, own_blocks)
        return (which * pieces + (piece ^ k_index)) * own_blocks + rest

    rows = 16
    row_index = lax.broadcasted_iota(jnp.int32, (rows, both), 0)
    lane = lax.broadcasted_iota(jnp.int32, (1, both), 1)
    per_block = neighbours // 2
    log2e = math.log2(math.e)

    def unit(b, pair, carry):
        own_place = jnp.full((1, both), -1, jnp.int32)
        for h in range(2):
            ident = neighbours_ref[b, 2 * pair + h]
            lanes = pl.ds(pl.multiple_of(place_of(ident) * block, block), block)
            here = pl.ds(pl.multiple_of(pair * both + h * block, block), block)
            near_scr[b, :, here] = feat_scr[:, lanes]
            spot_scr[0:3, h * block : (h + 1) * block] = pos_scr[0:3, lanes]
            inside = (lane >= h * block) & (lane < (h + 1) * block) & (ident == first + b)
            own_place = jnp.where(inside, lane - h * block, own_place)
        lanes = pl.ds(pl.multiple_of(pair * both, both), both)
        for at in range(0, block, rows):
            dist2 = (own_scr[b, 0, at : at + rows, :] - spot_scr[0:1, :]) ** 2
            dist2 += (own_scr[b, 1, at : at + rows, :] - spot_scr[1:2, :]) ** 2
            dist2 += (own_scr[b, 2, at : at + rows, :] - spot_scr[2:3, :]) ** 2
            radius = dist2 * lax.rsqrt(jnp.maximum(dist2, 1e-30))
            env = (16.0 * output_scale) / (16.0 + dist2)
            env = jnp.where(row_index + at == own_place, 0.0, env)
            v = radius * (log2e / width) - 0.5 * log2e
            value = jnp.exp2(v * v * (-0.5 / log2e)) * env
            ratio = jnp.exp2(v)
            for k in range(nbasis):
                if k:
                    value = value * ratio
                basis_scr[b, k * block + at : k * block + at + rows, lanes] = value.astype(BF16)
        return carry

    for b in range(own_blocks):
        lax.fori_loop(0, per_block, functools.partial(unit, b), 0)
    for b in range(own_blocks):
        total = jnp.zeros((block, channels), F32)
        for k in range(0, nbasis, 2):
            gathered = lax.dot_general(
                basis_scr[b, k * block : (k + 2) * block, :],
                near_scr[b],
                (((1,), (1,)), ((), ())),
                preferred_element_type=F32,
            )
            parts = [
                gathered[h * block : (h + 1) * block] * math.exp(-0.5 * (k + h) * (k + h))
                for h in range(2)
            ]
            total += jnp.dot(
                jnp.concatenate(parts, axis=1).astype(BF16),
                weight_ref[k * channels : (k + 2) * channels, :],
                preferred_element_type=F32,
            )
        out_ref[b * block : (b + 1) * block, :] = total


def pair_message(neighbours, own_pos, arrays, picks, weight, after):
    channels = weight.shape[1]
    nbasis = weight.shape[0] // channels
    pieces = len(picks) // 3
    shard = own_pos.shape[1]
    count = neighbours.shape[1]
    scale = float(count * BLOCK_ATOMS) ** (-0.5)
    window = 3 * pieces * shard
    blocks = shard // BLOCK_ATOMS
    return pl.pallas_call(
        functools.partial(pair_kernel, nbasis, pieces, scale, picks, len(arrays)),
        in_specs=[SMEM] + [VMEM] * (2 + len(arrays)) + [ANY],
        out_specs=VMEM,
        out_shape=jax.ShapeDtypeStruct((shard, channels), F32),
        scratch_shapes=[
            pltpu.VMEM((channels, window), BF16),
            pltpu.VMEM((8, window), F32),
            pltpu.VMEM((blocks, 3, BLOCK_ATOMS, 2 * BLOCK_ATOMS), F32),
            pltpu.VMEM((blocks, nbasis * BLOCK_ATOMS, count * BLOCK_ATOMS), BF16),
            pltpu.VMEM((blocks, channels, count * BLOCK_ATOMS), BF16),
            pltpu.VMEM((8, 2 * BLOCK_ATOMS), F32),
        ],
        compiler_params=params(),
        cost_estimate=pl.CostEstimate(
            flops=2 * shard * count * BLOCK_ATOMS * (nbasis * channels + 40),
            bytes_accessed=2 * window * channels,
            transcendentals=3 * shard * count * BLOCK_ATOMS,
        ),
        name="pair",
    )(neighbours, own_pos, *arrays, weight, after)


def update_kernel(*refs):
    features_ref, pair_ref, gain_ref, w_in_ref, w_out_ref = refs[:5]
    parts, out_ref = refs[5:-1], refs[-1]
    long_t = parts[0][...].astype(F32)
    for part in parts[1:]:
        long_t = long_t + part[...].astype(F32)
    total = features_ref[...].astype(F32) + pair_ref[...] + long_t.T
    mean = jnp.mean(total * total, axis=-1, keepdims=True)
    normed = (total * lax.rsqrt(mean + 1e-06) * gain_ref[...]).astype(BF16)
    pre = jnp.dot(normed, w_in_ref[...], preferred_element_type=F32)
    hidden = (pre / (1.0 + jnp.exp(-pre))).astype(BF16)
    out_ref[...] = (
        total + jnp.dot(hidden, w_out_ref[...], preferred_element_type=F32)
    ).astype(BF16)


def update(features, pair_msg, gain, w_in, w_out, parts):
    return pl.pallas_call(
        update_kernel,
        in_specs=[VMEM] * (5 + len(parts)),
        out_specs=VMEM,
        out_shape=jax.ShapeDtypeStruct(features.shape, BF16),
        compiler_params=params(),
        name="update",
    )(features, pair_msg, gain[None, :], w_in, w_out, *parts)


def swap(value, axis, bits):
    return lax.ppermute(value, axis, [(i, i ^ bits) for i in range(lax.axis_size(axis))])


def per_device(
    positions,
    features,
    atom_mask,
    neighbours,
    lattice,
    pair_weight,
    kfilter,
    norm_gain,
    w_in,
    w_out,
):
    shard, _ = features.shape
    n_atoms = lax.axis_size("atoms")
    n_kvec = lax.axis_size("kvec")
    far = n_atoms // 4
    count = lattice.shape[1] // (2 * far)
    width = 256 if count % 256 == 0 else count

    message, lattice, kfilter = pack(features, atom_mask, positions, lattice, kfilter)
    scale = float(n_atoms * n_kvec * shard * KW) ** (-0.5)
    waves, kfilt = setup(lattice, kfilter, far, width, scale)
    others = range(n_kvec - 1, 0, -1)
    zs = range(1, far)
    message_x = swap(message, "atoms", 1)
    near = {k: swap(message, "kvec", k) for k in others}
    distant = [swap(message, "atoms", 4 * z) for z in zs]
    blocks = waves.shape[0]
    tables, where = [], {}

    def keep(table, names):
        tables.append(table)
        for place, name in enumerate(names):
            where[name] = tuple((len(tables) - 1, j, place) for j in range(2 * blocks))

    table, total = wave(waves, [message, message_x], [(0, None), (1, None)], None)
    keep(table, [(0, 0, 0), (1, 0, 0)])
    near_own = collect([near[k] for k in others], [(i, None) for i in range(n_kvec - 1)], after=(total,))
    near_x = swap(near_own, "atoms", 1)
    names = [(0, 0, k) for k in others] + [(1, 0, k) for k in others]
    picks = [(core, i) for core in range(2) for i in range(n_kvec - 1)]
    table, total = wave(waves, [near_own], picks[:2], total)
    keep(table, names[:2])
    distant = collect(distant, [(z, None) for z in range(far - 1)], after=(total,))
    distant_x = swap(distant, "atoms", 1)
    relayed = {k: swap(distant, "kvec", k) for k in others}
    halo_pairs = [(a, (a + 1) % n_atoms if a % 2 else (a - 1) % n_atoms) for a in range(n_atoms)]
    group = [(0, None)] + [(1, n_kvec - 1 - k) for k in range(1, n_kvec)]
    halo = lax.ppermute(collect([message, near_own], group), "atoms", halo_pairs)
    table, total = wave(waves, [near_own, near_x], picks[2:], total)
    keep(table, names[2:])
    every = [(i, z) for i in range(n_kvec - 1) for z in range(far - 1)]
    far_own = collect([relayed[k] for k in others], every, after=(total,))
    far_x = swap(far_own, "atoms", 1)
    picks = [(0, z) for z in range(far - 1)] + [(1, i) for i in range(len(every))]
    spots = [(z, k) for k in (0, *others) for z in zs]
    table, total = wave(waves, [distant, far_own], picks, total)
    keep(table, [(0, *spot) for spot in spots])
    own_factors, other_factors, low = [], [], None
    for j in range(blocks):
        after = () if low is None else (low,)
        table, part, low = wave(
            waves, [distant_x, far_x], picks, total, subset=(j, 1), after=after, low=True
        )
        tables.append(table)
        own_factors.append(part)
        other_factors.append(swap(low, "atoms", 2))
    for place, spot in enumerate(spots):
        first = len(tables) - blocks
        where[1, *spot] = tuple((first + j, half, place) for half in range(2) for j in range(blocks))

    arrays = [message, message_x, near_own, near_x, halo]
    picks = [(0, None)] + [(2, n_kvec - 1 - k) for k in range(1, n_kvec)]
    picks += [(1, None)] + [(3, n_kvec - 1 - k) for k in range(1, n_kvec)]
    picks += [(4, k) for k in range(n_kvec)]
    pair_msg = pair_message(neighbours, positions, arrays, tuple(picks), pair_weight, low)

    def runs(core, distances):
        return tuple(where[core, z, k] for k in range(n_kvec) for z in distances)

    filt, away_far = inverse_first(
        own_factors, other_factors, kfilt, pair_msg, tables, runs(1, zs), shard
    )
    crossed_far = swap(away_far, "atoms", 1)
    away_near = inverse(filt, tables, runs(1, (0,)), shard, BF16)
    crossed_near = swap(away_near, "atoms", 1)
    here_far = inverse(filt, tables, runs(0, zs), shard, F32)
    sum_far, *sends = join(here_far, crossed_far, n_kvec)
    for k in others:
        sum_far = sum_far + swap(sends[k - 1], "kvec", k).astype(F32)
    sum_far = sum_far.astype(BF16)
    here_near = inverse(filt, tables, runs(0, (0,)), shard, F32)
    own_near, *sends = join(here_near, crossed_near, n_kvec)
    parts = [own_near] + [swap(sends[k - 1], "kvec", k) for k in others]
    for z in zs:
        parts.append(swap(sum_far[:, (z - 1) * shard : z * shard], "atoms", 4 * z))
    return update(features, pair_msg, norm_gain, w_in, w_out, parts)


def solution(mesh):
    return jax.shard_map(
        per_device,
        mesh=mesh,
        in_specs=(
            P(None, ("atoms", "kvec")),
            P(("atoms", "kvec"), None),
            P(("atoms", "kvec")),
            P(("atoms", "kvec"), None),
            P(None, "kvec"),
            P(),
            P(),
            P(),
            P(),
            P(),
        ),
        out_specs=P(("atoms", "kvec"), None),
        check_vma=False,
    )
```

```python
import functools
import math

import jax
import jax.numpy as jnp
from jax import lax
from jax.experimental import pallas as pl
from jax.experimental.pallas import tpu as pltpu
from jax.sharding import PartitionSpec as P

KW = 12288
BLOCK_ATOMS = 128
F32 = jnp.float32
BF16 = jnp.bfloat16

SIN_COEF = (4.442879586561992, -7.307818050390618, 3.5977887417720016, -0.7912382192058507)
SLACK = 1e-5
TAIL = 16


def params(mib=16):
    return pltpu.CompilerParams(vmem_limit_bytes=mib << 20)


SMEM = pl.BlockSpec(memory_space=pltpu.SMEM)
VMEM = pl.BlockSpec(memory_space=pltpu.VMEM)
ANY = pl.BlockSpec(memory_space=pl.ANY)


def horner(u, coef):
    acc = coef[-1] * u + coef[-2]
    for c in reversed(coef[:-2]):
        acc = acc * u + c
    return acc


def pack_kernel(*refs):
    features_hbm, mask_hbm, pos_hbm, lattice_hbm, kfilter_hbm = refs[:5]
    out_ref, lattice_ref, kfilter_ref, features_ref, mask_ref, pos_ref, scr, sems = refs[5:]
    copies = [
        pltpu.make_async_copy(source, target, sems.at[i])
        for i, (source, target) in enumerate(
            (
                (features_hbm, features_ref),
                (mask_hbm, mask_ref),
                (pos_hbm, pos_ref),
                (lattice_hbm, lattice_ref),
                (kfilter_hbm, kfilter_ref),
            )
        )
    ]
    for copy in copies:
        copy.start()
    for copy in copies:
        copy.wait()
    channels = features_ref.shape[1]
    mask = mask_ref[...].astype(F32)
    out_ref[0:channels, :] = (features_ref[...].astype(F32).T * mask).astype(BF16)
    value = pos_ref[...] * 0.125
    high = value.astype(BF16).astype(F32)
    rest = value - high
    mid = rest.astype(BF16).astype(F32)
    scr[...] = jnp.zeros_like(scr)
    scr[0:3, :] = high
    scr[3:6, :] = mid
    scr[6:9, :] = rest - mid
    out_ref[channels : channels + TAIL, :] = scr[...].astype(BF16)


def pack(features, mask, positions, lattice, kfilter):
    shard, channels = features.shape
    arrays = (features, mask[None, :], positions, lattice, kfilter)
    return pl.pallas_call(
        pack_kernel,
        in_specs=[pl.BlockSpec(memory_space=pltpu.HBM)] * 5,
        out_specs=[VMEM] * 3,
        out_shape=[
            jax.ShapeDtypeStruct((channels + TAIL, shard), BF16),
            jax.ShapeDtypeStruct(lattice.shape, lattice.dtype),
            jax.ShapeDtypeStruct(kfilter.shape, kfilter.dtype),
        ],
        scratch_shapes=[
            pltpu.VMEM((shard, channels), BF16),
            pltpu.VMEM((1, shard), jnp.int32),
            pltpu.VMEM((3, shard), F32),
            pltpu.VMEM((TAIL, shard), F32),
            pltpu.SemaphoreType.DMA((5,)),
        ],
        compiler_params=params(),
        name="pack",
    )(*(pltpu.with_memory_space_constraint(x, pltpu.HBM) for x in arrays))


def setup_kernel(far, nbasis, scale, lattice_ref, kfilter_ref, wave_ref, kfilt_ref, scr):
    blocks, width, _ = wave_ref.shape
    a_index = lax.axis_index("atoms")
    part = a_index % 2 + 2 * (a_index // 4)
    count = blocks * width
    kfilter = kfilter_ref[...].T
    for j in range(blocks):
        lattice = jnp.zeros((3, width), F32)
        for p in range(2 * far):
            at = p * count + j * width
            mine = (part == p).astype(F32)
            lattice += lattice_ref[:, at : at + width].astype(F32) * mine
        scr[...] = jnp.zeros_like(scr)
        for copy in range(3):
            scr[3 * copy : 3 * copy + 3, :] = lattice
        wave_ref[j] = scr[...].T.astype(BF16)
        wave = lattice * (2.0 * math.pi / 8.0)
        kmag = jnp.sqrt(
            wave[0:1] * wave[0:1] + wave[1:2] * wave[1:2] + wave[2:3] * wave[2:3]
        )
        total = jnp.zeros(kfilt_ref.shape[1:], F32)
        for p in range(nbasis):
            basis = jnp.exp(-0.5 * ((kmag - (p + 0.5) * (21.0 / nbasis)) / (21.0 / nbasis)) ** 2)
            total += kfilter[:, p : p + 1] * basis
        kfilt_ref[j] = total * scale


def setup(lattice, kfilter, far, width, scale):
    nbasis, channels = kfilter.shape
    blocks = lattice.shape[1] // (2 * far * width)
    return pl.pallas_call(
        functools.partial(setup_kernel, far, nbasis, scale),
        in_specs=[VMEM] * 2,
        out_specs=[VMEM] * 2,
        out_shape=[
            jax.ShapeDtypeStruct((blocks, width, TAIL), BF16),
            jax.ShapeDtypeStruct((blocks, channels, width), F32),
        ],
        scratch_shapes=[pltpu.VMEM((TAIL, width), F32)],
        compiler_params=params(),
        name="setup",
    )(lattice, kfilter)


def wave_kernel(picks, arrays, first, start, waits, low, *refs):
    refs = list(refs)
    take = lambda n: [refs.pop(0) for _ in range(n)]
    (lattice_ref,) = take(1)
    messages = take(arrays)
    before_ref = None if start else take(1)[0]
    take(waits)
    table_ref, total_ref = take(2)
    low_ref = take(1)[0] if low else None
    feat_scr, pos_scr = take(2)
    phases, buffers = take(2), take(2)
    blocks, width = table_ref.shape[0] // 2, table_ref.shape[1]
    every = lattice_ref.shape[0]
    pairs, channels, both = feat_scr.shape
    shard = both // 2
    for place, (array, index) in enumerate(picks):
        item = messages[array] if index is None else messages[array].at[index]
        lanes = slice(place % 2 * shard, (place % 2 + 1) * shard)
        feat_scr[place // 2, :, lanes] = item[0:channels, :]
        pos_scr[place // 2, :, lanes] = item[channels:, :]
    for j in range(2 * blocks):
        if start:
            total_ref[j] = jnp.zeros_like(total_ref[j])
        else:
            total_ref[j] = before_ref[j // blocks * every + first + j % blocks]
    buffers[1][...] = jnp.zeros_like(buffers[1])
    steps = pairs * blocks

    def phase(i, slot):
        i = jnp.minimum(i, steps - 1)
        phases[slot][...] = jnp.dot(
            lattice_ref[first + i % blocks], pos_scr[i // blocks], preferred_element_type=F32
        )

    def product(i, slot, half):
        pair, block = i // blocks, i % blocks
        total_ref[half * blocks + block] += lax.dot_general(
            feat_scr[pair], buffers[slot][half], (((1,), (1,)), ((), ())), preferred_element_type=F32
        )

    def unit(i, slot):
        pair, block = i // blocks, i % blocks
        before = jnp.maximum(i - 1, 0)
        lanes = pl.ds(pl.multiple_of(pair * both, both), both)
        rows = 16
        for n, at in enumerate(range(0, width, rows)):
            if n == 4:
                product(before, 1 - slot, 0)
            if n == 10:
                product(before, 1 - slot, 1)
            turns = phases[slot][at : at + rows, :]
            r = turns - jnp.round(turns)
            s = horner(r * r, SIN_COEF) * r
            square = s * s
            w = (2.0 + SLACK) - square
            cosine = (1.0 - square).astype(BF16)
            sine = (s * (w * lax.rsqrt(w))).astype(BF16)
            buffers[slot][0, at : at + rows, :] = cosine
            buffers[slot][1, at : at + rows, :] = sine
            table_ref[block, at : at + rows, lanes] = cosine
            table_ref[blocks + block, at : at + rows, lanes] = sine
        phase(i + 2, slot)

    phase(0, 0)
    phase(1, 1)

    def body(n, carry):
        unit(2 * n, 0)
        unit(2 * n + 1, 1)
        return carry

    lax.fori_loop(0, steps // 2, body, 0)
    if steps % 2:
        unit(steps - 1, 0)
    for half in range(2):
        product(steps - 1, (steps - 1) % 2, half)
    if low:
        low_ref[...] = total_ref[...].astype(BF16)


def wave(lattice, arrays, picks, before, subset=None, after=(), low=False):
    every, width, _ = lattice.shape
    first, blocks = subset or (0, every)
    pieces = len(picks)
    rows, shard = arrays[0].shape[-2:]
    channels = rows - TAIL
    args = [lattice, *arrays] + ([] if before is None else [before])
    factor = (2 * blocks, channels, width)
    shapes = [
        jax.ShapeDtypeStruct((2 * blocks, width, pieces * shard), BF16),
        jax.ShapeDtypeStruct(factor, F32),
    ]
    if low:
        shapes.append(jax.ShapeDtypeStruct(factor, BF16))
    pairs = blocks * width * pieces * shard
    return pl.pallas_call(
        functools.partial(
            wave_kernel, tuple(picks), len(arrays), first, before is None, len(after), low
        ),
        in_specs=[VMEM] * len(args) + [ANY] * len(after),
        out_specs=[VMEM] * len(shapes),
        out_shape=shapes,
        scratch_shapes=[
            pltpu.VMEM((pieces // 2, channels, 2 * shard), BF16),
            pltpu.VMEM((pieces // 2, TAIL, 2 * shard), BF16),
            pltpu.VMEM((width, 2 * shard), F32),
            pltpu.VMEM((width, 2 * shard), F32),
            pltpu.VMEM((2, width, 2 * shard), BF16),
            pltpu.VMEM((2, width, 2 * shard), BF16),
        ],
        compiler_params=params(),
        cost_estimate=pl.CostEstimate(
            flops=4 * pairs * channels, bytes_accessed=4 * pairs, transcendentals=pairs
        ),
        name="wave",
    )(*args, *after)


def collect_kernel(picks, *refs):
    for p, (array, index) in enumerate(picks):
        ref = refs[array]
        refs[-1][p] = ref[...] if index is None else ref[index]


def collect(arrays, picks, after=()):
    return pl.pallas_call(
        functools.partial(collect_kernel, picks),
        in_specs=[VMEM] * len(arrays) + [ANY] * len(after),
        out_specs=VMEM,
        out_shape=jax.ShapeDtypeStruct((len(picks), *arrays[0].shape[-2:]), BF16),
        compiler_params=params(),
        name="collect",
    )(*arrays, *after)


def transform(filt_ref, table_refs, pieces, out_ref, shard):
    for at, places in enumerate(pieces):
        acc = None
        for j, (table, index, place) in enumerate(places):
            part = jnp.dot(
                filt_ref[j],
                table_refs[table][index, :, place * shard : (place + 1) * shard],
                preferred_element_type=F32,
            )
            acc = part if acc is None else acc + part
        out_ref[:, at * shard : (at + 1) * shard] = acc.astype(out_ref.dtype)


def first_kernel(pieces, shard, parts, blocks, *refs):
    own_refs, other_refs, refs = refs[:parts], refs[parts : 2 * parts], refs[2 * parts :]
    kfilt_ref, table_refs, (filt_ref, out_ref) = refs[0], refs[2:-2], refs[-2:]
    count = kfilt_ref.shape[0]
    for half in range(2):
        for j in range(count):
            part, index = j // blocks, half * blocks + j % blocks
            total = own_refs[part][index] + other_refs[part][index].astype(F32)
            filt_ref[half * count + j] = (total * kfilt_ref[j]).astype(BF16)
    transform(filt_ref, table_refs, pieces, out_ref, shard)


def inverse_kernel(pieces, shard, filt_ref, *refs):
    transform(filt_ref, refs[:-1], pieces, refs[-1], shard)


def inverse_cost(count, channels, width, atoms):
    return pl.CostEstimate(
        flops=2 * count * channels * width * atoms,
        bytes_accessed=2 * count * width * atoms,
        transcendentals=0,
    )


def used(tables, pieces):
    names = sorted({place[0] for places in pieces for place in places})
    moved = tuple(tuple((names.index(t), i, p) for t, i, p in places) for places in pieces)
    return [tables[t] for t in names], moved


def inverse_first(own, other, kfilt, after, tables, pieces, shard):
    count, channels, width = kfilt.shape
    tables, pieces = used(tables, pieces)
    atoms = shard * len(pieces)
    blocks = count // len(own)
    return pl.pallas_call(
        functools.partial(first_kernel, pieces, shard, len(own), blocks),
        in_specs=[VMEM] * (2 * len(own) + 1) + [ANY] + [VMEM] * len(tables),
        out_specs=[VMEM] * 2,
        out_shape=[
            jax.ShapeDtypeStruct((2 * count, channels, width), BF16),
            jax.ShapeDtypeStruct((channels, atoms), BF16),
        ],
        compiler_params=params(),
        cost_estimate=inverse_cost(2 * count, channels, width, atoms),
        name="first",
    )(*own, *other, kfilt, after, *tables)


def inverse(filt, tables, pieces, shard, dtype):
    count, channels, width = filt.shape
    tables, pieces = used(tables, pieces)
    atoms = shard * len(pieces)
    return pl.pallas_call(
        functools.partial(inverse_kernel, pieces, shard),
        in_specs=[VMEM] * (1 + len(tables)),
        out_specs=VMEM,
        out_shape=jax.ShapeDtypeStruct((channels, atoms), dtype),
        compiler_params=params(),
        cost_estimate=inverse_cost(count, channels, width, atoms),
        name="inverse",
    )(filt, *tables)


def join_kernel(here_ref, arrived_ref, own_ref, *send_refs):
    width = own_ref.shape[1]
    for p in range(len(send_refs) + 1):
        lanes = slice(p * width, (p + 1) * width)
        total = here_ref[:, lanes] + arrived_ref[:, lanes].astype(F32)
        if p:
            send_refs[p - 1][...] = total.astype(BF16)
        else:
            own_ref[...] = total


def join(here, arrived, pieces):
    channels, atoms = here.shape
    shape = (channels, atoms // pieces)
    return pl.pallas_call(
        join_kernel,
        in_specs=[VMEM] * 2,
        out_specs=[VMEM] * pieces,
        out_shape=[jax.ShapeDtypeStruct(shape, F32)]
        + [jax.ShapeDtypeStruct(shape, BF16)] * (pieces - 1),
        compiler_params=params(),
        name="join",
    )(here, arrived)


def pair_kernel(nbasis, pieces, output_scale, picks, arrays, own, neighbours_ref, own_pos_ref, *refs):
    message_refs, refs = refs[:arrays], refs[arrays:]
    weight_ref, _, out_ref, feat_scr, pos_scr, own_scr, basis_scr, near_scr, spot_scr, acc_scr = refs
    block = BLOCK_ATOMS
    both = 2 * block
    width = 12.0 / nbasis
    own_blocks, neighbours = neighbours_ref.shape
    shard = own_blocks * block
    channels = out_ref.shape[0]

    views = [
        message_refs[array] if index is None else message_refs[array].at[index]
        for array, index in picks
    ]
    for place, ref in enumerate(views):
        lanes = slice(place * shard, (place + 1) * shard)
        feat_scr[:, lanes] = ref[0:channels, :]
        parts = ref[channels:, :].astype(F32)
        pos_scr[0:3, lanes] = (parts[0:3] + parts[3:6] + parts[6:9]) * 8.0
    for d in range(3):
        row = own_pos_ref[d : d + 1, own * block : (own + 1) * block]
        own_scr[d] = jnp.broadcast_to(row, (both, block)).T

    a_index = lax.axis_index("atoms")
    k_index = lax.axis_index("kvec")
    n_atoms = lax.axis_size("atoms")
    group_blk = own_blocks * pieces
    first = (a_index * pieces + k_index) * own_blocks
    toward = jnp.where(a_index % 2 == 0, 1, n_atoms - 1)

    def divide(value, by):
        if by & (by - 1):
            return value // by, value % by
        return lax.shift_right_logical(value, by.bit_length() - 1), value & (by - 1)

    def place_of(ident):
        group, within = divide(ident, group_blk)
        ahead = divide(group - a_index + n_atoms, n_atoms)[1]
        which = jnp.where(ahead == 0, 0, jnp.where(ahead == toward, 1, 2))
        piece, rest = divide(within, own_blocks)
        return (which * pieces + (piece ^ k_index)) * own_blocks + rest

    rows = 16
    row_index = lax.broadcasted_iota(jnp.int32, (rows, both), 0)
    lane = lax.broadcasted_iota(jnp.int32, (1, both), 1)
    per_block = neighbours // 2
    log2e = math.log2(math.e)

    def unit(pair, carry):
        own_place = jnp.full((1, both), -1, jnp.int32)
        for h in range(2):
            ident = neighbours_ref[own, 2 * pair + h]
            lanes = pl.ds(pl.multiple_of(place_of(ident) * block, block), block)
            here = pl.ds(pl.multiple_of(pair * both + h * block, block), block)
            near_scr[:, here] = feat_scr[:, lanes]
            spot_scr[0:3, h * block : (h + 1) * block] = pos_scr[0:3, lanes]
            inside = (lane >= h * block) & (lane < (h + 1) * block) & (ident == first + own)
            own_place = jnp.where(inside, lane - h * block, own_place)
        lanes = pl.ds(pl.multiple_of(pair * both, both), both)
        for at in range(0, block, rows):
            dist2 = (own_scr[0, at : at + rows, :] - spot_scr[0:1, :]) ** 2
            dist2 += (own_scr[1, at : at + rows, :] - spot_scr[1:2, :]) ** 2
            dist2 += (own_scr[2, at : at + rows, :] - spot_scr[2:3, :]) ** 2
            radius = dist2 * lax.rsqrt(jnp.maximum(dist2, 1e-30))
            env = (16.0 * output_scale) / (16.0 + dist2)
            env = jnp.where(row_index + at == own_place, 0.0, env)
            v = radius * (log2e / width) - 0.5 * log2e
            value = jnp.exp2(v * v * (-0.5 / log2e)) * env
            ratio = jnp.exp2(v)
            for k in range(nbasis):
                if k:
                    value = value * ratio
                basis_scr[k * block + at : k * block + at + rows, lanes] = value.astype(BF16)
        return carry

    lax.fori_loop(0, per_block, unit, 0)
    acc_scr[...] = lax.dot_general(
        near_scr[...], basis_scr[...], (((1,), (1,)), ((), ())), preferred_element_type=F32
    )
    total = jnp.zeros((channels, block), F32)
    for n in range(nbasis):
        part = acc_scr[:, n * block : (n + 1) * block] * math.exp(-0.5 * n * n)
        total += lax.dot_general(
            weight_ref[n * channels : (n + 1) * channels, :],
            part.astype(BF16),
            (((0,), (0,)), ((), ())),
            preferred_element_type=F32,
        )
    out_ref[...] = total


def pair_message(own, neighbours, own_pos, arrays, picks, weight, after):
    channels = weight.shape[1]
    nbasis = weight.shape[0] // channels
    pieces = len(picks) // 3
    shard = own_pos.shape[1]
    count = neighbours.shape[1]
    scale = float(count * BLOCK_ATOMS) ** (-0.5)
    window = 3 * pieces * shard
    return pl.pallas_call(
        functools.partial(pair_kernel, nbasis, pieces, scale, picks, len(arrays), own),
        in_specs=[SMEM] + [VMEM] * (2 + len(arrays)) + [ANY],
        out_specs=VMEM,
        out_shape=jax.ShapeDtypeStruct((channels, BLOCK_ATOMS), F32),
        scratch_shapes=[
            pltpu.VMEM((channels, window), BF16),
            pltpu.VMEM((8, window), F32),
            pltpu.VMEM((3, BLOCK_ATOMS, 2 * BLOCK_ATOMS), F32),
            pltpu.VMEM((nbasis * BLOCK_ATOMS, count * BLOCK_ATOMS), BF16),
            pltpu.VMEM((channels, count * BLOCK_ATOMS), BF16),
            pltpu.VMEM((8, 2 * BLOCK_ATOMS), F32),
            pltpu.VMEM((channels, nbasis * BLOCK_ATOMS), F32),
        ],
        compiler_params=params(),
        cost_estimate=pl.CostEstimate(
            flops=2 * BLOCK_ATOMS * count * BLOCK_ATOMS * (nbasis * channels + 40),
            bytes_accessed=2 * window * channels,
            transcendentals=3 * BLOCK_ATOMS * count * BLOCK_ATOMS,
        ),
        name="pair",
    )(neighbours, own_pos, *arrays, weight, after)


def update_kernel(pairs, *refs):
    features_ref, gain_ref, w_in_ref, w_out_ref = refs[:4]
    pair_refs, parts, out_ref = refs[4 : 4 + pairs], refs[4 + pairs : -1], refs[-1]
    long_t = parts[0][...].astype(F32)
    for part in parts[1:]:
        long_t = long_t + part[...].astype(F32)
    pair_t = jnp.concatenate([ref[...] for ref in pair_refs], axis=1)
    total = features_ref[...].astype(F32) + (pair_t + long_t).T
    mean = jnp.mean(total * total, axis=-1, keepdims=True)
    normed = (total * lax.rsqrt(mean + 1e-06) * gain_ref[...]).astype(BF16)
    pre = jnp.dot(normed, w_in_ref[...], preferred_element_type=F32)
    hidden = (pre / (1.0 + jnp.exp(-pre))).astype(BF16)
    out_ref[...] = (
        total + jnp.dot(hidden, w_out_ref[...], preferred_element_type=F32)
    ).astype(BF16)


def update(features, pairs, gain, w_in, w_out, parts):
    return pl.pallas_call(
        functools.partial(update_kernel, len(pairs)),
        in_specs=[VMEM] * (4 + len(pairs) + len(parts)),
        out_specs=VMEM,
        out_shape=jax.ShapeDtypeStruct(features.shape, BF16),
        compiler_params=params(),
        name="update",
    )(features, gain[None, :], w_in, w_out, *pairs, *parts)


def swap(value, axis, bits):
    return lax.ppermute(value, axis, [(i, i ^ bits) for i in range(lax.axis_size(axis))])


def per_device(
    positions,
    features,
    atom_mask,
    neighbours,
    lattice,
    pair_weight,
    kfilter,
    norm_gain,
    w_in,
    w_out,
):
    shard, _ = features.shape
    n_atoms = lax.axis_size("atoms")
    n_kvec = lax.axis_size("kvec")
    far = n_atoms // 4
    count = lattice.shape[1] // (2 * far)
    width = 256 if count % 256 == 0 else count

    message, lattice, kfilter = pack(features, atom_mask, positions, lattice, kfilter)
    scale = float(n_atoms * n_kvec * shard * KW) ** (-0.5)
    waves, kfilt = setup(lattice, kfilter, far, width, scale)
    others = range(n_kvec - 1, 0, -1)
    zs = range(1, far)
    message_x = swap(message, "atoms", 1)
    near = {k: swap(message, "kvec", k) for k in others}
    distant = [swap(message, "atoms", 4 * z) for z in zs]
    blocks = waves.shape[0]
    tables, where = [], {}

    def keep(table, names):
        tables.append(table)
        for place, name in enumerate(names):
            where[name] = tuple((len(tables) - 1, j, place) for j in range(2 * blocks))

    table, total = wave(waves, [message, message_x], [(0, None), (1, None)], None)
    keep(table, [(0, 0, 0), (1, 0, 0)])
    near_own = collect([near[k] for k in others], [(i, None) for i in range(n_kvec - 1)], after=(total,))
    near_x = swap(near_own, "atoms", 1)
    names = [(0, 0, k) for k in others] + [(1, 0, k) for k in others]
    picks = [(core, i) for core in range(2) for i in range(n_kvec - 1)]
    table, total = wave(waves, [near_own], picks[:2], total)
    keep(table, names[:2])
    distant = collect(distant, [(z, None) for z in range(far - 1)], after=(total,))
    distant_x = swap(distant, "atoms", 1)
    relayed = {k: swap(distant, "kvec", k) for k in others}
    halo_pairs = [(a, (a + 1) % n_atoms if a % 2 else (a - 1) % n_atoms) for a in range(n_atoms)]
    group = [(0, None)] + [(1, n_kvec - 1 - k) for k in range(1, n_kvec)]
    halo = lax.ppermute(collect([message, near_own], group), "atoms", halo_pairs)
    table, total = wave(waves, [near_own, near_x], picks[2:], total)
    keep(table, names[2:])
    every = [(i, z) for i in range(n_kvec - 1) for z in range(far - 1)]
    far_own = collect([relayed[k] for k in others], every, after=(total,))
    far_x = swap(far_own, "atoms", 1)
    picks = [(0, z) for z in range(far - 1)] + [(1, i) for i in range(len(every))]
    spots = [(z, k) for k in (0, *others) for z in zs]
    table, total = wave(waves, [distant, far_own], picks, total)
    keep(table, [(0, *spot) for spot in spots])
    own_factors, other_factors, low = [], [], None
    for j in range(blocks):
        after = () if low is None else (low,)
        table, part, low = wave(
            waves, [distant_x, far_x], picks, total, subset=(j, 1), after=after, low=True
        )
        tables.append(table)
        own_factors.append(part)
        other_factors.append(swap(low, "atoms", 2))
    for place, spot in enumerate(spots):
        first = len(tables) - blocks
        where[1, *spot] = tuple((first + j, half, place) for half in range(2) for j in range(blocks))

    arrays = [message, message_x, near_own, near_x, halo]
    picks = [(0, None)] + [(2, n_kvec - 1 - k) for k in range(1, n_kvec)]
    picks += [(1, None)] + [(3, n_kvec - 1 - k) for k in range(1, n_kvec)]
    picks += [(4, k) for k in range(n_kvec)]
    pairs = []
    for b in range(neighbours.shape[0]):
        pairs.append(pair_message(b, neighbours, positions, arrays, tuple(picks), pair_weight, low))

    def runs(core, distances):
        return tuple(where[core, z, k] for k in range(n_kvec) for z in distances)

    filt, away_far = inverse_first(
        own_factors, other_factors, kfilt, pairs[0], tables, runs(1, zs), shard
    )
    crossed_far = swap(away_far, "atoms", 1)
    away_near = inverse(filt, tables, runs(1, (0,)), shard, BF16)
    crossed_near = swap(away_near, "atoms", 1)
    here_far = inverse(filt, tables, runs(0, zs), shard, F32)
    sum_far, *sends = join(here_far, crossed_far, n_kvec)
    for k in others:
        sum_far = sum_far + swap(sends[k - 1], "kvec", k).astype(F32)
    sum_far = sum_far.astype(BF16)
    here_near = inverse(filt, tables, runs(0, (0,)), shard, F32)
    own_near, *sends = join(here_near, crossed_near, n_kvec)
    parts = [own_near]
    for k in others:
        parts.append(swap(sends[k - 1], "kvec", k))
    for z in zs:
        parts.append(swap(sum_far[:, (z - 1) * shard : z * shard], "atoms", 4 * z))
    return update(features, pairs, norm_gain, w_in, w_out, parts)


def solution(mesh):
    return jax.shard_map(
        per_device,
        mesh=mesh,
        in_specs=(
            P(None, ("atoms", "kvec")),
            P(("atoms", "kvec"), None),
            P(("atoms", "kvec")),
            P(("atoms", "kvec"), None),
            P(None, "kvec"),
            P(),
            P(),
            P(),
            P(),
            P(),
        ),
        out_specs=P(("atoms", "kvec"), None),
        check_vma=False,
    )
```

```python
import functools
import math

import jax
import jax.numpy as jnp
from jax import lax
from jax.experimental import pallas as pl
from jax.experimental.pallas import tpu as pltpu
from jax.sharding import PartitionSpec as P

KW = 12288
BLOCK_ATOMS = 128
F32 = jnp.float32
BF16 = jnp.bfloat16

SIN_COEF = (4.442879586561992, -7.307818050390618, 3.5977887417720016, -0.7912382192058507)
SLACK = 1e-5
TAIL = 16


def params(mib=16):
    return pltpu.CompilerParams(vmem_limit_bytes=mib << 20)


SMEM = pl.BlockSpec(memory_space=pltpu.SMEM)
VMEM = pl.BlockSpec(memory_space=pltpu.VMEM)
ANY = pl.BlockSpec(memory_space=pl.ANY)


def horner(u, coef):
    acc = coef[-1] * u + coef[-2]
    for c in reversed(coef[:-2]):
        acc = acc * u + c
    return acc


def pack_kernel(*refs):
    features_hbm, mask_hbm, pos_hbm, lattice_hbm, kfilter_hbm = refs[:5]
    out_ref, lattice_ref, kfilter_ref, features_ref, mask_ref, pos_ref, scr, sems = refs[5:]
    copies = [
        pltpu.make_async_copy(source, target, sems.at[i])
        for i, (source, target) in enumerate(
            (
                (features_hbm, features_ref),
                (mask_hbm, mask_ref),
                (pos_hbm, pos_ref),
                (lattice_hbm, lattice_ref),
                (kfilter_hbm, kfilter_ref),
            )
        )
    ]
    for copy in copies:
        copy.start()
    for copy in copies:
        copy.wait()
    channels = features_ref.shape[1]
    mask = mask_ref[...].astype(F32)
    out_ref[0:channels, :] = (features_ref[...].astype(F32).T * mask).astype(BF16)
    value = pos_ref[...] * 0.125
    high = value.astype(BF16).astype(F32)
    rest = value - high
    mid = rest.astype(BF16).astype(F32)
    scr[...] = jnp.zeros_like(scr)
    scr[0:3, :] = high
    scr[3:6, :] = mid
    scr[6:9, :] = rest - mid
    out_ref[channels : channels + TAIL, :] = scr[...].astype(BF16)


def pack(features, mask, positions, lattice, kfilter):
    shard, channels = features.shape
    arrays = (features, mask[None, :], positions, lattice, kfilter)
    return pl.pallas_call(
        pack_kernel,
        in_specs=[pl.BlockSpec(memory_space=pltpu.HBM)] * 5,
        out_specs=[VMEM] * 3,
        out_shape=[
            jax.ShapeDtypeStruct((channels + TAIL, shard), BF16),
            jax.ShapeDtypeStruct(lattice.shape, lattice.dtype),
            jax.ShapeDtypeStruct(kfilter.shape, kfilter.dtype),
        ],
        scratch_shapes=[
            pltpu.VMEM((shard, channels), BF16),
            pltpu.VMEM((1, shard), jnp.int32),
            pltpu.VMEM((3, shard), F32),
            pltpu.VMEM((TAIL, shard), F32),
            pltpu.SemaphoreType.DMA((5,)),
        ],
        compiler_params=params(),
        name="pack",
    )(*(pltpu.with_memory_space_constraint(x, pltpu.HBM) for x in arrays))


def setup_kernel(far, nbasis, scale, lattice_ref, kfilter_ref, wave_ref, kfilt_ref, scr):
    blocks, width, _ = wave_ref.shape
    a_index = lax.axis_index("atoms")
    part = a_index % 2 + 2 * (a_index // 4)
    count = blocks * width
    kfilter = kfilter_ref[...].T
    for j in range(blocks):
        lattice = jnp.zeros((3, width), F32)
        for p in range(2 * far):
            at = p * count + j * width
            mine = (part == p).astype(F32)
            lattice += lattice_ref[:, at : at + width].astype(F32) * mine
        scr[...] = jnp.zeros_like(scr)
        for copy in range(3):
            scr[3 * copy : 3 * copy + 3, :] = lattice
        wave_ref[j] = scr[...].T.astype(BF16)
        wave = lattice * (2.0 * math.pi / 8.0)
        kmag = jnp.sqrt(
            wave[0:1] * wave[0:1] + wave[1:2] * wave[1:2] + wave[2:3] * wave[2:3]
        )
        total = jnp.zeros(kfilt_ref.shape[1:], F32)
        for p in range(nbasis):
            basis = jnp.exp(-0.5 * ((kmag - (p + 0.5) * (21.0 / nbasis)) / (21.0 / nbasis)) ** 2)
            total += kfilter[:, p : p + 1] * basis
        kfilt_ref[j] = total * scale


def setup(lattice, kfilter, far, width, scale):
    nbasis, channels = kfilter.shape
    blocks = lattice.shape[1] // (2 * far * width)
    return pl.pallas_call(
        functools.partial(setup_kernel, far, nbasis, scale),
        in_specs=[VMEM] * 2,
        out_specs=[VMEM] * 2,
        out_shape=[
            jax.ShapeDtypeStruct((blocks, width, TAIL), BF16),
            jax.ShapeDtypeStruct((blocks, channels, width), F32),
        ],
        scratch_shapes=[pltpu.VMEM((TAIL, width), F32)],
        compiler_params=params(),
        name="setup",
    )(lattice, kfilter)


def wave_kernel(picks, arrays, first, start, waits, low, *refs):
    refs = list(refs)
    take = lambda n: [refs.pop(0) for _ in range(n)]
    (lattice_ref,) = take(1)
    messages = take(arrays)
    before_ref = None if start else take(1)[0]
    take(waits)
    table_ref, total_ref = take(2)
    low_ref = take(1)[0] if low else None
    feat_scr, pos_scr = take(2)
    phases, buffers = take(2), take(2)
    blocks, width = table_ref.shape[0] // 2, table_ref.shape[1]
    every = lattice_ref.shape[0]
    pairs, channels, both = feat_scr.shape
    shard = both // 2
    for place, (array, index) in enumerate(picks):
        item = messages[array] if index is None else messages[array].at[index]
        lanes = slice(place % 2 * shard, (place % 2 + 1) * shard)
        feat_scr[place // 2, :, lanes] = item[0:channels, :]
        pos_scr[place // 2, :, lanes] = item[channels:, :]
    for j in range(2 * blocks):
        if start:
            total_ref[j] = jnp.zeros_like(total_ref[j])
        else:
            total_ref[j] = before_ref[j // blocks * every + first + j % blocks]
    buffers[1][...] = jnp.zeros_like(buffers[1])
    steps = pairs * blocks

    def phase(i, slot):
        i = jnp.minimum(i, steps - 1)
        phases[slot][...] = jnp.dot(
            lattice_ref[first + i % blocks], pos_scr[i // blocks], preferred_element_type=F32
        )

    def product(i, slot, half):
        pair, block = i // blocks, i % blocks
        total_ref[half * blocks + block] += lax.dot_general(
            feat_scr[pair], buffers[slot][half], (((1,), (1,)), ((), ())), preferred_element_type=F32
        )

    def unit(i, slot):
        pair, block = i // blocks, i % blocks
        before = jnp.maximum(i - 1, 0)
        lanes = pl.ds(pl.multiple_of(pair * both, both), both)
        rows = 16
        for n, at in enumerate(range(0, width, rows)):
            if n == 4:
                product(before, 1 - slot, 0)
            if n == 10:
                product(before, 1 - slot, 1)
            turns = phases[slot][at : at + rows, :]
            r = turns - jnp.round(turns)
            s = horner(r * r, SIN_COEF) * r
            square = s * s
            w = (2.0 + SLACK) - square
            cosine = (1.0 - square).astype(BF16)
            sine = (s * (w * lax.rsqrt(w))).astype(BF16)
            buffers[slot][0, at : at + rows, :] = cosine
            buffers[slot][1, at : at + rows, :] = sine
            table_ref[block, at : at + rows, lanes] = cosine
            table_ref[blocks + block, at : at + rows, lanes] = sine
        phase(i + 2, slot)

    phase(0, 0)
    phase(1, 1)

    def body(n, carry):
        unit(2 * n, 0)
        unit(2 * n + 1, 1)
        return carry

    lax.fori_loop(0, steps // 2, body, 0)
    if steps % 2:
        unit(steps - 1, 0)
    for half in range(2):
        product(steps - 1, (steps - 1) % 2, half)
    if low:
        low_ref[...] = total_ref[...].astype(BF16)


def wave(lattice, arrays, picks, before, subset=None, after=(), low=False):
    every, width, _ = lattice.shape
    first, blocks = subset or (0, every)
    pieces = len(picks)
    rows, shard = arrays[0].shape[-2:]
    channels = rows - TAIL
    args = [lattice, *arrays] + ([] if before is None else [before])
    factor = (2 * blocks, channels, width)
    shapes = [
        jax.ShapeDtypeStruct((2 * blocks, width, pieces * shard), BF16),
        jax.ShapeDtypeStruct(factor, F32),
    ]
    if low:
        shapes.append(jax.ShapeDtypeStruct(factor, BF16))
    pairs = blocks * width * pieces * shard
    return pl.pallas_call(
        functools.partial(
            wave_kernel, tuple(picks), len(arrays), first, before is None, len(after), low
        ),
        in_specs=[VMEM] * len(args) + [ANY] * len(after),
        out_specs=[VMEM] * len(shapes),
        out_shape=shapes,
        scratch_shapes=[
            pltpu.VMEM((pieces // 2, channels, 2 * shard), BF16),
            pltpu.VMEM((pieces // 2, TAIL, 2 * shard), BF16),
            pltpu.VMEM((width, 2 * shard), F32),
            pltpu.VMEM((width, 2 * shard), F32),
            pltpu.VMEM((2, width, 2 * shard), BF16),
            pltpu.VMEM((2, width, 2 * shard), BF16),
        ],
        compiler_params=params(),
        cost_estimate=pl.CostEstimate(
            flops=4 * pairs * channels, bytes_accessed=4 * pairs, transcendentals=pairs
        ),
        name="wave",
    )(*args, *after)


def collect_kernel(picks, *refs):
    for p, (array, index) in enumerate(picks):
        ref = refs[array]
        refs[-1][p] = ref[...] if index is None else ref[index]


def collect(arrays, picks, after=()):
    return pl.pallas_call(
        functools.partial(collect_kernel, picks),
        in_specs=[VMEM] * len(arrays) + [ANY] * len(after),
        out_specs=VMEM,
        out_shape=jax.ShapeDtypeStruct((len(picks), *arrays[0].shape[-2:]), BF16),
        compiler_params=params(),
        name="collect",
    )(*arrays, *after)


def transform(filt_ref, table_refs, pieces, out_ref, shard):
    for at, places in enumerate(pieces):
        acc = None
        for j, (table, index, place) in enumerate(places):
            part = jnp.dot(
                filt_ref[j],
                table_refs[table][index, :, place * shard : (place + 1) * shard],
                preferred_element_type=F32,
            )
            acc = part if acc is None else acc + part
        out_ref[:, at * shard : (at + 1) * shard] = acc.astype(out_ref.dtype)


def first_kernel(pieces, shard, parts, blocks, *refs):
    own_refs, other_refs, refs = refs[:parts], refs[parts : 2 * parts], refs[2 * parts :]
    kfilt_ref, table_refs, (filt_ref, out_ref) = refs[0], refs[2:-2], refs[-2:]
    count = kfilt_ref.shape[0]
    for half in range(2):
        for j in range(count):
            part, index = j // blocks, half * blocks + j % blocks
            total = own_refs[part][index] + other_refs[part][index].astype(F32)
            filt_ref[half * count + j] = (total * kfilt_ref[j]).astype(BF16)
    transform(filt_ref, table_refs, pieces, out_ref, shard)


def inverse_kernel(pieces, shard, filt_ref, *refs):
    transform(filt_ref, refs[:-1], pieces, refs[-1], shard)


def inverse_cost(count, channels, width, atoms):
    return pl.CostEstimate(
        flops=2 * count * channels * width * atoms,
        bytes_accessed=2 * count * width * atoms,
        transcendentals=0,
    )


def used(tables, pieces):
    names = sorted({place[0] for places in pieces for place in places})
    moved = tuple(tuple((names.index(t), i, p) for t, i, p in places) for places in pieces)
    return [tables[t] for t in names], moved


def inverse_first(own, other, kfilt, after, tables, pieces, shard):
    count, channels, width = kfilt.shape
    tables, pieces = used(tables, pieces)
    atoms = shard * len(pieces)
    blocks = count // len(own)
    return pl.pallas_call(
        functools.partial(first_kernel, pieces, shard, len(own), blocks),
        in_specs=[VMEM] * (2 * len(own) + 1) + [ANY] + [VMEM] * len(tables),
        out_specs=[VMEM] * 2,
        out_shape=[
            jax.ShapeDtypeStruct((2 * count, channels, width), BF16),
            jax.ShapeDtypeStruct((channels, atoms), BF16),
        ],
        compiler_params=params(),
        cost_estimate=inverse_cost(2 * count, channels, width, atoms),
        name="first",
    )(*own, *other, kfilt, after, *tables)


def inverse(filt, tables, pieces, shard, dtype):
    count, channels, width = filt.shape
    tables, pieces = used(tables, pieces)
    atoms = shard * len(pieces)
    return pl.pallas_call(
        functools.partial(inverse_kernel, pieces, shard),
        in_specs=[VMEM] * (1 + len(tables)),
        out_specs=VMEM,
        out_shape=jax.ShapeDtypeStruct((channels, atoms), dtype),
        compiler_params=params(),
        cost_estimate=inverse_cost(count, channels, width, atoms),
        name="inverse",
    )(filt, *tables)


def join_kernel(here_ref, arrived_ref, own_ref, *send_refs):
    width = own_ref.shape[1]
    for p in range(len(send_refs) + 1):
        lanes = slice(p * width, (p + 1) * width)
        total = here_ref[:, lanes] + arrived_ref[:, lanes].astype(F32)
        if p:
            send_refs[p - 1][...] = total.astype(BF16)
        else:
            own_ref[...] = total


def join(here, arrived, pieces):
    channels, atoms = here.shape
    shape = (channels, atoms // pieces)
    return pl.pallas_call(
        join_kernel,
        in_specs=[VMEM] * 2,
        out_specs=[VMEM] * pieces,
        out_shape=[jax.ShapeDtypeStruct(shape, F32)]
        + [jax.ShapeDtypeStruct(shape, BF16)] * (pieces - 1),
        compiler_params=params(),
        name="join",
    )(here, arrived)


def pair_kernel(nbasis, pieces, output_scale, picks, arrays, own, neighbours_ref, own_pos_ref, *refs):
    message_refs, refs = refs[:arrays], refs[arrays:]
    weight_ref, _, out_ref, feat_scr, pos_scr, own_scr, basis_scr, near_scr, spot_scr, acc_scr = refs
    block = BLOCK_ATOMS
    both = 2 * block
    width = 12.0 / nbasis
    own_blocks, neighbours = neighbours_ref.shape
    shard = own_blocks * block
    channels = out_ref.shape[0]

    views = [
        message_refs[array] if index is None else message_refs[array].at[index]
        for array, index in picks
    ]
    for place, ref in enumerate(views):
        lanes = slice(place * shard, (place + 1) * shard)
        feat_scr[:, lanes] = ref[0:channels, :]
        parts = ref[channels:, :].astype(F32)
        pos_scr[0:3, lanes] = (parts[0:3] + parts[3:6] + parts[6:9]) * 8.0
    for d in range(3):
        row = own_pos_ref[d : d + 1, own * block : (own + 1) * block]
        own_scr[d] = jnp.broadcast_to(row, (both, block)).T

    a_index = lax.axis_index("atoms")
    k_index = lax.axis_index("kvec")
    n_atoms = lax.axis_size("atoms")
    group_blk = own_blocks * pieces
    first = (a_index * pieces + k_index) * own_blocks
    toward = jnp.where(a_index % 2 == 0, 1, n_atoms - 1)

    def divide(value, by):
        if by & (by - 1):
            return value // by, value % by
        return lax.shift_right_logical(value, by.bit_length() - 1), value & (by - 1)

    def place_of(ident):
        group, within = divide(ident, group_blk)
        ahead = divide(group - a_index + n_atoms, n_atoms)[1]
        which = jnp.where(ahead == 0, 0, jnp.where(ahead == toward, 1, 2))
        piece, rest = divide(within, own_blocks)
        return (which * pieces + (piece ^ k_index)) * own_blocks + rest

    rows = 16
    row_index = lax.broadcasted_iota(jnp.int32, (rows, both), 0)
    lane = lax.broadcasted_iota(jnp.int32, (1, both), 1)
    per_block = neighbours // 2
    log2e = math.log2(math.e)

    def unit(pair, carry):
        own_place = jnp.full((1, both), -1, jnp.int32)
        for h in range(2):
            ident = neighbours_ref[own, 2 * pair + h]
            lanes = pl.ds(pl.multiple_of(place_of(ident) * block, block), block)
            here = pl.ds(pl.multiple_of(pair * both + h * block, block), block)
            near_scr[:, here] = feat_scr[:, lanes]
            spot_scr[0:3, h * block : (h + 1) * block] = pos_scr[0:3, lanes]
            inside = (lane >= h * block) & (lane < (h + 1) * block) & (ident == first + own)
            own_place = jnp.where(inside, lane - h * block, own_place)
        lanes = pl.ds(pl.multiple_of(pair * both, both), both)
        for at in range(0, block, rows):
            dist2 = (own_scr[0, at : at + rows, :] - spot_scr[0:1, :]) ** 2
            dist2 += (own_scr[1, at : at + rows, :] - spot_scr[1:2, :]) ** 2
            dist2 += (own_scr[2, at : at + rows, :] - spot_scr[2:3, :]) ** 2
            radius = dist2 * lax.rsqrt(jnp.maximum(dist2, 1e-30))
            env = (16.0 * output_scale) / (16.0 + dist2)
            env = jnp.where(row_index + at == own_place, 0.0, env)
            v = radius * (log2e / width) - 0.5 * log2e
            value = jnp.exp2(v * v * (-0.5 / log2e)) * env
            ratio = jnp.exp2(v)
            for k in range(nbasis):
                if k:
                    value = value * ratio
                basis_scr[k * block + at : k * block + at + rows, lanes] = value.astype(BF16)
        return carry

    lax.fori_loop(0, per_block, unit, 0)
    acc_scr[...] = lax.dot_general(
        near_scr[...], basis_scr[...], (((1,), (1,)), ((), ())), preferred_element_type=F32
    )
    total = jnp.zeros((channels, block), F32)
    for n in range(nbasis):
        part = acc_scr[:, n * block : (n + 1) * block] * math.exp(-0.5 * n * n)
        total += lax.dot_general(
            weight_ref[n * channels : (n + 1) * channels, :],
            part.astype(BF16),
            (((0,), (0,)), ((), ())),
            preferred_element_type=F32,
        )
    out_ref[...] = total


def pair_message(own, neighbours, own_pos, arrays, picks, weight, after):
    channels = weight.shape[1]
    nbasis = weight.shape[0] // channels
    pieces = len(picks) // 3
    shard = own_pos.shape[1]
    count = neighbours.shape[1]
    scale = float(count * BLOCK_ATOMS) ** (-0.5)
    window = 3 * pieces * shard
    return pl.pallas_call(
        functools.partial(pair_kernel, nbasis, pieces, scale, picks, len(arrays), own),
        in_specs=[SMEM] + [VMEM] * (2 + len(arrays)) + [ANY],
        out_specs=VMEM,
        out_shape=jax.ShapeDtypeStruct((channels, BLOCK_ATOMS), F32),
        scratch_shapes=[
            pltpu.VMEM((channels, window), BF16),
            pltpu.VMEM((8, window), F32),
            pltpu.VMEM((3, BLOCK_ATOMS, 2 * BLOCK_ATOMS), F32),
            pltpu.VMEM((nbasis * BLOCK_ATOMS, count * BLOCK_ATOMS), BF16),
            pltpu.VMEM((channels, count * BLOCK_ATOMS), BF16),
            pltpu.VMEM((8, 2 * BLOCK_ATOMS), F32),
            pltpu.VMEM((channels, nbasis * BLOCK_ATOMS), F32),
        ],
        compiler_params=params(),
        cost_estimate=pl.CostEstimate(
            flops=2 * BLOCK_ATOMS * count * BLOCK_ATOMS * (nbasis * channels + 40),
            bytes_accessed=2 * window * channels,
            transcendentals=3 * BLOCK_ATOMS * count * BLOCK_ATOMS,
        ),
        name="pair",
    )(neighbours, own_pos, *arrays, weight, after)


def update_kernel(pairs, *refs):
    features_ref, gain_ref, w_in_ref, w_out_ref = refs[:4]
    pair_refs, parts, out_ref = refs[4 : 4 + pairs], refs[4 + pairs : -1], refs[-1]
    long_t = parts[0][...].astype(F32)
    for part in parts[1:]:
        long_t = long_t + part[...].astype(F32)
    pair_t = jnp.concatenate([ref[...] for ref in pair_refs], axis=1)
    total = features_ref[...].astype(F32) + (pair_t + long_t).T
    mean = jnp.mean(total * total, axis=-1, keepdims=True)
    normed = (total * lax.rsqrt(mean + 1e-06) * gain_ref[...]).astype(BF16)
    pre = jnp.dot(normed, w_in_ref[...], preferred_element_type=F32)
    hidden = (pre / (1.0 + jnp.exp(-pre))).astype(BF16)
    out_ref[...] = (
        total + jnp.dot(hidden, w_out_ref[...], preferred_element_type=F32)
    ).astype(BF16)


def update(features, pairs, gain, w_in, w_out, parts):
    return pl.pallas_call(
        functools.partial(update_kernel, len(pairs)),
        in_specs=[VMEM] * (4 + len(pairs) + len(parts)),
        out_specs=VMEM,
        out_shape=jax.ShapeDtypeStruct(features.shape, BF16),
        compiler_params=params(),
        name="update",
    )(features, gain[None, :], w_in, w_out, *pairs, *parts)


def swap(value, axis, bits):
    return lax.ppermute(value, axis, [(i, i ^ bits) for i in range(lax.axis_size(axis))])


def per_device(
    positions,
    features,
    atom_mask,
    neighbours,
    lattice,
    pair_weight,
    kfilter,
    norm_gain,
    w_in,
    w_out,
):
    shard, _ = features.shape
    n_atoms = lax.axis_size("atoms")
    n_kvec = lax.axis_size("kvec")
    far = n_atoms // 4
    count = lattice.shape[1] // (2 * far)
    width = 256 if count % 256 == 0 else count

    message, lattice, kfilter = pack(features, atom_mask, positions, lattice, kfilter)
    scale = float(n_atoms * n_kvec * shard * KW) ** (-0.5)
    waves, kfilt = setup(lattice, kfilter, far, width, scale)
    others = range(n_kvec - 1, 0, -1)
    zs = range(1, far)
    message_x = swap(message, "atoms", 1)
    near = {k: swap(message, "kvec", k) for k in others}
    distant = [swap(message, "atoms", 4 * z) for z in zs]
    blocks = waves.shape[0]
    tables, where = [], {}

    def keep(table, names):
        tables.append(table)
        for place, name in enumerate(names):
            where[name] = tuple((len(tables) - 1, j, place) for j in range(2 * blocks))

    table, total = wave(waves, [message, message_x], [(0, None), (1, None)], None)
    keep(table, [(0, 0, 0), (1, 0, 0)])
    near_own = collect([near[k] for k in others], [(i, None) for i in range(n_kvec - 1)], after=(total,))
    near_x = swap(near_own, "atoms", 1)
    names = [(0, 0, k) for k in others] + [(1, 0, k) for k in others]
    picks = [(core, i) for core in range(2) for i in range(n_kvec - 1)]
    table, total = wave(waves, [near_own], picks[:2], total)
    keep(table, names[:2])
    distant = collect(distant, [(z, None) for z in range(far - 1)], after=(total,))
    distant_x = swap(distant, "atoms", 1)
    relayed = {k: swap(distant, "kvec", k) for k in others}
    halo_pairs = [(a, (a + 1) % n_atoms if a % 2 else (a - 1) % n_atoms) for a in range(n_atoms)]
    group = [(0, None)] + [(1, n_kvec - 1 - k) for k in range(1, n_kvec)]
    halo = lax.ppermute(collect([message, near_own], group), "atoms", halo_pairs)
    middle = 2 + (len(picks) - 2) // 4 * 2
    table, total = wave(waves, [near_own, near_x], picks[2:middle], total)
    keep(table, names[2:middle])
    every = [(i, z) for i in range(n_kvec - 1) for z in range(far - 1)]
    far_own = collect([relayed[k] for k in others], every, after=(total,))
    far_x = swap(far_own, "atoms", 1)
    table, total = wave(waves, [near_own, near_x], picks[middle:], total, after=(far_own,))
    keep(table, names[middle:])
    arrays = [distant, far_own, distant_x, far_x]
    picks = []
    for core in range(2):
        picks += [(2 * core, z) for z in range(far - 1)]
        picks += [(2 * core + 1, i) for i in range(len(every))]
    spots = [(core, z, k) for core in range(2) for k in (0, *others) for z in zs]
    own_factors, other_factors, low = [], [], None
    for j in range(blocks):
        after = () if low is None else (low,)
        table, part, low = wave(waves, arrays, picks, total, subset=(j, 1), after=after, low=True)
        tables.append(table)
        own_factors.append(part)
        other_factors.append(swap(low, "atoms", 2))
    for place, spot in enumerate(spots):
        first = len(tables) - blocks
        where[spot] = tuple((first + j, half, place) for half in range(2) for j in range(blocks))

    arrays = [message, message_x, near_own, near_x, halo]
    picks = [(0, None)] + [(2, n_kvec - 1 - k) for k in range(1, n_kvec)]
    picks += [(1, None)] + [(3, n_kvec - 1 - k) for k in range(1, n_kvec)]
    picks += [(4, k) for k in range(n_kvec)]
    pairs = []
    for b in range(neighbours.shape[0]):
        pairs.append(pair_message(b, neighbours, positions, arrays, tuple(picks), pair_weight, low))

    def runs(core, distances):
        return tuple(where[core, z, k] for k in range(n_kvec) for z in distances)

    filt, away_far = inverse_first(
        own_factors, other_factors, kfilt, pairs[0], tables, runs(1, zs), shard
    )
    crossed_far = swap(away_far, "atoms", 1)
    away_near = inverse(filt, tables, runs(1, (0,)), shard, BF16)
    crossed_near = swap(away_near, "atoms", 1)
    here_far = inverse(filt, tables, runs(0, zs), shard, F32)
    sum_far, *sends = join(here_far, crossed_far, n_kvec)
    for k in others:
        sum_far = sum_far + swap(sends[k - 1], "kvec", k).astype(F32)
    sum_far = sum_far.astype(BF16)
    here_near = inverse(filt, tables, runs(0, (0,)), shard, F32)
    own_near, *sends = join(here_near, crossed_near, n_kvec)
    parts = [own_near]
    for k in others:
        parts.append(swap(sends[k - 1], "kvec", k))
    for z in zs:
        parts.append(swap(sum_far[:, (z - 1) * shard : z * shard], "atoms", 4 * z))
    return update(features, pairs, norm_gain, w_in, w_out, parts)


def solution(mesh):
    return jax.shard_map(
        per_device,
        mesh=mesh,
        in_specs=(
            P(None, ("atoms", "kvec")),
            P(("atoms", "kvec"), None),
            P(("atoms", "kvec")),
            P(("atoms", "kvec"), None),
            P(None, "kvec"),
            P(),
            P(),
            P(),
            P(),
            P(),
        ),
        out_specs=P(("atoms", "kvec"), None),
        check_vma=False,
    )
```

```python
import functools
import math

import jax
import jax.numpy as jnp
from jax import lax
from jax.experimental import pallas as pl
from jax.experimental.pallas import tpu as pltpu
from jax.sharding import PartitionSpec as P

KW = 12288
BLOCK_ATOMS = 128
F32 = jnp.float32
BF16 = jnp.bfloat16

SIN_COEF = (4.442879586561992, -7.307818050390618, 3.5977887417720016, -0.7912382192058507)
SLACK = 1e-5
TAIL = 16


def params(mib=16):
    return pltpu.CompilerParams(vmem_limit_bytes=mib << 20)


SMEM = pl.BlockSpec(memory_space=pltpu.SMEM)
VMEM = pl.BlockSpec(memory_space=pltpu.VMEM)
ANY = pl.BlockSpec(memory_space=pl.ANY)


def horner(u, coef):
    acc = coef[-1] * u + coef[-2]
    for c in reversed(coef[:-2]):
        acc = acc * u + c
    return acc


def pack_kernel(*refs):
    features_hbm, mask_hbm, pos_hbm, lattice_hbm, kfilter_hbm = refs[:5]
    out_ref, lattice_ref, kfilter_ref, features_ref, mask_ref, pos_ref, scr, sems = refs[5:]
    copies = [
        pltpu.make_async_copy(source, target, sems.at[i])
        for i, (source, target) in enumerate(
            (
                (features_hbm, features_ref),
                (mask_hbm, mask_ref),
                (pos_hbm, pos_ref),
                (lattice_hbm, lattice_ref),
                (kfilter_hbm, kfilter_ref),
            )
        )
    ]
    for copy in copies:
        copy.start()
    for copy in copies:
        copy.wait()
    channels = features_ref.shape[1]
    mask = mask_ref[...].astype(F32)
    out_ref[0:channels, :] = (features_ref[...].astype(F32).T * mask).astype(BF16)
    value = pos_ref[...] * 0.125
    high = value.astype(BF16).astype(F32)
    rest = value - high
    mid = rest.astype(BF16).astype(F32)
    scr[...] = jnp.zeros_like(scr)
    scr[0:3, :] = high
    scr[3:6, :] = mid
    scr[6:9, :] = rest - mid
    out_ref[channels : channels + TAIL, :] = scr[...].astype(BF16)


def pack(features, mask, positions, lattice, kfilter):
    shard, channels = features.shape
    arrays = (features, mask[None, :], positions, lattice, kfilter)
    return pl.pallas_call(
        pack_kernel,
        in_specs=[pl.BlockSpec(memory_space=pltpu.HBM)] * 5,
        out_specs=[VMEM] * 3,
        out_shape=[
            jax.ShapeDtypeStruct((channels + TAIL, shard), BF16),
            jax.ShapeDtypeStruct(lattice.shape, lattice.dtype),
            jax.ShapeDtypeStruct(kfilter.shape, kfilter.dtype),
        ],
        scratch_shapes=[
            pltpu.VMEM((shard, channels), BF16),
            pltpu.VMEM((1, shard), jnp.int32),
            pltpu.VMEM((3, shard), F32),
            pltpu.VMEM((TAIL, shard), F32),
            pltpu.SemaphoreType.DMA((5,)),
        ],
        compiler_params=params(),
        name="pack",
    )(*(pltpu.with_memory_space_constraint(x, pltpu.HBM) for x in arrays))


def setup_kernel(far, nbasis, scale, lattice_ref, kfilter_ref, wave_ref, kfilt_ref, scr):
    blocks, width, _ = wave_ref.shape
    a_index = lax.axis_index("atoms")
    part = a_index % 2 + 2 * (a_index // 4)
    count = blocks * width
    kfilter = kfilter_ref[...].T
    for j in range(blocks):
        lattice = jnp.zeros((3, width), F32)
        for p in range(2 * far):
            at = p * count + j * width
            mine = (part == p).astype(F32)
            lattice += lattice_ref[:, at : at + width].astype(F32) * mine
        scr[...] = jnp.zeros_like(scr)
        for copy in range(3):
            scr[3 * copy : 3 * copy + 3, :] = lattice
        wave_ref[j] = scr[...].T.astype(BF16)
        wave = lattice * (2.0 * math.pi / 8.0)
        kmag = jnp.sqrt(
            wave[0:1] * wave[0:1] + wave[1:2] * wave[1:2] + wave[2:3] * wave[2:3]
        )
        total = jnp.zeros(kfilt_ref.shape[1:], F32)
        for p in range(nbasis):
            basis = jnp.exp(-0.5 * ((kmag - (p + 0.5) * (21.0 / nbasis)) / (21.0 / nbasis)) ** 2)
            total += kfilter[:, p : p + 1] * basis
        kfilt_ref[j] = total * scale


def setup(lattice, kfilter, far, width, scale):
    nbasis, channels = kfilter.shape
    blocks = lattice.shape[1] // (2 * far * width)
    return pl.pallas_call(
        functools.partial(setup_kernel, far, nbasis, scale),
        in_specs=[VMEM] * 2,
        out_specs=[VMEM] * 2,
        out_shape=[
            jax.ShapeDtypeStruct((blocks, width, TAIL), BF16),
            jax.ShapeDtypeStruct((blocks, channels, width), F32),
        ],
        scratch_shapes=[pltpu.VMEM((TAIL, width), F32)],
        compiler_params=params(),
        name="setup",
    )(lattice, kfilter)


def wave_kernel(picks, arrays, first, start, waits, low, *refs):
    refs = list(refs)
    take = lambda n: [refs.pop(0) for _ in range(n)]
    (lattice_ref,) = take(1)
    messages = take(arrays)
    before_ref = None if start else take(1)[0]
    take(waits)
    table_ref, total_ref = take(2)
    low_ref = take(1)[0] if low else None
    feat_scr, pos_scr = take(2)
    phases, buffers = take(2), take(2)
    blocks, width = table_ref.shape[0] // 2, table_ref.shape[1]
    every = lattice_ref.shape[0]
    pairs, channels, both = feat_scr.shape
    shard = both // 2
    for place, (array, index) in enumerate(picks):
        item = messages[array] if index is None else messages[array].at[index]
        lanes = slice(place % 2 * shard, (place % 2 + 1) * shard)
        feat_scr[place // 2, :, lanes] = item[0:channels, :]
        pos_scr[place // 2, :, lanes] = item[channels:, :]
    for j in range(2 * blocks):
        if start:
            total_ref[j] = jnp.zeros_like(total_ref[j])
        else:
            total_ref[j] = before_ref[j // blocks * every + first + j % blocks]
    buffers[1][...] = jnp.zeros_like(buffers[1])
    steps = pairs * blocks

    def phase(i, slot):
        i = jnp.minimum(i, steps - 1)
        phases[slot][...] = jnp.dot(
            lattice_ref[first + i % blocks], pos_scr[i // blocks], preferred_element_type=F32
        )

    def product(i, slot, half):
        pair, block = i // blocks, i % blocks
        total_ref[half * blocks + block] += lax.dot_general(
            feat_scr[pair], buffers[slot][half], (((1,), (1,)), ((), ())), preferred_element_type=F32
        )

    def unit(i, slot):
        pair, block = i // blocks, i % blocks
        before = jnp.maximum(i - 1, 0)
        lanes = pl.ds(pl.multiple_of(pair * both, both), both)
        rows = 16
        for n, at in enumerate(range(0, width, rows)):
            if n == 4:
                product(before, 1 - slot, 0)
            if n == 10:
                product(before, 1 - slot, 1)
            turns = phases[slot][at : at + rows, :]
            r = turns - jnp.round(turns)
            s = horner(r * r, SIN_COEF) * r
            square = s * s
            w = (2.0 + SLACK) - square
            cosine = (1.0 - square).astype(BF16)
            sine = (s * (w * lax.rsqrt(w))).astype(BF16)
            buffers[slot][0, at : at + rows, :] = cosine
            buffers[slot][1, at : at + rows, :] = sine
            table_ref[block, at : at + rows, lanes] = cosine
            table_ref[blocks + block, at : at + rows, lanes] = sine
        phase(i + 2, slot)

    phase(0, 0)
    phase(1, 1)

    def body(n, carry):
        unit(2 * n, 0)
        unit(2 * n + 1, 1)
        return carry

    lax.fori_loop(0, steps // 2, body, 0)
    if steps % 2:
        unit(steps - 1, 0)
    for half in range(2):
        product(steps - 1, (steps - 1) % 2, half)
    if low:
        low_ref[...] = total_ref[...].astype(BF16)


def wave(lattice, arrays, picks, before, subset=None, after=(), low=False):
    every, width, _ = lattice.shape
    first, blocks = subset or (0, every)
    pieces = len(picks)
    rows, shard = arrays[0].shape[-2:]
    channels = rows - TAIL
    args = [lattice, *arrays] + ([] if before is None else [before])
    factor = (2 * blocks, channels, width)
    shapes = [
        jax.ShapeDtypeStruct((2 * blocks, width, pieces * shard), BF16),
        jax.ShapeDtypeStruct(factor, F32),
    ]
    if low:
        shapes.append(jax.ShapeDtypeStruct(factor, BF16))
    pairs = blocks * width * pieces * shard
    return pl.pallas_call(
        functools.partial(
            wave_kernel, tuple(picks), len(arrays), first, before is None, len(after), low
        ),
        in_specs=[VMEM] * len(args) + [ANY] * len(after),
        out_specs=[VMEM] * len(shapes),
        out_shape=shapes,
        scratch_shapes=[
            pltpu.VMEM((pieces // 2, channels, 2 * shard), BF16),
            pltpu.VMEM((pieces // 2, TAIL, 2 * shard), BF16),
            pltpu.VMEM((width, 2 * shard), F32),
            pltpu.VMEM((width, 2 * shard), F32),
            pltpu.VMEM((2, width, 2 * shard), BF16),
            pltpu.VMEM((2, width, 2 * shard), BF16),
        ],
        compiler_params=params(),
        cost_estimate=pl.CostEstimate(
            flops=4 * pairs * channels, bytes_accessed=4 * pairs, transcendentals=pairs
        ),
        name="wave",
    )(*args, *after)


def collect_kernel(picks, *refs):
    for p, (array, index) in enumerate(picks):
        ref = refs[array]
        refs[-1][p] = ref[...] if index is None else ref[index]


def collect(arrays, picks, after=()):
    return pl.pallas_call(
        functools.partial(collect_kernel, picks),
        in_specs=[VMEM] * len(arrays) + [ANY] * len(after),
        out_specs=VMEM,
        out_shape=jax.ShapeDtypeStruct((len(picks), *arrays[0].shape[-2:]), BF16),
        compiler_params=params(),
        name="collect",
    )(*arrays, *after)


def transform(filt_ref, table_refs, pieces, out_ref, shard):
    for at, places in enumerate(pieces):
        acc = None
        for j, (table, index, place) in enumerate(places):
            part = jnp.dot(
                filt_ref[j],
                table_refs[table][index, :, place * shard : (place + 1) * shard],
                preferred_element_type=F32,
            )
            acc = part if acc is None else acc + part
        out_ref[:, at * shard : (at + 1) * shard] = acc.astype(out_ref.dtype)


def first_kernel(pieces, shard, parts, blocks, *refs):
    own_refs, other_refs, refs = refs[:parts], refs[parts : 2 * parts], refs[2 * parts :]
    kfilt_ref, table_refs, (filt_ref, out_ref) = refs[0], refs[2:-2], refs[-2:]
    count = kfilt_ref.shape[0]
    for half in range(2):
        for j in range(count):
            part, index = j // blocks, half * blocks + j % blocks
            total = own_refs[part][index] + other_refs[part][index].astype(F32)
            filt_ref[half * count + j] = (total * kfilt_ref[j]).astype(BF16)
    transform(filt_ref, table_refs, pieces, out_ref, shard)


def inverse_kernel(pieces, shard, filt_ref, *refs):
    transform(filt_ref, refs[:-1], pieces, refs[-1], shard)


def inverse_cost(count, channels, width, atoms):
    return pl.CostEstimate(
        flops=2 * count * channels * width * atoms,
        bytes_accessed=2 * count * width * atoms,
        transcendentals=0,
    )


def used(tables, pieces):
    names = sorted({place[0] for places in pieces for place in places})
    moved = tuple(tuple((names.index(t), i, p) for t, i, p in places) for places in pieces)
    return [tables[t] for t in names], moved


def inverse_first(own, other, kfilt, after, tables, pieces, shard):
    count, channels, width = kfilt.shape
    tables, pieces = used(tables, pieces)
    atoms = shard * len(pieces)
    blocks = count // len(own)
    return pl.pallas_call(
        functools.partial(first_kernel, pieces, shard, len(own), blocks),
        in_specs=[VMEM] * (2 * len(own) + 1) + [ANY] + [VMEM] * len(tables),
        out_specs=[VMEM] * 2,
        out_shape=[
            jax.ShapeDtypeStruct((2 * count, channels, width), BF16),
            jax.ShapeDtypeStruct((channels, atoms), BF16),
        ],
        compiler_params=params(),
        cost_estimate=inverse_cost(2 * count, channels, width, atoms),
        name="first",
    )(*own, *other, kfilt, after, *tables)


def inverse(filt, tables, pieces, shard, dtype):
    count, channels, width = filt.shape
    tables, pieces = used(tables, pieces)
    atoms = shard * len(pieces)
    return pl.pallas_call(
        functools.partial(inverse_kernel, pieces, shard),
        in_specs=[VMEM] * (1 + len(tables)),
        out_specs=VMEM,
        out_shape=jax.ShapeDtypeStruct((channels, atoms), dtype),
        compiler_params=params(),
        cost_estimate=inverse_cost(count, channels, width, atoms),
        name="inverse",
    )(filt, *tables)


def join_kernel(here_ref, arrived_ref, own_ref, *send_refs):
    width = own_ref.shape[1]
    for p in range(len(send_refs) + 1):
        lanes = slice(p * width, (p + 1) * width)
        total = here_ref[:, lanes] + arrived_ref[:, lanes].astype(F32)
        if p:
            send_refs[p - 1][...] = total.astype(BF16)
        else:
            own_ref[...] = total


def join(here, arrived, pieces):
    channels, atoms = here.shape
    shape = (channels, atoms // pieces)
    return pl.pallas_call(
        join_kernel,
        in_specs=[VMEM] * 2,
        out_specs=[VMEM] * pieces,
        out_shape=[jax.ShapeDtypeStruct(shape, F32)]
        + [jax.ShapeDtypeStruct(shape, BF16)] * (pieces - 1),
        compiler_params=params(),
        name="join",
    )(here, arrived)


def pair_kernel(nbasis, pieces, output_scale, picks, arrays, own, neighbours_ref, own_pos_ref, *refs):
    message_refs, refs = refs[:arrays], refs[arrays:]
    weight_ref, _, out_ref, feat_scr, pos_scr, own_scr, basis_scr, near_scr, spot_scr, acc_scr = refs
    block = BLOCK_ATOMS
    both = 2 * block
    width = 12.0 / nbasis
    own_blocks, neighbours = neighbours_ref.shape
    shard = own_blocks * block
    channels = out_ref.shape[0]

    views = [
        message_refs[array] if index is None else message_refs[array].at[index]
        for array, index in picks
    ]
    for place, ref in enumerate(views):
        lanes = slice(place * shard, (place + 1) * shard)
        feat_scr[:, lanes] = ref[0:channels, :]
        parts = ref[channels:, :].astype(F32)
        pos_scr[0:3, lanes] = (parts[0:3] + parts[3:6] + parts[6:9]) * 8.0
    for d in range(3):
        row = own_pos_ref[d : d + 1, own * block : (own + 1) * block]
        own_scr[d] = jnp.broadcast_to(row, (both, block)).T

    a_index = lax.axis_index("atoms")
    k_index = lax.axis_index("kvec")
    n_atoms = lax.axis_size("atoms")
    group_blk = own_blocks * pieces
    first = (a_index * pieces + k_index) * own_blocks
    toward = jnp.where(a_index % 2 == 0, 1, n_atoms - 1)

    def divide(value, by):
        if by & (by - 1):
            return value // by, value % by
        return lax.shift_right_logical(value, by.bit_length() - 1), value & (by - 1)

    def place_of(ident):
        group, within = divide(ident, group_blk)
        ahead = divide(group - a_index + n_atoms, n_atoms)[1]
        which = jnp.where(ahead == 0, 0, jnp.where(ahead == toward, 1, 2))
        piece, rest = divide(within, own_blocks)
        return (which * pieces + (piece ^ k_index)) * own_blocks + rest

    rows = 16
    row_index = lax.broadcasted_iota(jnp.int32, (rows, both), 0)
    lane = lax.broadcasted_iota(jnp.int32, (1, both), 1)
    per_block = neighbours // 2
    log2e = math.log2(math.e)

    def unit(pair, carry):
        own_place = jnp.full((1, both), -1, jnp.int32)
        for h in range(2):
            ident = neighbours_ref[own, 2 * pair + h]
            lanes = pl.ds(pl.multiple_of(place_of(ident) * block, block), block)
            here = pl.ds(pl.multiple_of(pair * both + h * block, block), block)
            near_scr[:, here] = feat_scr[:, lanes]
            spot_scr[0:3, h * block : (h + 1) * block] = pos_scr[0:3, lanes]
            inside = (lane >= h * block) & (lane < (h + 1) * block) & (ident == first + own)
            own_place = jnp.where(inside, lane - h * block, own_place)
        lanes = pl.ds(pl.multiple_of(pair * both, both), both)
        for at in range(0, block, rows):
            dist2 = (own_scr[0, at : at + rows, :] - spot_scr[0:1, :]) ** 2
            dist2 += (own_scr[1, at : at + rows, :] - spot_scr[1:2, :]) ** 2
            dist2 += (own_scr[2, at : at + rows, :] - spot_scr[2:3, :]) ** 2
            radius = dist2 * lax.rsqrt(jnp.maximum(dist2, 1e-30))
            env = (16.0 * output_scale) / (16.0 + dist2)
            env = jnp.where(row_index + at == own_place, 0.0, env)
            v = radius * (log2e / width) - 0.5 * log2e
            value = jnp.exp2(v * v * (-0.5 / log2e)) * env
            ratio = jnp.exp2(v)
            for k in range(nbasis):
                if k:
                    value = value * ratio
                basis_scr[k * block + at : k * block + at + rows, lanes] = value.astype(BF16)
        return carry

    lax.fori_loop(0, per_block, unit, 0)
    acc_scr[...] = lax.dot_general(
        near_scr[...], basis_scr[...], (((1,), (1,)), ((), ())), preferred_element_type=F32
    )
    total = jnp.zeros((channels, block), F32)
    for n in range(nbasis):
        part = acc_scr[:, n * block : (n + 1) * block] * math.exp(-0.5 * n * n)
        total += lax.dot_general(
            weight_ref[n * channels : (n + 1) * channels, :],
            part.astype(BF16),
            (((0,), (0,)), ((), ())),
            preferred_element_type=F32,
        )
    out_ref[...] = total


def pair_message(own, neighbours, own_pos, arrays, picks, weight, after):
    channels = weight.shape[1]
    nbasis = weight.shape[0] // channels
    pieces = len(picks) // 3
    shard = own_pos.shape[1]
    count = neighbours.shape[1]
    scale = float(count * BLOCK_ATOMS) ** (-0.5)
    window = 3 * pieces * shard
    return pl.pallas_call(
        functools.partial(pair_kernel, nbasis, pieces, scale, picks, len(arrays), own),
        in_specs=[SMEM] + [VMEM] * (2 + len(arrays)) + [ANY],
        out_specs=VMEM,
        out_shape=jax.ShapeDtypeStruct((channels, BLOCK_ATOMS), F32),
        scratch_shapes=[
            pltpu.VMEM((channels, window), BF16),
            pltpu.VMEM((8, window), F32),
            pltpu.VMEM((3, BLOCK_ATOMS, 2 * BLOCK_ATOMS), F32),
            pltpu.VMEM((nbasis * BLOCK_ATOMS, count * BLOCK_ATOMS), BF16),
            pltpu.VMEM((channels, count * BLOCK_ATOMS), BF16),
            pltpu.VMEM((8, 2 * BLOCK_ATOMS), F32),
            pltpu.VMEM((channels, nbasis * BLOCK_ATOMS), F32),
        ],
        compiler_params=params(),
        cost_estimate=pl.CostEstimate(
            flops=2 * BLOCK_ATOMS * count * BLOCK_ATOMS * (nbasis * channels + 40),
            bytes_accessed=2 * window * channels,
            transcendentals=3 * BLOCK_ATOMS * count * BLOCK_ATOMS,
        ),
        name="pair",
    )(neighbours, own_pos, *arrays, weight, after)


def update_kernel(pairs, *refs):
    features_ref, gain_ref, w_in_ref, w_out_ref = refs[:4]
    pair_refs, parts, out_ref = refs[4 : 4 + pairs], refs[4 + pairs : -1], refs[-1]
    long_t = parts[0][...].astype(F32)
    for part in parts[1:]:
        long_t = long_t + part[...].astype(F32)
    pair_t = jnp.concatenate([ref[...] for ref in pair_refs], axis=1)
    total = features_ref[...].astype(F32) + (pair_t + long_t).T
    mean = jnp.mean(total * total, axis=-1, keepdims=True)
    normed = (total * lax.rsqrt(mean + 1e-06) * gain_ref[...]).astype(BF16)
    pre = jnp.dot(normed, w_in_ref[...], preferred_element_type=F32)
    hidden = (pre / (1.0 + jnp.exp(-pre))).astype(BF16)
    out_ref[...] = (
        total + jnp.dot(hidden, w_out_ref[...], preferred_element_type=F32)
    ).astype(BF16)


def update(features, pairs, gain, w_in, w_out, parts):
    return pl.pallas_call(
        functools.partial(update_kernel, len(pairs)),
        in_specs=[VMEM] * (4 + len(pairs) + len(parts)),
        out_specs=VMEM,
        out_shape=jax.ShapeDtypeStruct(features.shape, BF16),
        compiler_params=params(),
        name="update",
    )(features, gain[None, :], w_in, w_out, *pairs, *parts)


def swap(value, axis, bits):
    return lax.ppermute(value, axis, [(i, i ^ bits) for i in range(lax.axis_size(axis))])


def per_device(
    positions,
    features,
    atom_mask,
    neighbours,
    lattice,
    pair_weight,
    kfilter,
    norm_gain,
    w_in,
    w_out,
):
    shard, _ = features.shape
    n_atoms = lax.axis_size("atoms")
    n_kvec = lax.axis_size("kvec")
    far = n_atoms // 4
    count = lattice.shape[1] // (2 * far)
    width = 256 if count % 256 == 0 else count

    message, lattice, kfilter = pack(features, atom_mask, positions, lattice, kfilter)
    scale = float(n_atoms * n_kvec * shard * KW) ** (-0.5)
    waves, kfilt = setup(lattice, kfilter, far, width, scale)
    others = range(n_kvec - 1, 0, -1)
    zs = range(1, far)
    message_x = swap(message, "atoms", 1)
    near = {k: swap(message, "kvec", k) for k in others}
    distant = [swap(message, "atoms", 4 * z) for z in zs]
    blocks = waves.shape[0]
    tables, where = [], {}

    def keep(table, names):
        tables.append(table)
        for place, name in enumerate(names):
            where[name] = tuple((len(tables) - 1, j, place) for j in range(2 * blocks))

    near_own = collect(
        [near[k] for k in others], [(i, None) for i in range(n_kvec - 1)], after=(waves,)
    )
    near_x = swap(near_own, "atoms", 1)
    names = [(0, 0, k) for k in others] + [(1, 0, k) for k in others]
    picks = [(core, i) for core in range(2) for i in range(n_kvec - 1)]
    start = [(0, None), (1, None)] + [(2, index) for _, index in picks[:2]]
    table, total = wave(waves, [message, message_x, near_own], start, None)
    keep(table, [(0, 0, 0), (1, 0, 0)] + names[:2])
    distant = collect(distant, [(z, None) for z in range(far - 1)], after=(total,))
    relayed = {k: swap(distant, "kvec", k) for k in others}
    halo_pairs = [(a, (a + 1) % n_atoms if a % 2 else (a - 1) % n_atoms) for a in range(n_atoms)]
    group = [(0, None)] + [(1, n_kvec - 1 - k) for k in range(1, n_kvec)]
    halo = lax.ppermute(collect([message, near_own], group), "atoms", halo_pairs)
    middle = 2 + (len(picks) - 2) // 4 * 2
    table, total = wave(waves, [near_own, near_x], picks[2:middle], total)
    keep(table, names[2:middle])
    every = [(i, z) for i in range(n_kvec) for z in range(far - 1)]
    far_own = collect([distant, *[relayed[k] for k in others]], every, after=(total,))
    far_x = swap(far_own, "atoms", 1)
    table, total = wave(waves, [near_own, near_x], picks[middle:], total, after=(far_own,))
    keep(table, names[middle:])
    arrays = [far_own, far_x]
    picks = [(core, i) for core in range(2) for i in range(len(every))]
    spots = [(core, z, k) for core in range(2) for k in (0, *others) for z in zs]
    own_factors, other_factors, low = [], [], None
    for j in range(blocks):
        after = () if low is None else (low,)
        table, part, low = wave(waves, arrays, picks, total, subset=(j, 1), after=after, low=True)
        tables.append(table)
        own_factors.append(part)
        other_factors.append(swap(low, "atoms", 2))
    for place, spot in enumerate(spots):
        first = len(tables) - blocks
        where[spot] = tuple((first + j, half, place) for half in range(2) for j in range(blocks))

    arrays = [message, message_x, near_own, near_x, halo]
    picks = [(0, None)] + [(2, n_kvec - 1 - k) for k in range(1, n_kvec)]
    picks += [(1, None)] + [(3, n_kvec - 1 - k) for k in range(1, n_kvec)]
    picks += [(4, k) for k in range(n_kvec)]
    pairs = []
    for b in range(neighbours.shape[0]):
        pairs.append(pair_message(b, neighbours, positions, arrays, tuple(picks), pair_weight, low))

    def runs(core, distances):
        return tuple(where[core, z, k] for k in range(n_kvec) for z in distances)

    filt, away_far = inverse_first(
        own_factors, other_factors, kfilt, pairs[0], tables, runs(1, zs), shard
    )
    crossed_far = swap(away_far, "atoms", 1)
    away_near = inverse(filt, tables, runs(1, (0,)), shard, BF16)
    crossed_near = swap(away_near, "atoms", 1)
    here_far = inverse(filt, tables, runs(0, zs), shard, F32)
    sum_far, *sends = join(here_far, crossed_far, n_kvec)
    for k in others:
        sum_far = sum_far + swap(sends[k - 1], "kvec", k).astype(F32)
    sum_far = sum_far.astype(BF16)
    here_near = inverse(filt, tables, runs(0, (0,)), shard, F32)
    own_near, *sends = join(here_near, crossed_near, n_kvec)
    parts = [own_near]
    for k in others:
        parts.append(swap(sends[k - 1], "kvec", k))
    for z in zs:
        parts.append(swap(sum_far[:, (z - 1) * shard : z * shard], "atoms", 4 * z))
    return update(features, pairs, norm_gain, w_in, w_out, parts)


def solution(mesh):
    return jax.shard_map(
        per_device,
        mesh=mesh,
        in_specs=(
            P(None, ("atoms", "kvec")),
            P(("atoms", "kvec"), None),
            P(("atoms", "kvec")),
            P(("atoms", "kvec"), None),
            P(None, "kvec"),
            P(),
            P(),
            P(),
            P(),
            P(),
        ),
        out_specs=P(("atoms", "kvec"), None),
        check_vma=False,
    )
```

```python
import functools
import math

import jax
import jax.numpy as jnp
from jax import lax
from jax.experimental import pallas as pl
from jax.experimental.pallas import tpu as pltpu
from jax.sharding import PartitionSpec as P

KW = 12288
BLOCK_ATOMS = 128
F32 = jnp.float32
BF16 = jnp.bfloat16

SIN_COEF = (4.442879586561992, -7.307818050390618, 3.5977887417720016, -0.7912382192058507)
SLACK = 1e-5
TAIL = 16


def params(mib=16):
    return pltpu.CompilerParams(vmem_limit_bytes=mib << 20)


SMEM = pl.BlockSpec(memory_space=pltpu.SMEM)
VMEM = pl.BlockSpec(memory_space=pltpu.VMEM)
ANY = pl.BlockSpec(memory_space=pl.ANY)


def horner(u, coef):
    acc = coef[-1] * u + coef[-2]
    for c in reversed(coef[:-2]):
        acc = acc * u + c
    return acc


def pack_kernel(*refs):
    features_hbm, mask_hbm, pos_hbm, lattice_hbm, kfilter_hbm = refs[:5]
    out_ref, lattice_ref, kfilter_ref, features_ref, mask_ref, pos_ref, scr, sems = refs[5:]
    copies = [
        pltpu.make_async_copy(source, target, sems.at[i])
        for i, (source, target) in enumerate(
            (
                (features_hbm, features_ref),
                (mask_hbm, mask_ref),
                (pos_hbm, pos_ref),
                (lattice_hbm, lattice_ref),
                (kfilter_hbm, kfilter_ref),
            )
        )
    ]
    for copy in copies:
        copy.start()
    for copy in copies:
        copy.wait()
    channels = features_ref.shape[1]
    mask = mask_ref[...].astype(F32)
    out_ref[0:channels, :] = (features_ref[...].astype(F32).T * mask).astype(BF16)
    value = pos_ref[...] * 0.125
    high = value.astype(BF16).astype(F32)
    rest = value - high
    mid = rest.astype(BF16).astype(F32)
    scr[...] = jnp.zeros_like(scr)
    scr[0:3, :] = high
    scr[3:6, :] = mid
    scr[6:9, :] = rest - mid
    out_ref[channels : channels + TAIL, :] = scr[...].astype(BF16)


def pack(features, mask, positions, lattice, kfilter):
    shard, channels = features.shape
    arrays = (features, mask[None, :], positions, lattice, kfilter)
    return pl.pallas_call(
        pack_kernel,
        in_specs=[pl.BlockSpec(memory_space=pltpu.HBM)] * 5,
        out_specs=[VMEM] * 3,
        out_shape=[
            jax.ShapeDtypeStruct((channels + TAIL, shard), BF16),
            jax.ShapeDtypeStruct(lattice.shape, lattice.dtype),
            jax.ShapeDtypeStruct(kfilter.shape, kfilter.dtype),
        ],
        scratch_shapes=[
            pltpu.VMEM((shard, channels), BF16),
            pltpu.VMEM((1, shard), jnp.int32),
            pltpu.VMEM((3, shard), F32),
            pltpu.VMEM((TAIL, shard), F32),
            pltpu.SemaphoreType.DMA((5,)),
        ],
        compiler_params=params(),
        name="pack",
    )(*(pltpu.with_memory_space_constraint(x, pltpu.HBM) for x in arrays))


def setup_kernel(far, nbasis, scale, lattice_ref, kfilter_ref, wave_ref, kfilt_ref, scr):
    blocks, width, _ = wave_ref.shape
    a_index = lax.axis_index("atoms")
    part = a_index % 2 + 2 * (a_index // 4)
    count = blocks * width
    kfilter = kfilter_ref[...].T
    for j in range(blocks):
        lattice = jnp.zeros((3, width), F32)
        for p in range(2 * far):
            at = p * count + j * width
            mine = (part == p).astype(F32)
            lattice += lattice_ref[:, at : at + width].astype(F32) * mine
        scr[...] = jnp.zeros_like(scr)
        for copy in range(3):
            scr[3 * copy : 3 * copy + 3, :] = lattice
        wave_ref[j] = scr[...].T.astype(BF16)
        wave = lattice * (2.0 * math.pi / 8.0)
        kmag = jnp.sqrt(
            wave[0:1] * wave[0:1] + wave[1:2] * wave[1:2] + wave[2:3] * wave[2:3]
        )
        total = jnp.zeros(kfilt_ref.shape[1:], F32)
        for p in range(nbasis):
            basis = jnp.exp(-0.5 * ((kmag - (p + 0.5) * (21.0 / nbasis)) / (21.0 / nbasis)) ** 2)
            total += kfilter[:, p : p + 1] * basis
        kfilt_ref[j] = total * scale


def setup(lattice, kfilter, far, width, scale):
    nbasis, channels = kfilter.shape
    blocks = lattice.shape[1] // (2 * far * width)
    return pl.pallas_call(
        functools.partial(setup_kernel, far, nbasis, scale),
        in_specs=[VMEM] * 2,
        out_specs=[VMEM] * 2,
        out_shape=[
            jax.ShapeDtypeStruct((blocks, width, TAIL), BF16),
            jax.ShapeDtypeStruct((blocks, channels, width), F32),
        ],
        scratch_shapes=[pltpu.VMEM((TAIL, width), F32)],
        compiler_params=params(),
        name="setup",
    )(lattice, kfilter)


def wave_kernel(picks, arrays, first, start, waits, low, *refs):
    refs = list(refs)
    take = lambda n: [refs.pop(0) for _ in range(n)]
    (lattice_ref,) = take(1)
    messages = take(arrays)
    before_ref = None if start else take(1)[0]
    take(waits)
    table_ref, total_ref = take(2)
    low_ref = take(1)[0] if low else None
    feat_scr, pos_scr = take(2)
    phases, buffers = take(2), take(2)
    blocks, width = table_ref.shape[0] // 2, table_ref.shape[1]
    every = lattice_ref.shape[0]
    pairs, channels, both = feat_scr.shape
    shard = both // 2
    for place, (array, index) in enumerate(picks):
        item = messages[array] if index is None else messages[array].at[index]
        lanes = slice(place % 2 * shard, (place % 2 + 1) * shard)
        feat_scr[place // 2, :, lanes] = item[0:channels, :]
        pos_scr[place // 2, :, lanes] = item[channels:, :]
    for j in range(2 * blocks):
        if start:
            total_ref[j] = jnp.zeros_like(total_ref[j])
        else:
            total_ref[j] = before_ref[j // blocks * every + first + j % blocks]
    buffers[1][...] = jnp.zeros_like(buffers[1])
    steps = pairs * blocks

    def phase(i, slot):
        i = jnp.minimum(i, steps - 1)
        phases[slot][...] = jnp.dot(
            lattice_ref[first + i % blocks], pos_scr[i // blocks], preferred_element_type=F32
        )

    def product(i, slot, half):
        pair, block = i // blocks, i % blocks
        total_ref[half * blocks + block] += lax.dot_general(
            feat_scr[pair], buffers[slot][half], (((1,), (1,)), ((), ())), preferred_element_type=F32
        )

    def unit(i, slot):
        pair, block = i // blocks, i % blocks
        before = jnp.maximum(i - 1, 0)
        lanes = pl.ds(pl.multiple_of(pair * both, both), both)
        rows = 16
        for n, at in enumerate(range(0, width, rows)):
            if n == 4:
                product(before, 1 - slot, 0)
            if n == 10:
                product(before, 1 - slot, 1)
            turns = phases[slot][at : at + rows, :]
            r = turns - jnp.round(turns)
            s = horner(r * r, SIN_COEF) * r
            square = s * s
            w = (2.0 + SLACK) - square
            cosine = (1.0 - square).astype(BF16)
            sine = (s * (w * lax.rsqrt(w))).astype(BF16)
            buffers[slot][0, at : at + rows, :] = cosine
            buffers[slot][1, at : at + rows, :] = sine
            table_ref[block, at : at + rows, lanes] = cosine
            table_ref[blocks + block, at : at + rows, lanes] = sine
        phase(i + 2, slot)

    phase(0, 0)
    phase(1, 1)

    def body(n, carry):
        unit(2 * n, 0)
        unit(2 * n + 1, 1)
        return carry

    lax.fori_loop(0, steps // 2, body, 0)
    if steps % 2:
        unit(steps - 1, 0)
    for half in range(2):
        product(steps - 1, (steps - 1) % 2, half)
    if low:
        low_ref[...] = total_ref[...].astype(BF16)


def wave(lattice, arrays, picks, before, subset=None, after=(), low=False):
    every, width, _ = lattice.shape
    first, blocks = subset or (0, every)
    pieces = len(picks)
    rows, shard = arrays[0].shape[-2:]
    channels = rows - TAIL
    args = [lattice, *arrays] + ([] if before is None else [before])
    factor = (2 * blocks, channels, width)
    shapes = [
        jax.ShapeDtypeStruct((2 * blocks, width, pieces * shard), BF16),
        jax.ShapeDtypeStruct(factor, F32),
    ]
    if low:
        shapes.append(jax.ShapeDtypeStruct(factor, BF16))
    pairs = blocks * width * pieces * shard
    return pl.pallas_call(
        functools.partial(
            wave_kernel, tuple(picks), len(arrays), first, before is None, len(after), low
        ),
        in_specs=[VMEM] * len(args) + [ANY] * len(after),
        out_specs=[VMEM] * len(shapes),
        out_shape=shapes,
        scratch_shapes=[
            pltpu.VMEM((pieces // 2, channels, 2 * shard), BF16),
            pltpu.VMEM((pieces // 2, TAIL, 2 * shard), BF16),
            pltpu.VMEM((width, 2 * shard), F32),
            pltpu.VMEM((width, 2 * shard), F32),
            pltpu.VMEM((2, width, 2 * shard), BF16),
            pltpu.VMEM((2, width, 2 * shard), BF16),
        ],
        compiler_params=params(),
        cost_estimate=pl.CostEstimate(
            flops=4 * pairs * channels, bytes_accessed=4 * pairs, transcendentals=pairs
        ),
        name="wave",
    )(*args, *after)


def collect_kernel(picks, *refs):
    for p, (array, index) in enumerate(picks):
        ref = refs[array]
        refs[-1][p] = ref[...] if index is None else ref[index]


def collect(arrays, picks, after=()):
    return pl.pallas_call(
        functools.partial(collect_kernel, picks),
        in_specs=[VMEM] * len(arrays) + [ANY] * len(after),
        out_specs=VMEM,
        out_shape=jax.ShapeDtypeStruct((len(picks), *arrays[0].shape[-2:]), BF16),
        compiler_params=params(),
        name="collect",
    )(*arrays, *after)


def transform(filt_ref, table_refs, pieces, out_ref, shard):
    for at, places in enumerate(pieces):
        acc = None
        for j, (table, index, place) in enumerate(places):
            part = jnp.dot(
                filt_ref[j],
                table_refs[table][index, :, place * shard : (place + 1) * shard],
                preferred_element_type=F32,
            )
            acc = part if acc is None else acc + part
        out_ref[:, at * shard : (at + 1) * shard] = acc.astype(out_ref.dtype)


def first_kernel(pieces, shard, parts, blocks, *refs):
    own_refs, other_refs, refs = refs[:parts], refs[parts : 2 * parts], refs[2 * parts :]
    kfilt_ref, table_refs, (filt_ref, out_ref) = refs[0], refs[2:-2], refs[-2:]
    count = kfilt_ref.shape[0]
    for half in range(2):
        for j in range(count):
            part, index = j // blocks, half * blocks + j % blocks
            total = own_refs[part][index] + other_refs[part][index].astype(F32)
            filt_ref[half * count + j] = (total * kfilt_ref[j]).astype(BF16)
    transform(filt_ref, table_refs, pieces, out_ref, shard)


def inverse_kernel(pieces, shard, filt_ref, *refs):
    transform(filt_ref, refs[:-1], pieces, refs[-1], shard)


def inverse_cost(count, channels, width, atoms):
    return pl.CostEstimate(
        flops=2 * count * channels * width * atoms,
        bytes_accessed=2 * count * width * atoms,
        transcendentals=0,
    )


def used(tables, pieces):
    names = sorted({place[0] for places in pieces for place in places})
    moved = tuple(tuple((names.index(t), i, p) for t, i, p in places) for places in pieces)
    return [tables[t] for t in names], moved


def inverse_first(own, other, kfilt, after, tables, pieces, shard):
    count, channels, width = kfilt.shape
    tables, pieces = used(tables, pieces)
    atoms = shard * len(pieces)
    blocks = count // len(own)
    return pl.pallas_call(
        functools.partial(first_kernel, pieces, shard, len(own), blocks),
        in_specs=[VMEM] * (2 * len(own) + 1) + [ANY] + [VMEM] * len(tables),
        out_specs=[VMEM] * 2,
        out_shape=[
            jax.ShapeDtypeStruct((2 * count, channels, width), BF16),
            jax.ShapeDtypeStruct((channels, atoms), BF16),
        ],
        compiler_params=params(),
        cost_estimate=inverse_cost(2 * count, channels, width, atoms),
        name="first",
    )(*own, *other, kfilt, after, *tables)


def inverse(filt, tables, pieces, shard, dtype):
    count, channels, width = filt.shape
    tables, pieces = used(tables, pieces)
    atoms = shard * len(pieces)
    return pl.pallas_call(
        functools.partial(inverse_kernel, pieces, shard),
        in_specs=[VMEM] * (1 + len(tables)),
        out_specs=VMEM,
        out_shape=jax.ShapeDtypeStruct((channels, atoms), dtype),
        compiler_params=params(),
        cost_estimate=inverse_cost(count, channels, width, atoms),
        name="inverse",
    )(filt, *tables)


def join_kernel(here_ref, arrived_ref, own_ref, *send_refs):
    width = own_ref.shape[1]
    for p in range(len(send_refs) + 1):
        lanes = slice(p * width, (p + 1) * width)
        total = here_ref[:, lanes] + arrived_ref[:, lanes].astype(F32)
        if p:
            send_refs[p - 1][...] = total.astype(BF16)
        else:
            own_ref[...] = total


def join(here, arrived, pieces):
    channels, atoms = here.shape
    shape = (channels, atoms // pieces)
    return pl.pallas_call(
        join_kernel,
        in_specs=[VMEM] * 2,
        out_specs=[VMEM] * pieces,
        out_shape=[jax.ShapeDtypeStruct(shape, F32)]
        + [jax.ShapeDtypeStruct(shape, BF16)] * (pieces - 1),
        compiler_params=params(),
        name="join",
    )(here, arrived)


def pair_kernel(nbasis, pieces, output_scale, picks, arrays, own, neighbours_ref, own_pos_ref, *refs):
    message_refs, refs = refs[:arrays], refs[arrays:]
    weight_ref, _, out_ref, feat_scr, pos_scr, own_scr, basis_scr, near_scr, spot_scr, acc_scr = refs
    block = BLOCK_ATOMS
    both = 2 * block
    width = 12.0 / nbasis
    own_blocks, neighbours = neighbours_ref.shape
    shard = own_blocks * block
    channels = out_ref.shape[0]

    views = [
        message_refs[array] if index is None else message_refs[array].at[index]
        for array, index in picks
    ]
    for place, ref in enumerate(views):
        lanes = slice(place * shard, (place + 1) * shard)
        feat_scr[:, lanes] = ref[0:channels, :]
        parts = ref[channels:, :].astype(F32)
        pos_scr[0:3, lanes] = (parts[0:3] + parts[3:6] + parts[6:9]) * 8.0
    for d in range(3):
        row = own_pos_ref[d : d + 1, own * block : (own + 1) * block]
        own_scr[d] = jnp.broadcast_to(row, (both, block)).T

    a_index = lax.axis_index("atoms")
    k_index = lax.axis_index("kvec")
    n_atoms = lax.axis_size("atoms")
    group_blk = own_blocks * pieces
    first = (a_index * pieces + k_index) * own_blocks
    toward = jnp.where(a_index % 2 == 0, 1, n_atoms - 1)

    def divide(value, by):
        if by & (by - 1):
            return value // by, value % by
        return lax.shift_right_logical(value, by.bit_length() - 1), value & (by - 1)

    def place_of(ident):
        group, within = divide(ident, group_blk)
        ahead = divide(group - a_index + n_atoms, n_atoms)[1]
        which = jnp.where(ahead == 0, 0, jnp.where(ahead == toward, 1, 2))
        piece, rest = divide(within, own_blocks)
        return (which * pieces + (piece ^ k_index)) * own_blocks + rest

    rows = 16
    row_index = lax.broadcasted_iota(jnp.int32, (rows, both), 0)
    lane = lax.broadcasted_iota(jnp.int32, (1, both), 1)
    per_block = neighbours // 2
    log2e = math.log2(math.e)

    def unit(pair, carry):
        own_place = jnp.full((1, both), -1, jnp.int32)
        for h in range(2):
            ident = neighbours_ref[own, 2 * pair + h]
            lanes = pl.ds(pl.multiple_of(place_of(ident) * block, block), block)
            here = pl.ds(pl.multiple_of(pair * both + h * block, block), block)
            near_scr[:, here] = feat_scr[:, lanes]
            spot_scr[0:3, h * block : (h + 1) * block] = pos_scr[0:3, lanes]
            inside = (lane >= h * block) & (lane < (h + 1) * block) & (ident == first + own)
            own_place = jnp.where(inside, lane - h * block, own_place)
        lanes = pl.ds(pl.multiple_of(pair * both, both), both)
        for at in range(0, block, rows):
            dist2 = (own_scr[0, at : at + rows, :] - spot_scr[0:1, :]) ** 2
            dist2 += (own_scr[1, at : at + rows, :] - spot_scr[1:2, :]) ** 2
            dist2 += (own_scr[2, at : at + rows, :] - spot_scr[2:3, :]) ** 2
            radius = dist2 * lax.rsqrt(jnp.maximum(dist2, 1e-30))
            env = (16.0 * output_scale) / (16.0 + dist2)
            env = jnp.where(row_index + at == own_place, 0.0, env)
            v = radius * (log2e / width) - 0.5 * log2e
            value = jnp.exp2(v * v * (-0.5 / log2e)) * env
            ratio = jnp.exp2(v)
            for k in range(nbasis):
                if k:
                    value = value * ratio
                basis_scr[k * block + at : k * block + at + rows, lanes] = value.astype(BF16)
        return carry

    lax.fori_loop(0, per_block, unit, 0)
    acc_scr[...] = lax.dot_general(
        near_scr[...], basis_scr[...], (((1,), (1,)), ((), ())), preferred_element_type=F32
    )
    total = jnp.zeros((channels, block), F32)
    for n in range(nbasis):
        part = acc_scr[:, n * block : (n + 1) * block] * math.exp(-0.5 * n * n)
        total += lax.dot_general(
            weight_ref[n * channels : (n + 1) * channels, :],
            part.astype(BF16),
            (((0,), (0,)), ((), ())),
            preferred_element_type=F32,
        )
    out_ref[...] = total


def pair_message(own, neighbours, own_pos, arrays, picks, weight, after):
    channels = weight.shape[1]
    nbasis = weight.shape[0] // channels
    pieces = len(picks) // 3
    shard = own_pos.shape[1]
    count = neighbours.shape[1]
    scale = float(count * BLOCK_ATOMS) ** (-0.5)
    window = 3 * pieces * shard
    return pl.pallas_call(
        functools.partial(pair_kernel, nbasis, pieces, scale, picks, len(arrays), own),
        in_specs=[SMEM] + [VMEM] * (2 + len(arrays)) + [ANY],
        out_specs=VMEM,
        out_shape=jax.ShapeDtypeStruct((channels, BLOCK_ATOMS), F32),
        scratch_shapes=[
            pltpu.VMEM((channels, window), BF16),
            pltpu.VMEM((8, window), F32),
            pltpu.VMEM((3, BLOCK_ATOMS, 2 * BLOCK_ATOMS), F32),
            pltpu.VMEM((nbasis * BLOCK_ATOMS, count * BLOCK_ATOMS), BF16),
            pltpu.VMEM((channels, count * BLOCK_ATOMS), BF16),
            pltpu.VMEM((8, 2 * BLOCK_ATOMS), F32),
            pltpu.VMEM((channels, nbasis * BLOCK_ATOMS), F32),
        ],
        compiler_params=params(),
        cost_estimate=pl.CostEstimate(
            flops=2 * BLOCK_ATOMS * count * BLOCK_ATOMS * (nbasis * channels + 40),
            bytes_accessed=2 * window * channels,
            transcendentals=3 * BLOCK_ATOMS * count * BLOCK_ATOMS,
        ),
        name="pair",
    )(neighbours, own_pos, *arrays, weight, after)


def update_kernel(pairs, *refs):
    features_ref, gain_ref, w_in_ref, w_out_ref = refs[:4]
    pair_refs, parts, out_ref = refs[4 : 4 + pairs], refs[4 + pairs : -1], refs[-1]
    long_t = parts[0][...].astype(F32)
    for part in parts[1:]:
        long_t = long_t + part[...].astype(F32)
    pair_t = jnp.concatenate([ref[...] for ref in pair_refs], axis=1)
    total = features_ref[...].astype(F32) + (pair_t + long_t).T
    mean = jnp.mean(total * total, axis=-1, keepdims=True)
    normed = (total * lax.rsqrt(mean + 1e-06) * gain_ref[...]).astype(BF16)
    pre = jnp.dot(normed, w_in_ref[...], preferred_element_type=F32)
    hidden = (pre / (1.0 + jnp.exp(-pre))).astype(BF16)
    out_ref[...] = (
        total + jnp.dot(hidden, w_out_ref[...], preferred_element_type=F32)
    ).astype(BF16)


def update(features, pairs, gain, w_in, w_out, parts):
    return pl.pallas_call(
        functools.partial(update_kernel, len(pairs)),
        in_specs=[VMEM] * (4 + len(pairs) + len(parts)),
        out_specs=VMEM,
        out_shape=jax.ShapeDtypeStruct(features.shape, BF16),
        compiler_params=params(),
        name="update",
    )(features, gain[None, :], w_in, w_out, *pairs, *parts)


def swap(value, axis, bits):
    return lax.ppermute(value, axis, [(i, i ^ bits) for i in range(lax.axis_size(axis))])


def per_device(
    positions,
    features,
    atom_mask,
    neighbours,
    lattice,
    pair_weight,
    kfilter,
    norm_gain,
    w_in,
    w_out,
):
    shard, _ = features.shape
    n_atoms = lax.axis_size("atoms")
    n_kvec = lax.axis_size("kvec")
    far = n_atoms // 4
    count = lattice.shape[1] // (2 * far)
    width = 256 if count % 256 == 0 else count

    message, lattice, kfilter = pack(features, atom_mask, positions, lattice, kfilter)
    scale = float(n_atoms * n_kvec * shard * KW) ** (-0.5)
    waves, kfilt = setup(lattice, kfilter, far, width, scale)
    others = range(n_kvec - 1, 0, -1)
    zs = range(1, far)
    message_x = swap(message, "atoms", 1)
    near = {k: swap(message, "kvec", k) for k in others}
    distant = [swap(message, "atoms", 4 * z) for z in zs]
    blocks = waves.shape[0]
    tables, where = [], {}

    def keep(table, names):
        tables.append(table)
        for place, name in enumerate(names):
            where[name] = tuple((len(tables) - 1, j, place) for j in range(2 * blocks))

    table, total = wave(waves, [message, message_x], [(0, None), (1, None)], None)
    keep(table, [(0, 0, 0), (1, 0, 0)])
    near_own = collect([near[k] for k in others], [(i, None) for i in range(n_kvec - 1)], after=(total,))
    near_x = swap(near_own, "atoms", 1)
    names = [(0, 0, k) for k in others] + [(1, 0, k) for k in others]
    picks = [(core, i) for core in range(2) for i in range(n_kvec - 1)]
    table, total = wave(waves, [near_own], picks[:2], total)
    keep(table, names[:2])
    distant = collect(distant, [(z, None) for z in range(far - 1)], after=(total,))
    relayed = {k: swap(distant, "kvec", k) for k in others}
    halo_pairs = [(a, (a + 1) % n_atoms if a % 2 else (a - 1) % n_atoms) for a in range(n_atoms)]
    group = [(0, None)] + [(1, n_kvec - 1 - k) for k in range(1, n_kvec)]
    halo = lax.ppermute(collect([message, near_own], group), "atoms", halo_pairs)
    middle = 2 + (len(picks) - 2) // 4 * 2
    table, total = wave(waves, [near_own, near_x], picks[2:middle], total)
    keep(table, names[2:middle])
    every = [(i, z) for i in range(n_kvec) for z in range(far - 1)]
    far_own = collect([distant, *[relayed[k] for k in others]], every, after=(total,))
    far_x = swap(far_own, "atoms", 1)
    table, total = wave(waves, [near_own, near_x], picks[middle:], total, after=(far_own,))
    keep(table, names[middle:])
    arrays = [far_own, far_x]
    picks = [(core, i) for core in range(2) for i in range(len(every))]
    spots = [(core, z, k) for core in range(2) for k in (0, *others) for z in zs]
    own_factors, other_factors, low = [], [], None
    for j in range(blocks):
        after = () if low is None else (low,)
        table, part, low = wave(waves, arrays, picks, total, subset=(j, 1), after=after, low=True)
        tables.append(table)
        own_factors.append(part)
        other_factors.append(swap(low, "atoms", 2))
    for place, spot in enumerate(spots):
        first = len(tables) - blocks
        where[spot] = tuple((first + j, half, place) for half in range(2) for j in range(blocks))

    arrays = [message, message_x, near_own, near_x, halo]
    picks = [(0, None)] + [(2, n_kvec - 1 - k) for k in range(1, n_kvec)]
    picks += [(1, None)] + [(3, n_kvec - 1 - k) for k in range(1, n_kvec)]
    picks += [(4, k) for k in range(n_kvec)]
    pairs = []
    for b in range(neighbours.shape[0]):
        pairs.append(pair_message(b, neighbours, positions, arrays, tuple(picks), pair_weight, low))

    def runs(core, distances):
        return tuple(where[core, z, k] for k in range(n_kvec) for z in distances)

    filt, away_far = inverse_first(
        own_factors, other_factors, kfilt, pairs[0], tables, runs(1, zs), shard
    )
    crossed_far = swap(away_far, "atoms", 1)
    away_near = inverse(filt, tables, runs(1, (0,)), shard, BF16)
    crossed_near = swap(away_near, "atoms", 1)
    here_far = inverse(filt, tables, runs(0, zs), shard, F32)
    sum_far, *sends = join(here_far, crossed_far, n_kvec)
    for k in others:
        sum_far = sum_far + swap(sends[k - 1], "kvec", k).astype(F32)
    sum_far = sum_far.astype(BF16)
    here_near = inverse(filt, tables, runs(0, (0,)), shard, F32)
    own_near, *sends = join(here_near, crossed_near, n_kvec)
    parts = [own_near]
    for k in others:
        parts.append(swap(sends[k - 1], "kvec", k))
    for z in zs:
        parts.append(swap(sum_far[:, (z - 1) * shard : z * shard], "atoms", 4 * z))
    return update(features, pairs, norm_gain, w_in, w_out, parts)


def solution(mesh):
    return jax.shard_map(
        per_device,
        mesh=mesh,
        in_specs=(
            P(None, ("atoms", "kvec")),
            P(("atoms", "kvec"), None),
            P(("atoms", "kvec")),
            P(("atoms", "kvec"), None),
            P(None, "kvec"),
            P(),
            P(),
            P(),
            P(),
            P(),
        ),
        out_specs=P(("atoms", "kvec"), None),
        check_vma=False,
    )
```

```python
import functools
import math

import jax
import jax.numpy as jnp
from jax import lax
from jax.experimental import pallas as pl
from jax.experimental.pallas import tpu as pltpu
from jax.sharding import PartitionSpec as P

KW = 12288
BLOCK_ATOMS = 128
F32 = jnp.float32
BF16 = jnp.bfloat16

SIN_COEF = (4.442879586561992, -7.307818050390618, 3.5977887417720016, -0.7912382192058507)
SLACK = 1e-5
TAIL = 16


def params(mib=16):
    return pltpu.CompilerParams(vmem_limit_bytes=mib << 20)


SMEM = pl.BlockSpec(memory_space=pltpu.SMEM)
VMEM = pl.BlockSpec(memory_space=pltpu.VMEM)
ANY = pl.BlockSpec(memory_space=pl.ANY)


def horner(u, coef):
    acc = coef[-1] * u + coef[-2]
    for c in reversed(coef[:-2]):
        acc = acc * u + c
    return acc


def pack_kernel(*refs):
    features_hbm, mask_hbm, pos_hbm, lattice_hbm, kfilter_hbm = refs[:5]
    out_ref, lattice_ref, kfilter_ref, features_ref, mask_ref, pos_ref, scr, sems = refs[5:]
    copies = [
        pltpu.make_async_copy(source, target, sems.at[i])
        for i, (source, target) in enumerate(
            (
                (features_hbm, features_ref),
                (mask_hbm, mask_ref),
                (pos_hbm, pos_ref),
                (lattice_hbm, lattice_ref),
                (kfilter_hbm, kfilter_ref),
            )
        )
    ]
    for copy in copies:
        copy.start()
    for copy in copies:
        copy.wait()
    channels = features_ref.shape[1]
    mask = mask_ref[...].astype(F32)
    out_ref[0:channels, :] = (features_ref[...].astype(F32).T * mask).astype(BF16)
    value = pos_ref[...] * 0.125
    high = value.astype(BF16).astype(F32)
    rest = value - high
    mid = rest.astype(BF16).astype(F32)
    scr[...] = jnp.zeros_like(scr)
    scr[0:3, :] = high
    scr[3:6, :] = mid
    scr[6:9, :] = rest - mid
    out_ref[channels : channels + TAIL, :] = scr[...].astype(BF16)


def pack(features, mask, positions, lattice, kfilter):
    shard, channels = features.shape
    arrays = (features, mask[None, :], positions, lattice, kfilter)
    return pl.pallas_call(
        pack_kernel,
        in_specs=[pl.BlockSpec(memory_space=pltpu.HBM)] * 5,
        out_specs=[VMEM] * 3,
        out_shape=[
            jax.ShapeDtypeStruct((channels + TAIL, shard), BF16),
            jax.ShapeDtypeStruct(lattice.shape, lattice.dtype),
            jax.ShapeDtypeStruct(kfilter.shape, kfilter.dtype),
        ],
        scratch_shapes=[
            pltpu.VMEM((shard, channels), BF16),
            pltpu.VMEM((1, shard), jnp.int32),
            pltpu.VMEM((3, shard), F32),
            pltpu.VMEM((TAIL, shard), F32),
            pltpu.SemaphoreType.DMA((5,)),
        ],
        compiler_params=params(),
        name="pack",
    )(*(pltpu.with_memory_space_constraint(x, pltpu.HBM) for x in arrays))


def setup_kernel(far, nbasis, scale, lattice_ref, kfilter_ref, wave_ref, kfilt_ref, scr):
    blocks, width, _ = wave_ref.shape
    a_index = lax.axis_index("atoms")
    part = a_index % 2 + 2 * (a_index // 4)
    count = blocks * width
    kfilter = kfilter_ref[...].T
    for j in range(blocks):
        lattice = jnp.zeros((3, width), F32)
        for p in range(2 * far):
            at = p * count + j * width
            mine = (part == p).astype(F32)
            lattice += lattice_ref[:, at : at + width].astype(F32) * mine
        scr[...] = jnp.zeros_like(scr)
        for copy in range(3):
            scr[3 * copy : 3 * copy + 3, :] = lattice
        wave_ref[j] = scr[...].T.astype(BF16)
        wave = lattice * (2.0 * math.pi / 8.0)
        kmag = jnp.sqrt(
            wave[0:1] * wave[0:1] + wave[1:2] * wave[1:2] + wave[2:3] * wave[2:3]
        )
        total = jnp.zeros(kfilt_ref.shape[1:], F32)
        for p in range(nbasis):
            basis = jnp.exp(-0.5 * ((kmag - (p + 0.5) * (21.0 / nbasis)) / (21.0 / nbasis)) ** 2)
            total += kfilter[:, p : p + 1] * basis
        kfilt_ref[j] = total * scale


def setup(lattice, kfilter, far, width, scale):
    nbasis, channels = kfilter.shape
    blocks = lattice.shape[1] // (2 * far * width)
    return pl.pallas_call(
        functools.partial(setup_kernel, far, nbasis, scale),
        in_specs=[VMEM] * 2,
        out_specs=[VMEM] * 2,
        out_shape=[
            jax.ShapeDtypeStruct((blocks, width, TAIL), BF16),
            jax.ShapeDtypeStruct((blocks, channels, width), F32),
        ],
        scratch_shapes=[pltpu.VMEM((TAIL, width), F32)],
        compiler_params=params(),
        name="setup",
    )(lattice, kfilter)


def wave_kernel(picks, arrays, first, start, waits, low, packed, *refs):
    refs = list(refs)
    take = lambda n: [refs.pop(0) for _ in range(n)]
    (lattice_ref,) = take(1)
    messages = take(arrays)
    laid = take(2) if packed == "in" else None
    before_ref = None if start else take(1)[0]
    take(waits)
    table_ref, total_ref = take(2)
    low_ref = take(1)[0] if low else None
    feat_scr, pos_scr = laid or take(2)
    phases, buffers = take(2), take(2)
    blocks, width = table_ref.shape[0] // 2, table_ref.shape[1]
    every = lattice_ref.shape[0]
    pairs, channels, both = feat_scr.shape
    shard = both // 2
    for place, (array, index) in enumerate(picks if packed != "in" else ()):
        item = messages[array] if index is None else messages[array].at[index]
        lanes = slice(place % 2 * shard, (place % 2 + 1) * shard)
        feat_scr[place // 2, :, lanes] = item[0:channels, :]
        pos_scr[place // 2, :, lanes] = item[channels:, :]
    for j in range(2 * blocks):
        if start:
            total_ref[j] = jnp.zeros_like(total_ref[j])
        else:
            total_ref[j] = before_ref[j // blocks * every + first + j % blocks]
    buffers[1][...] = jnp.zeros_like(buffers[1])
    steps = pairs * blocks

    def phase(i, slot):
        i = jnp.minimum(i, steps - 1)
        phases[slot][...] = jnp.dot(
            lattice_ref[first + i % blocks], pos_scr[i // blocks], preferred_element_type=F32
        )

    def product(i, slot, half):
        pair, block = i // blocks, i % blocks
        total_ref[half * blocks + block] += lax.dot_general(
            feat_scr[pair], buffers[slot][half], (((1,), (1,)), ((), ())), preferred_element_type=F32
        )

    def unit(i, slot):
        pair, block = i // blocks, i % blocks
        before = jnp.maximum(i - 1, 0)
        lanes = pl.ds(pl.multiple_of(pair * both, both), both)
        rows = 16
        for n, at in enumerate(range(0, width, rows)):
            if n == 4:
                product(before, 1 - slot, 0)
            if n == 10:
                product(before, 1 - slot, 1)
            turns = phases[slot][at : at + rows, :]
            r = turns - jnp.round(turns)
            s = horner(r * r, SIN_COEF) * r
            square = s * s
            w = (2.0 + SLACK) - square
            cosine = (1.0 - square).astype(BF16)
            sine = (s * (w * lax.rsqrt(w))).astype(BF16)
            buffers[slot][0, at : at + rows, :] = cosine
            buffers[slot][1, at : at + rows, :] = sine
            table_ref[block, at : at + rows, lanes] = cosine
            table_ref[blocks + block, at : at + rows, lanes] = sine
        phase(i + 2, slot)

    phase(0, 0)
    phase(1, 1)

    def body(n, carry):
        unit(2 * n, 0)
        unit(2 * n + 1, 1)
        return carry

    lax.fori_loop(0, steps // 2, body, 0)
    if steps % 2:
        unit(steps - 1, 0)
    for half in range(2):
        product(steps - 1, (steps - 1) % 2, half)
    if low:
        low_ref[...] = total_ref[...].astype(BF16)


def wave(lattice, arrays, picks, before, subset=None, after=(), low=False, packed=None, laid=()):
    every, width, _ = lattice.shape
    first, blocks = subset or (0, every)
    pieces = len(picks)
    rows, shard = arrays[0].shape[-2:]
    channels = rows - TAIL
    if packed == "in":
        arrays = []
    args = [lattice, *arrays, *laid] + ([] if before is None else [before])
    factor = (2 * blocks, channels, width)
    shapes = [
        jax.ShapeDtypeStruct((2 * blocks, width, pieces * shard), BF16),
        jax.ShapeDtypeStruct(factor, F32),
    ]
    if low:
        shapes.append(jax.ShapeDtypeStruct(factor, BF16))
    feat = (pieces // 2, channels, 2 * shard)
    spot = (pieces // 2, TAIL, 2 * shard)
    if packed == "out":
        shapes += [jax.ShapeDtypeStruct(feat, BF16), jax.ShapeDtypeStruct(spot, BF16)]
    pairs = blocks * width * pieces * shard
    return pl.pallas_call(
        functools.partial(
            wave_kernel, tuple(picks), len(arrays), first, before is None, len(after), low, packed
        ),
        in_specs=[VMEM] * len(args) + [ANY] * len(after),
        out_specs=[VMEM] * len(shapes),
        out_shape=shapes,
        scratch_shapes=[
            *([] if packed else [pltpu.VMEM(feat, BF16), pltpu.VMEM(spot, BF16)]),
            pltpu.VMEM((width, 2 * shard), F32),
            pltpu.VMEM((width, 2 * shard), F32),
            pltpu.VMEM((2, width, 2 * shard), BF16),
            pltpu.VMEM((2, width, 2 * shard), BF16),
        ],
        compiler_params=params(),
        cost_estimate=pl.CostEstimate(
            flops=4 * pairs * channels, bytes_accessed=4 * pairs, transcendentals=pairs
        ),
        name="wave",
    )(*args, *after)


def collect_kernel(picks, *refs):
    for p, (array, index) in enumerate(picks):
        ref = refs[array]
        refs[-1][p] = ref[...] if index is None else ref[index]


def collect(arrays, picks, after=()):
    return pl.pallas_call(
        functools.partial(collect_kernel, picks),
        in_specs=[VMEM] * len(arrays) + [ANY] * len(after),
        out_specs=VMEM,
        out_shape=jax.ShapeDtypeStruct((len(picks), *arrays[0].shape[-2:]), BF16),
        compiler_params=params(),
        name="collect",
    )(*arrays, *after)


def transform(filt_ref, table_refs, pieces, out_ref, shard):
    for at, places in enumerate(pieces):
        acc = None
        for j, (table, index, place) in enumerate(places):
            part = jnp.dot(
                filt_ref[j],
                table_refs[table][index, :, place * shard : (place + 1) * shard],
                preferred_element_type=F32,
            )
            acc = part if acc is None else acc + part
        out_ref[:, at * shard : (at + 1) * shard] = acc.astype(out_ref.dtype)


def first_kernel(pieces, shard, parts, blocks, *refs):
    own_refs, other_refs, refs = refs[:parts], refs[parts : 2 * parts], refs[2 * parts :]
    kfilt_ref, table_refs, (filt_ref, out_ref) = refs[0], refs[2:-2], refs[-2:]
    count = kfilt_ref.shape[0]
    for half in range(2):
        for j in range(count):
            part, index = j // blocks, half * blocks + j % blocks
            total = own_refs[part][index] + other_refs[part][index].astype(F32)
            filt_ref[half * count + j] = (total * kfilt_ref[j]).astype(BF16)
    transform(filt_ref, table_refs, pieces, out_ref, shard)


def inverse_kernel(pieces, shard, filt_ref, *refs):
    transform(filt_ref, refs[:-1], pieces, refs[-1], shard)


def inverse_cost(count, channels, width, atoms):
    return pl.CostEstimate(
        flops=2 * count * channels * width * atoms,
        bytes_accessed=2 * count * width * atoms,
        transcendentals=0,
    )


def used(tables, pieces):
    names = sorted({place[0] for places in pieces for place in places})
    moved = tuple(tuple((names.index(t), i, p) for t, i, p in places) for places in pieces)
    return [tables[t] for t in names], moved


def inverse_first(own, other, kfilt, after, tables, pieces, shard):
    count, channels, width = kfilt.shape
    tables, pieces = used(tables, pieces)
    atoms = shard * len(pieces)
    blocks = count // len(own)
    return pl.pallas_call(
        functools.partial(first_kernel, pieces, shard, len(own), blocks),
        in_specs=[VMEM] * (2 * len(own) + 1) + [ANY] + [VMEM] * len(tables),
        out_specs=[VMEM] * 2,
        out_shape=[
            jax.ShapeDtypeStruct((2 * count, channels, width), BF16),
            jax.ShapeDtypeStruct((channels, atoms), BF16),
        ],
        compiler_params=params(),
        cost_estimate=inverse_cost(2 * count, channels, width, atoms),
        name="first",
    )(*own, *other, kfilt, after, *tables)


def inverse(filt, tables, pieces, shard, dtype):
    count, channels, width = filt.shape
    tables, pieces = used(tables, pieces)
    atoms = shard * len(pieces)
    return pl.pallas_call(
        functools.partial(inverse_kernel, pieces, shard),
        in_specs=[VMEM] * (1 + len(tables)),
        out_specs=VMEM,
        out_shape=jax.ShapeDtypeStruct((channels, atoms), dtype),
        compiler_params=params(),
        cost_estimate=inverse_cost(count, channels, width, atoms),
        name="inverse",
    )(filt, *tables)


def join_kernel(here_ref, arrived_ref, own_ref, *send_refs):
    width = own_ref.shape[1]
    for p in range(len(send_refs) + 1):
        lanes = slice(p * width, (p + 1) * width)
        total = here_ref[:, lanes] + arrived_ref[:, lanes].astype(F32)
        if p:
            send_refs[p - 1][...] = total.astype(BF16)
        else:
            own_ref[...] = total


def join(here, arrived, pieces):
    channels, atoms = here.shape
    shape = (channels, atoms // pieces)
    return pl.pallas_call(
        join_kernel,
        in_specs=[VMEM] * 2,
        out_specs=[VMEM] * pieces,
        out_shape=[jax.ShapeDtypeStruct(shape, F32)]
        + [jax.ShapeDtypeStruct(shape, BF16)] * (pieces - 1),
        compiler_params=params(),
        name="join",
    )(here, arrived)


def pair_kernel(nbasis, pieces, output_scale, picks, arrays, own, neighbours_ref, own_pos_ref, *refs):
    message_refs, refs = refs[:arrays], refs[arrays:]
    weight_ref, _, out_ref, feat_scr, pos_scr, own_scr, basis_scr, near_scr, spot_scr, acc_scr = refs
    block = BLOCK_ATOMS
    both = 2 * block
    width = 12.0 / nbasis
    own_blocks, neighbours = neighbours_ref.shape
    shard = own_blocks * block
    channels = out_ref.shape[0]

    views = [
        message_refs[array] if index is None else message_refs[array].at[index]
        for array, index in picks
    ]
    for place, ref in enumerate(views):
        lanes = slice(place * shard, (place + 1) * shard)
        feat_scr[:, lanes] = ref[0:channels, :]
        parts = ref[channels:, :].astype(F32)
        pos_scr[0:3, lanes] = (parts[0:3] + parts[3:6] + parts[6:9]) * 8.0
    for d in range(3):
        row = own_pos_ref[d : d + 1, own * block : (own + 1) * block]
        own_scr[d] = jnp.broadcast_to(row, (both, block)).T

    a_index = lax.axis_index("atoms")
    k_index = lax.axis_index("kvec")
    n_atoms = lax.axis_size("atoms")
    group_blk = own_blocks * pieces
    first = (a_index * pieces + k_index) * own_blocks
    toward = jnp.where(a_index % 2 == 0, 1, n_atoms - 1)

    def divide(value, by):
        if by & (by - 1):
            return value // by, value % by
        return lax.shift_right_logical(value, by.bit_length() - 1), value & (by - 1)

    def place_of(ident):
        group, within = divide(ident, group_blk)
        ahead = divide(group - a_index + n_atoms, n_atoms)[1]
        which = jnp.where(ahead == 0, 0, jnp.where(ahead == toward, 1, 2))
        piece, rest = divide(within, own_blocks)
        return (which * pieces + (piece ^ k_index)) * own_blocks + rest

    rows = 16
    row_index = lax.broadcasted_iota(jnp.int32, (rows, both), 0)
    lane = lax.broadcasted_iota(jnp.int32, (1, both), 1)
    per_block = neighbours // 2
    log2e = math.log2(math.e)

    def unit(pair, carry):
        own_place = jnp.full((1, both), -1, jnp.int32)
        for h in range(2):
            ident = neighbours_ref[own, 2 * pair + h]
            lanes = pl.ds(pl.multiple_of(place_of(ident) * block, block), block)
            here = pl.ds(pl.multiple_of(pair * both + h * block, block), block)
            near_scr[:, here] = feat_scr[:, lanes]
            spot_scr[0:3, h * block : (h + 1) * block] = pos_scr[0:3, lanes]
            inside = (lane >= h * block) & (lane < (h + 1) * block) & (ident == first + own)
            own_place = jnp.where(inside, lane - h * block, own_place)
        lanes = pl.ds(pl.multiple_of(pair * both, both), both)
        for at in range(0, block, rows):
            dist2 = (own_scr[0, at : at + rows, :] - spot_scr[0:1, :]) ** 2
            dist2 += (own_scr[1, at : at + rows, :] - spot_scr[1:2, :]) ** 2
            dist2 += (own_scr[2, at : at + rows, :] - spot_scr[2:3, :]) ** 2
            radius = dist2 * lax.rsqrt(jnp.maximum(dist2, 1e-30))
            env = (16.0 * output_scale) / (16.0 + dist2)
            env = jnp.where(row_index + at == own_place, 0.0, env)
            v = radius * (log2e / width) - 0.5 * log2e
            value = jnp.exp2(v * v * (-0.5 / log2e)) * env
            ratio = jnp.exp2(v)
            for k in range(nbasis):
                if k:
                    value = value * ratio
                basis_scr[k * block + at : k * block + at + rows, lanes] = value.astype(BF16)
        return carry

    lax.fori_loop(0, per_block, unit, 0)
    acc_scr[...] = lax.dot_general(
        near_scr[...], basis_scr[...], (((1,), (1,)), ((), ())), preferred_element_type=F32
    )
    total = jnp.zeros((channels, block), F32)
    for n in range(nbasis):
        part = acc_scr[:, n * block : (n + 1) * block] * math.exp(-0.5 * n * n)
        total += lax.dot_general(
            weight_ref[n * channels : (n + 1) * channels, :],
            part.astype(BF16),
            (((0,), (0,)), ((), ())),
            preferred_element_type=F32,
        )
    out_ref[...] = total


def pair_message(own, neighbours, own_pos, arrays, picks, weight, after):
    channels = weight.shape[1]
    nbasis = weight.shape[0] // channels
    pieces = len(picks) // 3
    shard = own_pos.shape[1]
    count = neighbours.shape[1]
    scale = float(count * BLOCK_ATOMS) ** (-0.5)
    window = 3 * pieces * shard
    return pl.pallas_call(
        functools.partial(pair_kernel, nbasis, pieces, scale, picks, len(arrays), own),
        in_specs=[SMEM] + [VMEM] * (2 + len(arrays)) + [ANY],
        out_specs=VMEM,
        out_shape=jax.ShapeDtypeStruct((channels, BLOCK_ATOMS), F32),
        scratch_shapes=[
            pltpu.VMEM((channels, window), BF16),
            pltpu.VMEM((8, window), F32),
            pltpu.VMEM((3, BLOCK_ATOMS, 2 * BLOCK_ATOMS), F32),
            pltpu.VMEM((nbasis * BLOCK_ATOMS, count * BLOCK_ATOMS), BF16),
            pltpu.VMEM((channels, count * BLOCK_ATOMS), BF16),
            pltpu.VMEM((8, 2 * BLOCK_ATOMS), F32),
            pltpu.VMEM((channels, nbasis * BLOCK_ATOMS), F32),
        ],
        compiler_params=params(),
        cost_estimate=pl.CostEstimate(
            flops=2 * BLOCK_ATOMS * count * BLOCK_ATOMS * (nbasis * channels + 40),
            bytes_accessed=2 * window * channels,
            transcendentals=3 * BLOCK_ATOMS * count * BLOCK_ATOMS,
        ),
        name="pair",
    )(neighbours, own_pos, *arrays, weight, after)


def update_kernel(pairs, *refs):
    features_ref, gain_ref, w_in_ref, w_out_ref = refs[:4]
    pair_refs, parts, out_ref = refs[4 : 4 + pairs], refs[4 + pairs : -1], refs[-1]
    long_t = parts[0][...].astype(F32)
    for part in parts[1:]:
        long_t = long_t + part[...].astype(F32)
    pair_t = jnp.concatenate([ref[...] for ref in pair_refs], axis=1)
    total = features_ref[...].astype(F32) + (pair_t + long_t).T
    mean = jnp.mean(total * total, axis=-1, keepdims=True)
    normed = (total * lax.rsqrt(mean + 1e-06) * gain_ref[...]).astype(BF16)
    pre = jnp.dot(normed, w_in_ref[...], preferred_element_type=F32)
    hidden = (pre / (1.0 + jnp.exp(-pre))).astype(BF16)
    out_ref[...] = (
        total + jnp.dot(hidden, w_out_ref[...], preferred_element_type=F32)
    ).astype(BF16)


def update(features, pairs, gain, w_in, w_out, parts):
    return pl.pallas_call(
        functools.partial(update_kernel, len(pairs)),
        in_specs=[VMEM] * (4 + len(pairs) + len(parts)),
        out_specs=VMEM,
        out_shape=jax.ShapeDtypeStruct(features.shape, BF16),
        compiler_params=params(),
        name="update",
    )(features, gain[None, :], w_in, w_out, *pairs, *parts)


def swap(value, axis, bits):
    return lax.ppermute(value, axis, [(i, i ^ bits) for i in range(lax.axis_size(axis))])


def per_device(
    positions,
    features,
    atom_mask,
    neighbours,
    lattice,
    pair_weight,
    kfilter,
    norm_gain,
    w_in,
    w_out,
):
    shard, _ = features.shape
    n_atoms = lax.axis_size("atoms")
    n_kvec = lax.axis_size("kvec")
    far = n_atoms // 4
    count = lattice.shape[1] // (2 * far)
    width = 256 if count % 256 == 0 else count

    message, lattice, kfilter = pack(features, atom_mask, positions, lattice, kfilter)
    scale = float(n_atoms * n_kvec * shard * KW) ** (-0.5)
    waves, kfilt = setup(lattice, kfilter, far, width, scale)
    others = range(n_kvec - 1, 0, -1)
    zs = range(1, far)
    message_x = swap(message, "atoms", 1)
    near = {k: swap(message, "kvec", k) for k in others}
    distant = [swap(message, "atoms", 4 * z) for z in zs]
    blocks = waves.shape[0]
    tables, where = [], {}

    def keep(table, names):
        tables.append(table)
        for place, name in enumerate(names):
            where[name] = tuple((len(tables) - 1, j, place) for j in range(2 * blocks))

    table, total = wave(waves, [message, message_x], [(0, None), (1, None)], None)
    keep(table, [(0, 0, 0), (1, 0, 0)])
    near_own = collect([near[k] for k in others], [(i, None) for i in range(n_kvec - 1)], after=(total,))
    near_x = swap(near_own, "atoms", 1)
    names = [(0, 0, k) for k in others] + [(1, 0, k) for k in others]
    picks = [(core, i) for core in range(2) for i in range(n_kvec - 1)]
    table, total = wave(waves, [near_own], picks[:2], total)
    keep(table, names[:2])
    distant = collect(distant, [(z, None) for z in range(far - 1)], after=(total,))
    relayed = {k: swap(distant, "kvec", k) for k in others}
    halo_pairs = [(a, (a + 1) % n_atoms if a % 2 else (a - 1) % n_atoms) for a in range(n_atoms)]
    group = [(0, None)] + [(1, n_kvec - 1 - k) for k in range(1, n_kvec)]
    halo = lax.ppermute(collect([message, near_own], group), "atoms", halo_pairs)
    middle = 2 + (len(picks) - 2) // 4 * 2
    table, total = wave(waves, [near_own, near_x], picks[2:middle], total)
    keep(table, names[2:middle])
    every = [(i, z) for i in range(n_kvec) for z in range(far - 1)]
    far_own = collect([distant, *[relayed[k] for k in others]], every, after=(total,))
    far_x = swap(far_own, "atoms", 1)
    table, total = wave(waves, [near_own, near_x], picks[middle:], total, after=(far_own,))
    keep(table, names[middle:])
    arrays = [far_own, far_x]
    picks = [(core, i) for core in range(2) for i in range(len(every))]
    spots = [(core, z, k) for core in range(2) for k in (0, *others) for z in zs]
    own_factors, other_factors, low, laid = [], [], None, ()
    for j in range(blocks):
        after = () if low is None else (low,)
        table, part, low, *more = wave(
            waves,
            arrays,
            picks,
            total,
            subset=(j, 1),
            after=after,
            low=True,
            packed="in" if j else "out",
            laid=laid,
        )
        laid = laid or tuple(more)
        tables.append(table)
        own_factors.append(part)
        other_factors.append(swap(low, "atoms", 2))
    for place, spot in enumerate(spots):
        first = len(tables) - blocks
        where[spot] = tuple((first + j, half, place) for half in range(2) for j in range(blocks))

    arrays = [message, message_x, near_own, near_x, halo]
    picks = [(0, None)] + [(2, n_kvec - 1 - k) for k in range(1, n_kvec)]
    picks += [(1, None)] + [(3, n_kvec - 1 - k) for k in range(1, n_kvec)]
    picks += [(4, k) for k in range(n_kvec)]
    pairs = []
    for b in range(neighbours.shape[0]):
        pairs.append(pair_message(b, neighbours, positions, arrays, tuple(picks), pair_weight, low))

    def runs(core, distances):
        return tuple(where[core, z, k] for k in range(n_kvec) for z in distances)

    filt, away_far = inverse_first(
        own_factors, other_factors, kfilt, pairs[0], tables, runs(1, zs), shard
    )
    crossed_far = swap(away_far, "atoms", 1)
    away_near = inverse(filt, tables, runs(1, (0,)), shard, BF16)
    crossed_near = swap(away_near, "atoms", 1)
    here_far = inverse(filt, tables, runs(0, zs), shard, F32)
    sum_far, *sends = join(here_far, crossed_far, n_kvec)
    for k in others:
        sum_far = sum_far + swap(sends[k - 1], "kvec", k).astype(F32)
    sum_far = sum_far.astype(BF16)
    here_near = inverse(filt, tables, runs(0, (0,)), shard, F32)
    own_near, *sends = join(here_near, crossed_near, n_kvec)
    parts = [own_near]
    for k in others:
        parts.append(swap(sends[k - 1], "kvec", k))
    for z in zs:
        parts.append(swap(sum_far[:, (z - 1) * shard : z * shard], "atoms", 4 * z))
    return update(features, pairs, norm_gain, w_in, w_out, parts)


def solution(mesh):
    return jax.shard_map(
        per_device,
        mesh=mesh,
        in_specs=(
            P(None, ("atoms", "kvec")),
            P(("atoms", "kvec"), None),
            P(("atoms", "kvec")),
            P(("atoms", "kvec"), None),
            P(None, "kvec"),
            P(),
            P(),
            P(),
            P(),
            P(),
        ),
        out_specs=P(("atoms", "kvec"), None),
        check_vma=False,
    )
```

```python
import functools
import math

import jax
import jax.numpy as jnp
from jax import lax
from jax.experimental import pallas as pl
from jax.experimental.pallas import tpu as pltpu
from jax.sharding import PartitionSpec as P

KW = 12288
BLOCK_ATOMS = 128
F32 = jnp.float32
BF16 = jnp.bfloat16

SIN_COEF = (4.442866003912508, -7.307368462859549, 3.5940784351469652, -0.7825084116727845)
SLACK = 1e-6
TAIL = 16


def params(mib=16):
    return pltpu.CompilerParams(vmem_limit_bytes=mib << 20)


SMEM = pl.BlockSpec(memory_space=pltpu.SMEM)
VMEM = pl.BlockSpec(memory_space=pltpu.VMEM)
ANY = pl.BlockSpec(memory_space=pl.ANY)


def horner(u, coef):
    acc = coef[-1] * u + coef[-2]
    for c in reversed(coef[:-2]):
        acc = acc * u + c
    return acc


def pack_kernel(*refs):
    features_hbm, mask_hbm, pos_hbm, lattice_hbm, kfilter_hbm = refs[:5]
    out_ref, lattice_ref, kfilter_ref, features_ref, mask_ref, pos_ref, scr, sems = refs[5:]
    copies = [
        pltpu.make_async_copy(source, target, sems.at[i])
        for i, (source, target) in enumerate(
            (
                (features_hbm, features_ref),
                (mask_hbm, mask_ref),
                (pos_hbm, pos_ref),
                (lattice_hbm, lattice_ref),
                (kfilter_hbm, kfilter_ref),
            )
        )
    ]
    for copy in copies:
        copy.start()
    for copy in copies:
        copy.wait()
    channels = features_ref.shape[1]
    mask = mask_ref[...].astype(F32)
    out_ref[0:channels, :] = (features_ref[...].astype(F32).T * mask).astype(BF16)
    value = pos_ref[...] * 0.125
    high = value.astype(BF16).astype(F32)
    rest = value - high
    mid = rest.astype(BF16).astype(F32)
    scr[...] = jnp.zeros_like(scr)
    scr[0:3, :] = high
    scr[3:6, :] = mid
    scr[6:9, :] = rest - mid
    out_ref[channels : channels + TAIL, :] = scr[...].astype(BF16)


def pack(features, mask, positions, lattice, kfilter):
    shard, channels = features.shape
    arrays = (features, mask[None, :], positions, lattice, kfilter)
    return pl.pallas_call(
        pack_kernel,
        in_specs=[pl.BlockSpec(memory_space=pltpu.HBM)] * 5,
        out_specs=[VMEM] * 3,
        out_shape=[
            jax.ShapeDtypeStruct((channels + TAIL, shard), BF16),
            jax.ShapeDtypeStruct(lattice.shape, lattice.dtype),
            jax.ShapeDtypeStruct(kfilter.shape, kfilter.dtype),
        ],
        scratch_shapes=[
            pltpu.VMEM((shard, channels), BF16),
            pltpu.VMEM((1, shard), jnp.int32),
            pltpu.VMEM((3, shard), F32),
            pltpu.VMEM((TAIL, shard), F32),
            pltpu.SemaphoreType.DMA((5,)),
        ],
        compiler_params=params(),
        name="pack",
    )(*(pltpu.with_memory_space_constraint(x, pltpu.HBM) for x in arrays))


def setup_kernel(far, nbasis, scale, lattice_ref, kfilter_ref, wave_ref, kfilt_ref, scr):
    blocks, width, _ = wave_ref.shape
    a_index = lax.axis_index("atoms")
    part = a_index % 2 + 2 * (a_index // 4)
    count = blocks * width
    kfilter = kfilter_ref[...].T
    for j in range(blocks):
        lattice = jnp.zeros((3, width), F32)
        for p in range(2 * far):
            at = p * count + j * width
            mine = (part == p).astype(F32)
            lattice += lattice_ref[:, at : at + width].astype(F32) * mine
        scr[...] = jnp.zeros_like(scr)
        for copy in range(3):
            scr[3 * copy : 3 * copy + 3, :] = lattice
        wave_ref[j] = scr[...].T.astype(BF16)
        wave = lattice * (2.0 * math.pi / 8.0)
        kmag = jnp.sqrt(
            wave[0:1] * wave[0:1] + wave[1:2] * wave[1:2] + wave[2:3] * wave[2:3]
        )
        total = jnp.zeros(kfilt_ref.shape[1:], F32)
        for p in range(nbasis):
            basis = jnp.exp(-0.5 * ((kmag - (p + 0.5) * (21.0 / nbasis)) / (21.0 / nbasis)) ** 2)
            total += kfilter[:, p : p + 1] * basis
        kfilt_ref[j] = total * scale


def setup(lattice, kfilter, far, width, scale):
    nbasis, channels = kfilter.shape
    blocks = lattice.shape[1] // (2 * far * width)
    return pl.pallas_call(
        functools.partial(setup_kernel, far, nbasis, scale),
        in_specs=[VMEM] * 2,
        out_specs=[VMEM] * 2,
        out_shape=[
            jax.ShapeDtypeStruct((blocks, width, TAIL), BF16),
            jax.ShapeDtypeStruct((blocks, channels, width), F32),
        ],
        scratch_shapes=[pltpu.VMEM((TAIL, width), F32)],
        compiler_params=params(),
        name="setup",
    )(lattice, kfilter)


def wave_kernel(picks, arrays, first, start, waits, low, packed, *refs):
    refs = list(refs)
    take = lambda n: [refs.pop(0) for _ in range(n)]
    (lattice_ref,) = take(1)
    messages = take(arrays)
    laid = take(2) if packed == "in" else None
    before_ref = None if start else take(1)[0]
    take(waits)
    table_ref, total_ref = take(2)
    low_ref = take(1)[0] if low else None
    feat_scr, pos_scr = laid or take(2)
    phases, buffers = take(2), take(2)
    blocks, width = table_ref.shape[0] // 2, table_ref.shape[1]
    every = lattice_ref.shape[0]
    pairs, channels, both = feat_scr.shape
    shard = both // 2
    for place, (array, index) in enumerate(picks if packed != "in" else ()):
        item = messages[array] if index is None else messages[array].at[index]
        lanes = slice(place % 2 * shard, (place % 2 + 1) * shard)
        feat_scr[place // 2, :, lanes] = item[0:channels, :]
        pos_scr[place // 2, :, lanes] = item[channels:, :]
    for j in range(2 * blocks):
        if start:
            total_ref[j] = jnp.zeros_like(total_ref[j])
        else:
            total_ref[j] = before_ref[j // blocks * every + first + j % blocks]
    buffers[1][...] = jnp.zeros_like(buffers[1])
    steps = pairs * blocks

    def phase(i, slot):
        i = jnp.minimum(i, steps - 1)
        phases[slot][...] = jnp.dot(
            lattice_ref[first + i % blocks], pos_scr[i // blocks], preferred_element_type=F32
        )

    def product(i, slot, half):
        pair, block = i // blocks, i % blocks
        total_ref[half * blocks + block] += lax.dot_general(
            feat_scr[pair], buffers[slot][half], (((1,), (1,)), ((), ())), preferred_element_type=F32
        )

    def unit(i, slot):
        pair, block = i // blocks, i % blocks
        before = jnp.maximum(i - 1, 0)
        lanes = pl.ds(pl.multiple_of(pair * both, both), both)
        rows = 16
        for n, at in enumerate(range(0, width, rows)):
            if n == 4:
                product(before, 1 - slot, 0)
            if n == 10:
                product(before, 1 - slot, 1)
            turns = phases[slot][at : at + rows, :]
            r = turns - jnp.round(turns)
            s = horner(r * r, SIN_COEF) * r
            square = s * s
            w = (2.0 + SLACK) - square
            cosine = (1.0 - square).astype(BF16)
            sine = (s * (w * lax.rsqrt(w))).astype(BF16)
            buffers[slot][0, at : at + rows, :] = cosine
            buffers[slot][1, at : at + rows, :] = sine
            table_ref[block, at : at + rows, lanes] = cosine
            table_ref[blocks + block, at : at + rows, lanes] = sine
        phase(i + 2, slot)

    phase(0, 0)
    phase(1, 1)

    def body(n, carry):
        unit(2 * n, 0)
        unit(2 * n + 1, 1)
        return carry

    lax.fori_loop(0, steps // 2, body, 0)
    if steps % 2:
        unit(steps - 1, 0)
    for half in range(2):
        product(steps - 1, (steps - 1) % 2, half)
    if low:
        low_ref[...] = total_ref[...].astype(BF16)


def wave(lattice, arrays, picks, before, subset=None, after=(), low=False, packed=None, laid=()):
    every, width, _ = lattice.shape
    first, blocks = subset or (0, every)
    pieces = len(picks)
    rows, shard = arrays[0].shape[-2:]
    channels = rows - TAIL
    if packed == "in":
        arrays = []
    args = [lattice, *arrays, *laid] + ([] if before is None else [before])
    factor = (2 * blocks, channels, width)
    shapes = [
        jax.ShapeDtypeStruct((2 * blocks, width, pieces * shard), BF16),
        jax.ShapeDtypeStruct(factor, F32),
    ]
    if low:
        shapes.append(jax.ShapeDtypeStruct(factor, BF16))
    feat = (pieces // 2, channels, 2 * shard)
    spot = (pieces // 2, TAIL, 2 * shard)
    if packed == "out":
        shapes += [jax.ShapeDtypeStruct(feat, BF16), jax.ShapeDtypeStruct(spot, BF16)]
    pairs = blocks * width * pieces * shard
    return pl.pallas_call(
        functools.partial(
            wave_kernel, tuple(picks), len(arrays), first, before is None, len(after), low, packed
        ),
        in_specs=[VMEM] * len(args) + [ANY] * len(after),
        out_specs=[VMEM] * len(shapes),
        out_shape=shapes,
        scratch_shapes=[
            *([] if packed else [pltpu.VMEM(feat, BF16), pltpu.VMEM(spot, BF16)]),
            pltpu.VMEM((width, 2 * shard), F32),
            pltpu.VMEM((width, 2 * shard), F32),
            pltpu.VMEM((2, width, 2 * shard), BF16),
            pltpu.VMEM((2, width, 2 * shard), BF16),
        ],
        compiler_params=params(),
        cost_estimate=pl.CostEstimate(
            flops=4 * pairs * channels, bytes_accessed=4 * pairs, transcendentals=pairs
        ),
        name="wave",
    )(*args, *after)


def collect_kernel(picks, *refs):
    for p, (array, index) in enumerate(picks):
        ref = refs[array]
        refs[-1][p] = ref[...] if index is None else ref[index]


def collect(arrays, picks, after=()):
    return pl.pallas_call(
        functools.partial(collect_kernel, picks),
        in_specs=[VMEM] * len(arrays) + [ANY] * len(after),
        out_specs=VMEM,
        out_shape=jax.ShapeDtypeStruct((len(picks), *arrays[0].shape[-2:]), BF16),
        compiler_params=params(),
        name="collect",
    )(*arrays, *after)


def transform(filt_ref, table_refs, pieces, out_ref, shard):
    for at, places in enumerate(pieces):
        acc = None
        for j, (table, index, place) in enumerate(places):
            part = jnp.dot(
                filt_ref[j],
                table_refs[table][index, :, place * shard : (place + 1) * shard],
                preferred_element_type=F32,
            )
            acc = part if acc is None else acc + part
        out_ref[:, at * shard : (at + 1) * shard] = acc.astype(out_ref.dtype)


def first_kernel(pieces, shard, parts, blocks, *refs):
    own_refs, other_refs, refs = refs[:parts], refs[parts : 2 * parts], refs[2 * parts :]
    kfilt_ref, table_refs, (filt_ref, out_ref) = refs[0], refs[2:-2], refs[-2:]
    count = kfilt_ref.shape[0]
    for half in range(2):
        for j in range(count):
            part, index = j // blocks, half * blocks + j % blocks
            total = own_refs[part][index] + other_refs[part][index].astype(F32)
            filt_ref[half * count + j] = (total * kfilt_ref[j]).astype(BF16)
    transform(filt_ref, table_refs, pieces, out_ref, shard)


def inverse_kernel(pieces, shard, filt_ref, *refs):
    transform(filt_ref, refs[:-1], pieces, refs[-1], shard)


def inverse_cost(count, channels, width, atoms):
    return pl.CostEstimate(
        flops=2 * count * channels * width * atoms,
        bytes_accessed=2 * count * width * atoms,
        transcendentals=0,
    )


def used(tables, pieces):
    names = sorted({place[0] for places in pieces for place in places})
    moved = tuple(tuple((names.index(t), i, p) for t, i, p in places) for places in pieces)
    return [tables[t] for t in names], moved


def inverse_first(own, other, kfilt, after, tables, pieces, shard):
    count, channels, width = kfilt.shape
    tables, pieces = used(tables, pieces)
    atoms = shard * len(pieces)
    blocks = count // len(own)
    return pl.pallas_call(
        functools.partial(first_kernel, pieces, shard, len(own), blocks),
        in_specs=[VMEM] * (2 * len(own) + 1) + [ANY] + [VMEM] * len(tables),
        out_specs=[VMEM] * 2,
        out_shape=[
            jax.ShapeDtypeStruct((2 * count, channels, width), BF16),
            jax.ShapeDtypeStruct((channels, atoms), BF16),
        ],
        compiler_params=params(),
        cost_estimate=inverse_cost(2 * count, channels, width, atoms),
        name="first",
    )(*own, *other, kfilt, after, *tables)


def inverse(filt, tables, pieces, shard, dtype):
    count, channels, width = filt.shape
    tables, pieces = used(tables, pieces)
    atoms = shard * len(pieces)
    return pl.pallas_call(
        functools.partial(inverse_kernel, pieces, shard),
        in_specs=[VMEM] * (1 + len(tables)),
        out_specs=VMEM,
        out_shape=jax.ShapeDtypeStruct((channels, atoms), dtype),
        compiler_params=params(),
        cost_estimate=inverse_cost(count, channels, width, atoms),
        name="inverse",
    )(filt, *tables)


def join_kernel(here_ref, arrived_ref, own_ref, *send_refs):
    width = own_ref.shape[1]
    for p in range(len(send_refs) + 1):
        lanes = slice(p * width, (p + 1) * width)
        total = here_ref[:, lanes] + arrived_ref[:, lanes].astype(F32)
        if p:
            send_refs[p - 1][...] = total.astype(BF16)
        else:
            own_ref[...] = total


def join(here, arrived, pieces):
    channels, atoms = here.shape
    shape = (channels, atoms // pieces)
    return pl.pallas_call(
        join_kernel,
        in_specs=[VMEM] * 2,
        out_specs=[VMEM] * pieces,
        out_shape=[jax.ShapeDtypeStruct(shape, F32)]
        + [jax.ShapeDtypeStruct(shape, BF16)] * (pieces - 1),
        compiler_params=params(),
        name="join",
    )(here, arrived)


def pair_kernel(nbasis, pieces, output_scale, picks, arrays, own, neighbours_ref, own_pos_ref, *refs):
    message_refs, refs = refs[:arrays], refs[arrays:]
    weight_ref, _, out_ref, feat_scr, pos_scr, own_scr, basis_scr, near_scr, spot_scr, acc_scr = refs
    block = BLOCK_ATOMS
    both = 2 * block
    width = 12.0 / nbasis
    own_blocks, neighbours = neighbours_ref.shape
    shard = own_blocks * block
    channels = out_ref.shape[0]

    views = [
        message_refs[array] if index is None else message_refs[array].at[index]
        for array, index in picks
    ]
    for place, ref in enumerate(views):
        lanes = slice(place * shard, (place + 1) * shard)
        feat_scr[:, lanes] = ref[0:channels, :]
        parts = ref[channels:, :].astype(F32)
        pos_scr[0:3, lanes] = (parts[0:3] + parts[3:6] + parts[6:9]) * 8.0
    for d in range(3):
        row = own_pos_ref[d : d + 1, own * block : (own + 1) * block]
        own_scr[d] = jnp.broadcast_to(row, (both, block)).T

    a_index = lax.axis_index("atoms")
    k_index = lax.axis_index("kvec")
    n_atoms = lax.axis_size("atoms")
    group_blk = own_blocks * pieces
    first = (a_index * pieces + k_index) * own_blocks
    toward = jnp.where(a_index % 2 == 0, 1, n_atoms - 1)

    def divide(value, by):
        if by & (by - 1):
            return value // by, value % by
        return lax.shift_right_logical(value, by.bit_length() - 1), value & (by - 1)

    def place_of(ident):
        group, within = divide(ident, group_blk)
        ahead = divide(group - a_index + n_atoms, n_atoms)[1]
        which = jnp.where(ahead == 0, 0, jnp.where(ahead == toward, 1, 2))
        piece, rest = divide(within, own_blocks)
        return (which * pieces + (piece ^ k_index)) * own_blocks + rest

    rows = 16
    row_index = lax.broadcasted_iota(jnp.int32, (rows, both), 0)
    lane = lax.broadcasted_iota(jnp.int32, (1, both), 1)
    per_block = neighbours // 2
    log2e = math.log2(math.e)

    def unit(pair, carry):
        own_place = jnp.full((1, both), -1, jnp.int32)
        for h in range(2):
            ident = neighbours_ref[own, 2 * pair + h]
            lanes = pl.ds(pl.multiple_of(place_of(ident) * block, block), block)
            here = pl.ds(pl.multiple_of(pair * both + h * block, block), block)
            near_scr[:, here] = feat_scr[:, lanes]
            spot_scr[0:3, h * block : (h + 1) * block] = pos_scr[0:3, lanes]
            inside = (lane >= h * block) & (lane < (h + 1) * block) & (ident == first + own)
            own_place = jnp.where(inside, lane - h * block, own_place)
        lanes = pl.ds(pl.multiple_of(pair * both, both), both)
        for at in range(0, block, rows):
            dist2 = (own_scr[0, at : at + rows, :] - spot_scr[0:1, :]) ** 2
            dist2 += (own_scr[1, at : at + rows, :] - spot_scr[1:2, :]) ** 2
            dist2 += (own_scr[2, at : at + rows, :] - spot_scr[2:3, :]) ** 2
            radius = dist2 * lax.rsqrt(jnp.maximum(dist2, 1e-30))
            env = (16.0 * output_scale) / (16.0 + dist2)
            env = jnp.where(row_index + at == own_place, 0.0, env)
            v = radius * (log2e / width) - 0.5 * log2e
            value = jnp.exp2(v * v * (-0.5 / log2e)) * env
            ratio = jnp.exp2(v)
            for k in range(nbasis):
                if k:
                    value = value * ratio
                basis_scr[k * block + at : k * block + at + rows, lanes] = value.astype(BF16)
        return carry

    lax.fori_loop(0, per_block, unit, 0)
    acc_scr[...] = lax.dot_general(
        near_scr[...], basis_scr[...], (((1,), (1,)), ((), ())), preferred_element_type=F32
    )
    total = jnp.zeros((channels, block), F32)
    for n in range(nbasis):
        part = acc_scr[:, n * block : (n + 1) * block] * math.exp(-0.5 * n * n)
        total += lax.dot_general(
            weight_ref[n * channels : (n + 1) * channels, :],
            part.astype(BF16),
            (((0,), (0,)), ((), ())),
            preferred_element_type=F32,
        )
    out_ref[...] = total


def pair_message(own, neighbours, own_pos, arrays, picks, weight, after):
    channels = weight.shape[1]
    nbasis = weight.shape[0] // channels
    pieces = len(picks) // 3
    shard = own_pos.shape[1]
    count = neighbours.shape[1]
    scale = float(count * BLOCK_ATOMS) ** (-0.5)
    window = 3 * pieces * shard
    return pl.pallas_call(
        functools.partial(pair_kernel, nbasis, pieces, scale, picks, len(arrays), own),
        in_specs=[SMEM] + [VMEM] * (2 + len(arrays)) + [ANY],
        out_specs=VMEM,
        out_shape=jax.ShapeDtypeStruct((channels, BLOCK_ATOMS), F32),
        scratch_shapes=[
            pltpu.VMEM((channels, window), BF16),
            pltpu.VMEM((8, window), F32),
            pltpu.VMEM((3, BLOCK_ATOMS, 2 * BLOCK_ATOMS), F32),
            pltpu.VMEM((nbasis * BLOCK_ATOMS, count * BLOCK_ATOMS), BF16),
            pltpu.VMEM((channels, count * BLOCK_ATOMS), BF16),
            pltpu.VMEM((8, 2 * BLOCK_ATOMS), F32),
            pltpu.VMEM((channels, nbasis * BLOCK_ATOMS), F32),
        ],
        compiler_params=params(),
        cost_estimate=pl.CostEstimate(
            flops=2 * BLOCK_ATOMS * count * BLOCK_ATOMS * (nbasis * channels + 40),
            bytes_accessed=2 * window * channels,
            transcendentals=3 * BLOCK_ATOMS * count * BLOCK_ATOMS,
        ),
        name="pair",
    )(neighbours, own_pos, *arrays, weight, after)


def update_kernel(pairs, *refs):
    features_ref, gain_ref, w_in_ref, w_out_ref = refs[:4]
    pair_refs, parts, out_ref = refs[4 : 4 + pairs], refs[4 + pairs : -1], refs[-1]
    long_t = parts[0][...].astype(F32)
    for part in parts[1:]:
        long_t = long_t + part[...].astype(F32)
    pair_t = jnp.concatenate([ref[...] for ref in pair_refs], axis=1)
    total = features_ref[...].astype(F32) + (pair_t + long_t).T
    mean = jnp.mean(total * total, axis=-1, keepdims=True)
    normed = (total * lax.rsqrt(mean + 1e-06) * gain_ref[...]).astype(BF16)
    pre = jnp.dot(normed, w_in_ref[...], preferred_element_type=F32)
    hidden = (pre / (1.0 + jnp.exp(-pre))).astype(BF16)
    out_ref[...] = (
        total + jnp.dot(hidden, w_out_ref[...], preferred_element_type=F32)
    ).astype(BF16)


def update(features, pairs, gain, w_in, w_out, parts):
    return pl.pallas_call(
        functools.partial(update_kernel, len(pairs)),
        in_specs=[VMEM] * (4 + len(pairs) + len(parts)),
        out_specs=VMEM,
        out_shape=jax.ShapeDtypeStruct(features.shape, BF16),
        compiler_params=params(),
        name="update",
    )(features, gain[None, :], w_in, w_out, *pairs, *parts)


def swap(value, axis, bits):
    return lax.ppermute(value, axis, [(i, i ^ bits) for i in range(lax.axis_size(axis))])


def per_device(
    positions,
    features,
    atom_mask,
    neighbours,
    lattice,
    pair_weight,
    kfilter,
    norm_gain,
    w_in,
    w_out,
):
    shard, _ = features.shape
    n_atoms = lax.axis_size("atoms")
    n_kvec = lax.axis_size("kvec")
    far = n_atoms // 4
    count = lattice.shape[1] // (2 * far)
    width = 256 if count % 256 == 0 else count

    message, lattice, kfilter = pack(features, atom_mask, positions, lattice, kfilter)
    scale = float(n_atoms * n_kvec * shard * KW) ** (-0.5)
    waves, kfilt = setup(lattice, kfilter, far, width, scale)
    others = range(n_kvec - 1, 0, -1)
    zs = range(1, far)
    message_x = swap(message, "atoms", 1)
    near = {k: swap(message, "kvec", k) for k in others}
    distant = [swap(message, "atoms", 4 * z) for z in zs]
    blocks = waves.shape[0]
    tables, where = [], {}

    def keep(table, names):
        tables.append(table)
        for place, name in enumerate(names):
            where[name] = tuple((len(tables) - 1, j, place) for j in range(2 * blocks))

    table, total = wave(waves, [message, message_x], [(0, None), (1, None)], None)
    keep(table, [(0, 0, 0), (1, 0, 0)])
    near_own = collect([near[k] for k in others], [(i, None) for i in range(n_kvec - 1)], after=(total,))
    near_x = swap(near_own, "atoms", 1)
    names = [(0, 0, k) for k in others] + [(1, 0, k) for k in others]
    picks = [(core, i) for core in range(2) for i in range(n_kvec - 1)]
    table, total = wave(waves, [near_own], picks[:2], total)
    keep(table, names[:2])
    distant = collect(distant, [(z, None) for z in range(far - 1)], after=(total,))
    relayed = {k: swap(distant, "kvec", k) for k in others}
    halo_pairs = [(a, (a + 1) % n_atoms if a % 2 else (a - 1) % n_atoms) for a in range(n_atoms)]
    group = [(0, None)] + [(1, n_kvec - 1 - k) for k in range(1, n_kvec)]
    halo = lax.ppermute(collect([message, near_own], group), "atoms", halo_pairs)
    middle = 2 + (len(picks) - 2) // 4 * 2
    table, total = wave(waves, [near_own, near_x], picks[2:middle], total)
    keep(table, names[2:middle])
    every = [(i, z) for i in range(n_kvec) for z in range(far - 1)]
    far_own = collect([distant, *[relayed[k] for k in others]], every, after=(total,))
    far_x = swap(far_own, "atoms", 1)
    table, total = wave(waves, [near_own, near_x], picks[middle:], total, after=(far_own,))
    keep(table, names[middle:])
    arrays = [far_own, far_x]
    picks = [(core, i) for core in range(2) for i in range(len(every))]
    spots = [(core, z, k) for core in range(2) for k in (0, *others) for z in zs]
    own_factors, other_factors, low, laid = [], [], None, ()
    for j in range(blocks):
        after = () if low is None else (low,)
        table, part, low, *more = wave(
            waves,
            arrays,
            picks,
            total,
            subset=(j, 1),
            after=after,
            low=True,
            packed="in" if j else "out",
            laid=laid,
        )
        laid = laid or tuple(more)
        tables.append(table)
        own_factors.append(part)
        other_factors.append(swap(low, "atoms", 2))
    for place, spot in enumerate(spots):
        first = len(tables) - blocks
        where[spot] = tuple((first + j, half, place) for half in range(2) for j in range(blocks))

    arrays = [message, message_x, near_own, near_x, halo]
    picks = [(0, None)] + [(2, n_kvec - 1 - k) for k in range(1, n_kvec)]
    picks += [(1, None)] + [(3, n_kvec - 1 - k) for k in range(1, n_kvec)]
    picks += [(4, k) for k in range(n_kvec)]
    pairs = []
    for b in range(neighbours.shape[0]):
        pairs.append(pair_message(b, neighbours, positions, arrays, tuple(picks), pair_weight, low))

    def runs(core, distances):
        return tuple(where[core, z, k] for k in range(n_kvec) for z in distances)

    filt, away_far = inverse_first(
        own_factors, other_factors, kfilt, pairs[0], tables, runs(1, zs), shard
    )
    crossed_far = swap(away_far, "atoms", 1)
    away_near = inverse(filt, tables, runs(1, (0,)), shard, BF16)
    crossed_near = swap(away_near, "atoms", 1)
    here_far = inverse(filt, tables, runs(0, zs), shard, F32)
    sum_far, *sends = join(here_far, crossed_far, n_kvec)
    for k in range(1, n_kvec):
        sum_far = sum_far + swap(sends[k - 1], "kvec", k).astype(F32)
    sum_far = sum_far.astype(BF16)
    here_near = inverse(filt, tables, runs(0, (0,)), shard, F32)
    own_near, *sends = join(here_near, crossed_near, n_kvec)
    parts = [own_near]
    for k in range(1, n_kvec):
        parts.append(swap(sends[k - 1], "kvec", k))
    for z in zs:
        parts.append(swap(sum_far[:, (z - 1) * shard : z * shard], "atoms", 4 * z))
    return update(features, pairs, norm_gain, w_in, w_out, parts)


def solution(mesh):
    return jax.shard_map(
        per_device,
        mesh=mesh,
        in_specs=(
            P(None, ("atoms", "kvec")),
            P(("atoms", "kvec"), None),
            P(("atoms", "kvec")),
            P(("atoms", "kvec"), None),
            P(None, "kvec"),
            P(),
            P(),
            P(),
            P(),
            P(),
        ),
        out_specs=P(("atoms", "kvec"), None),
        check_vma=False,
    )
```
